32 devices in a mesh: dp: 2 (over x), expert: 16 (over z, y, core).
Axes of the slice: x: 2, y: 2, z: 4, core: 2. Of those that a mesh axis runs over, the one named last changes fastest.
Arguments:
- tokens: bfloat16 [4096, 2048], P(('dp', 'expert')), may hold values from -6 to 6
- segments: int32 [4096], P('dp'), may hold values from 0 to 15, never falling along the last dimension, each value on 1 to 2048 neighbouring positions
- routes: int32 [4096, 8], P(('dp', 'expert')), may hold values from 0 to 15, all different within a row; in each aligned block of 128 rows (0 to 127, 128 to 255, ...) at most 96 rows name the same one
- route_gates: float32 [4096, 8], P(('dp', 'expert')), may hold values from 0.0625 to 0.1875
- attn_gain: float32 [2048], replicated, may hold values from 0.5 to 1.5
- query_gain: float32 [2048], replicated, may hold values from 0.5 to 1.5
- key_gain: float32 [2048], replicated, may hold values from 0.5 to 1.5
- ffn_gain: float32 [2048], replicated, may hold values from 0.5 to 1.5
- w_query: bfloat16 [2048, 2048], P('expert'), may hold values from -0.125 to 0.125
- w_key: bfloat16 [2048, 2048], P('expert'), may hold values from -0.125 to 0.125
- w_value: bfloat16 [2048, 2048], P('expert'), may hold values from -0.125 to 0.125
- w_out: bfloat16 [2048, 2048], P('expert'), may hold values from -0.375 to 0.375
- w_gate: bfloat16 [16, 2048, 1024], P('expert'), may hold values from -0.125 to 0.125
- w_up: bfloat16 [16, 2048, 1024], P('expert'), may hold values from -0.125 to 0.125
- w_down: bfloat16 [16, 1024, 2048], P('expert'), may hold values from -0.75 to 0.75
- cotangent: bfloat16 [4096, 2048], P(('dp', 'expert')), may hold values from -6 to 6
Outputs:
- activations: bfloat16 [4096, 2048], P(('dp', 'expert'))
- input_grad: bfloat16 [4096, 2048], P(('dp', 'expert'))
- grad_attn_gain: float32 [2048], replicated
- grad_query_gain: float32 [2048], replicated
- grad_key_gain: float32 [2048], replicated
- grad_ffn_gain: float32 [2048], replicated
- grad_w_query: float32 [2048, 2048], P('expert')
- grad_w_key: float32 [2048, 2048], P('expert')
- grad_w_value: float32 [2048, 2048], P('expert')
- grad_w_out: float32 [2048, 2048], P('expert')
- grad_w_gate: float32 [16, 2048, 1024], P('expert')
- grad_w_up: float32 [16, 2048, 1024], P('expert')
- grad_w_down: float32 [16, 1024, 2048], P('expert')
The draws below stay inside these ranges and needn't reach their ends.
Inputs may be any that keep to these rules, and one draw needn't show every extreme that they name: `segments`: segment numbers never fall along the tokens; a document holds 1 to 2048 tokens, and one holds exactly 2048. `routes`: each token names 8 different experts. In the rows of one device no expert is named more than 96 times, and in some device's rows one expert is named exactly 96 times.
All inputs are finite; a program needn't handle non-finite values.
Results may differ from the reference program's by a relative error of at most 0.023.
Values may be sent and summed in bfloat16 or wider, within the bound.
No kernel may reach another device: no remote copies, remote signals or barrier semaphores. Data moves between devices by JAX's collectives and lax.ppermute only.
A program may use at most 384 MiB of HBM per device.

```python
import math
import jax
import jax.numpy as jnp
import numpy as np
from jax import lax

D = 2048
HEADS = 16
HEAD_DIM = 128
FF = 1024
TOP = 8
TOK_DEV = 128
EXPERTS = 16
SLOTS = 96
LENGTH = 2048
TOKENS = 4096
DOCS = 16


def strengthened(values, key, source, target, shards_of, factor):
    owner, partner = [(jnp.arange(values.shape[dim]) // (values.shape[dim] // shards_of)).reshape([-1 if axis == dim else 1 for axis in range(values.ndim)]) for dim in (source, target)]
    chosen = jax.random.permutation(key, shards_of)[partner]
    strong = (owner == chosen) | (owner == (partner + shards_of // 2) % shards_of)
    return jnp.where(strong, factor * values, values)


def levels(own_key, dims, pieces, low, top_value):
    level = 1.0
    for dim, parts in pieces:
        heights = jax.random.uniform(jax.random.fold_in(jax.random.fold_in(own_key, 6), dim), (parts,), jnp.float32, low / len(pieces), top_value / len(pieces))
        level = level * jnp.repeat(jnp.exp(heights), dims[dim] // parts).reshape((-1,) + (1,) * (len(dims) - 1 - dim))
    return level


def profile(amount, total, limit, slope):
    weights = [(1 << 20) // math.isqrt(grade ** slope) + 1 for grade in range(2, amount + 1)]
    rest, counts = total - limit - (amount - 1), [1] * (amount - 1)
    while rest > 0:
        movable = [i for i in range(amount - 1) if counts[i] < limit]
        whole, budget = sum([weights[i] for i in movable]), rest
        for i in movable:
            extra = min(limit - counts[i], max(1, budget * weights[i] // whole), rest)
            counts[i] = counts[i] + extra
            rest = rest - extra
    return np.array([limit] + counts)


def uneven_parts(rng, number_of, total, bound, skew):
    if number_of == 2:
        one = jax.random.randint(rng, (), max(1, total - bound), min(bound, total - 1) + 1)
        return jnp.stack([one, total - one])
    sizes = jnp.asarray(profile(number_of, total, bound, skew), jnp.int32)
    couples = (number_of - 1) // 2
    giver, taker = sizes[1:1 + 2 * couples:2], sizes[2:2 + 2 * couples:2]
    room = jnp.minimum(giver - 1, bound - taker)
    moved = jax.random.randint(jax.random.fold_in(rng, 1), (couples,), 0, 1 << 20) % (room + 1)
    sizes = sizes.at[1:1 + 2 * couples:2].set(giver - moved).at[2:2 + 2 * couples:2].set(taker + moved)
    return sizes[jax.random.permutation(jax.random.fold_in(rng, 2), number_of)]


def deal_out(rng, own, number, rows, amount, top, bound, skew):
    sequence = jax.random.permutation(rng, amount)
    heavy_load, usual = shares(amount, rows * top, bound, skew, True), shares(amount, rows * top, bound, skew, False)
    places = jnp.arange(amount)

    def named(tallies, turn):
        used = int((tallies > 0).sum())
        fixed = max(1, used // 4)
        moved = fixed + (places - fixed + turn * (used - fixed)) % max(1, amount - fixed)
        return jnp.zeros((amount,), jnp.int32).at[sequence[jnp.where(places < fixed, places, moved)]].set(jnp.asarray(tallies, jnp.int32))

    tallies = jnp.where(number % 4 == 0, named(heavy_load, number // 4), named(usual, number - number // 4 - 1))
    mixed = jax.random.permutation(jax.random.fold_in(own, 3), amount)
    giver, sink = mixed[0:amount // 2 * 2:2], mixed[1:amount // 2 * 2:2]
    margin = jnp.minimum(tallies[giver] - 1, bound - tallies[sink]) // 2
    margin = jnp.where((giver == sequence[0]) | (sink == sequence[0]) | (tallies[sink] == 0), 0, jnp.maximum(margin, 0))
    moved = jax.random.randint(jax.random.fold_in(own, 4), (amount // 2,), 0, 1 << 20) % (margin + 1)
    tallies = tallies.at[giver].add(-moved).at[sink].add(moved)
    items = jnp.searchsorted(jnp.cumsum(tallies), jnp.arange(rows * top), side="right").astype(jnp.int32)
    grid = items.reshape(top, rows).T
    grid = grid[jax.random.permutation(jax.random.fold_in(own, 1), rows)]
    turn = jax.random.randint(jax.random.fold_in(own, 2), (rows, 1), 0, top)
    return jnp.take_along_axis(grid, (jnp.arange(top)[None, :] + turn) % top, axis=1)


def shares(count, total, most, lean, full):
    portions = [(1 << 20) // math.isqrt(standing ** lean) + 1 for standing in range(1, count + 1)]
    largest = most if full else min(most, max(-(-total // count), total * portions[0] // sum(portions)))
    least = 1 if total - largest >= count - 1 else 0
    given, surplus = [largest] + [least] * (count - 1), total - largest - least * (count - 1)
    while surplus > 0:
        movable = [i for i in range(1, count) if given[i] < largest] or [i for i in range(1, count) if given[i] < most]
        whole, remaining = sum([portions[i] for i in movable]), surplus
        for i in movable:
            addition = min(most - given[i], max(1, remaining * portions[i] // whole), surplus)
            given[i] = given[i] + addition
            surplus = surplus - addition
    return np.array(given)


def gaussian(rng, extent, spread, most, split=(), held_as=jnp.bfloat16):
    entries = spread * jax.random.normal(rng, extent, jnp.float32)
    if split:
        entries = entries * levels(rng, extent, split, -0.22, 0.18)
    return jnp.clip(entries, -most, most).astype(held_as)


def heavy_noise(own_key, shape, width, most, shards, heavy, kind=jnp.bfloat16):
    drawn = width * jax.random.normal(own_key, shape, jnp.float32)
    if shards:
        drawn = drawn * levels(own_key, shape, shards, -0.22, 0.18)
    return jnp.clip(strengthened(drawn, jax.random.fold_in(own_key, 3), *heavy), -most, most).astype(kind)


def setup_inputs(seed: int = 0) -> dict:
    splits = jax.random.split(jax.random.key(seed), 17)
    tokens = heavy_noise(splits[0], (TOKENS, D), 1.0, 6.0, ((0, 32),), (0, 1, 32, 2.75))
    segments = jnp.searchsorted(jnp.cumsum(uneven_parts(splits[1], DOCS, TOKENS, LENGTH, 2)), jnp.arange(TOKENS), side="right").astype(jnp.int32)
    routes_keys = jax.random.split(jax.random.fold_in(splits[2], 1), TOKENS // TOK_DEV)
    routes_turns = jax.random.permutation(jax.random.fold_in(splits[2], 3), TOKENS // TOK_DEV)
    routes = jax.vmap(lambda own, number: deal_out(jax.random.fold_in(splits[2], 2), own, number, TOK_DEV, EXPERTS, TOP, SLOTS, 1))(routes_keys, routes_turns).reshape((TOKENS, TOP))
    route_gates = jnp.clip(0.0625 + 0.125 * jax.random.uniform(splits[3], (TOKENS, TOP), jnp.float32) ** levels(splits[3], (TOKENS, TOP), ((0, 32),), -0.2, 0.2), 0.0625, 0.1875)
    attn_gain = jnp.clip(1.0 + 0.1 * jax.random.normal(splits[4], (D,), jnp.float32), 0.5, 1.5)
    query_gain = jnp.clip(1.0 + 0.1 * jax.random.normal(splits[5], (D,), jnp.float32), 0.5, 1.5)
    key_gain = jnp.clip(1.0 + 0.1 * jax.random.normal(splits[6], (D,), jnp.float32), 0.5, 1.5)
    ffn_gain = jnp.clip(1.0 + 0.1 * jax.random.normal(splits[7], (D,), jnp.float32), 0.5, 1.5)
    w_query = gaussian(splits[8], (D, D), D ** -0.5, 0.125, ((0, 16),))
    w_key = gaussian(splits[9], (D, D), D ** -0.5, 0.125, ((0, 16),))
    w_value = gaussian(splits[10], (D, D), D ** -0.5, 0.125, ((0, 16),))
    w_out = gaussian(splits[11], (D, D), (D // 8) ** -0.5, 0.375, ((0, 16),))
    w_gate = gaussian(splits[12], (EXPERTS, D, FF), D ** -0.5, 0.125, ((0, 16),))
    w_up = gaussian(splits[13], (EXPERTS, D, FF), D ** -0.5, 0.125, ((0, 16),))
    w_down = gaussian(splits[14], (EXPERTS, FF, D), (FF // 16) ** -0.5, 0.75, ((0, 16),))
    cotangent = gaussian(splits[15], (TOKENS, D), 1.0, 6.0, ((0, 32),))
    return dict(tokens=tokens, segments=segments, routes=routes, route_gates=route_gates, attn_gain=attn_gain, query_gain=query_gain, key_gain=key_gain, ffn_gain=ffn_gain, w_query=w_query, w_key=w_key, w_value=w_value, w_out=w_out, w_gate=w_gate, w_up=w_up, w_down=w_down, cotangent=cotangent)


eps = 1e-05
rope_base = 50000.0
negative = -1e+30
highest = lax.Precision.HIGHEST

@jax.custom_vjp
def low(v):
    return lax.optimization_barrier(v.astype(jnp.bfloat16)).astype(jnp.float32)

@jax.custom_vjp
def low_back(v):
    return v

def low_keep(v):
    return (low(v), None)

def low_pass(kept, grad):
    return (grad,)

def back_keep(v):
    return (v, None)

def back_low(kept, grad):
    return (low(grad),)
low.defvjp(low_keep, low_pass)
low_back.defvjp(back_keep, back_low)

def rms_norm(values, norm_gain):
    return values * lax.rsqrt(lax.optimization_barrier(jnp.mean(values * values, axis=-1, keepdims=True)) + eps) * norm_gain

def matmul(left, right):
    return jnp.dot(left, right, precision=highest)

def rope_angles(positions):
    half_dim = HEAD_DIM // 2
    frequency = rope_base ** (-(jnp.arange(half_dim, dtype=jnp.float32) * 2.0 / HEAD_DIM))
    theta = positions.astype(jnp.float32)[:, None] * frequency[None, :]
    return (jnp.cos(theta)[:, None, :], jnp.sin(theta)[:, None, :])

def rotate(tensor, cosine, rope_sine):
    half_dim = tensor.shape[-1] // 2
    first_half = tensor[..., :half_dim]
    second_half = tensor[..., half_dim:]
    return jnp.concatenate([first_half * cosine - second_half * rope_sine, second_half * cosine + first_half * rope_sine], axis=-1)

def one_sequence(packed):
    queries, key_rows, value_rows, seg_ids = packed
    scores = low_back(jnp.einsum('qhd,khd->hqk', queries, key_rows, precision=highest) * HEAD_DIM ** (-0.5))
    same_doc = seg_ids[:, None] == seg_ids[None, :]
    scores = jnp.where(same_doc[None], scores, negative)
    row_peak = lax.optimization_barrier(jnp.max(scores, axis=-1, keepdims=True))
    exp_scores = jnp.exp(scores - row_peak)
    attn_probs = exp_scores / lax.optimization_barrier(jnp.sum(exp_scores, axis=-1, keepdims=True))
    return jnp.einsum('hqk,khd->qhd', low(attn_probs), value_rows, precision=highest)

def forward(resid_in, attn_gain, query_gain, key_gain, ffn_gain, query_w, key_w, value_w, out_w, gate_w, up_w, down_w, segments, routes, route_gates):
    token_count = resid_in.shape[0]
    normed_in = low(rms_norm(resid_in, attn_gain))
    query_raw = low_back(matmul(normed_in, query_w))
    key_raw = low_back(matmul(normed_in, key_w))
    value_rows = low(low_back(matmul(normed_in, value_w)))
    cosine, rope_sine = rope_angles(jnp.arange(token_count, dtype=jnp.int32) % LENGTH)
    query_rot = low(rotate(rms_norm(query_raw, query_gain).reshape(token_count, HEADS, HEAD_DIM), cosine, rope_sine))
    key_rot = low(rotate(rms_norm(key_raw, key_gain).reshape(token_count, HEADS, HEAD_DIM), cosine, rope_sine))
    seq_count = token_count // LENGTH
    shaped = (query_rot.reshape(seq_count, LENGTH, HEADS, HEAD_DIM), key_rot.reshape(seq_count, LENGTH, HEADS, HEAD_DIM), value_rows.reshape(seq_count, LENGTH, HEADS, HEAD_DIM), segments.reshape(seq_count, LENGTH))
    attended = lax.map(jax.checkpoint(one_sequence), shaped)
    attended = low(low_back(attended.reshape(token_count, HEADS * HEAD_DIM)))
    middle = resid_in + low_back(matmul(attended, out_w))
    normed_mid = low(rms_norm(middle, ffn_gain))
    choice_hits = routes[:, :, None] == jnp.arange(EXPERTS, dtype=jnp.int32)[None, None, :]
    combine_w = lax.optimization_barrier(jnp.sum(jnp.where(choice_hits, route_gates[:, :, None], 0.0), axis=1))

    def expert_step(running, packed):
        gate_e, up_e, down_e, column = packed
        expert_in = low_back(normed_mid)
        gate_pre = low_back(matmul(expert_in, gate_e))
        up_pre = low_back(matmul(expert_in, up_e))
        hidden = low(gate_pre * jax.nn.sigmoid(gate_pre) * up_pre)
        expert_out = low(low_back(matmul(hidden, down_e)))
        return (running + column[:, None] * expert_out, None)
    mixed, _ = lax.scan(jax.checkpoint(expert_step), jnp.zeros_like(middle), (gate_w, up_w, down_w, combine_w.T))
    return middle + mixed

def reference(tokens, segments, routes, route_gates, attn_gain, query_gain, key_gain, ffn_gain, w_query, w_key, w_value, w_out, w_gate, w_up, w_down, cotangent):
    float_args = tuple((array_in.astype(jnp.float32) for array_in in (tokens, attn_gain, query_gain, key_gain, ffn_gain, w_query, w_key, w_value, w_out, w_gate, w_up, w_down)))

    def layer(*params):
        return forward(*params, segments, routes, route_gates)
    result, pullback = jax.vjp(layer, *float_args)
    grads = pullback(cotangent.astype(jnp.float32))
    return (result.astype(jnp.bfloat16), grads[0].astype(jnp.bfloat16), grads[1], grads[2], grads[3], grads[4], grads[5], grads[6], grads[7], grads[8], grads[9], grads[10], grads[11])
```

```python
import functools

import jax
import jax.numpy as jnp
from jax import lax
from jax.experimental import pallas as pl
from jax.experimental.pallas import tpu as pltpu
from jax.sharding import PartitionSpec as P

HEADS = 16
HEAD_DIM = 128


eps = 1e-05
rope_base = 50000.0
negative = -1e30
score_scale = HEAD_DIM ** (-0.5)
query_block = 256


def norm_rows(values, norm_gain):
    inverse = lax.rsqrt(jnp.mean(values * values, axis=-1, keepdims=True) + eps)
    normal = values * inverse
    return (normal * norm_gain, normal, inverse)


def norm_back(upstream, normal, inverse, norm_gain):
    weighted = upstream * norm_gain
    inner_mean = jnp.mean(weighted * normal, axis=-1, keepdims=True)
    return (inverse * (weighted - normal * inner_mean), jnp.sum(upstream * normal, axis=0))


def rope_tables(positions):
    half_dim = HEAD_DIM // 2
    frequency = rope_base ** (-(jnp.arange(half_dim, dtype=jnp.float32) * 2.0 / HEAD_DIM))
    theta = positions.astype(jnp.float32)[:, None] * frequency[None, :]
    return (jnp.cos(theta), jnp.sin(theta))


def rotate(tensor, cosine, rope_sine):
    half_dim = tensor.shape[-1] // 2
    first_half = tensor[..., :half_dim]
    second_half = tensor[..., half_dim:]
    return jnp.concatenate(
        [
            first_half * cosine - second_half * rope_sine,
            second_half * cosine + first_half * rope_sine,
        ],
        axis=-1,
    )


def mm(left, right):
    return jnp.dot(left, right, preferred_element_type=jnp.float32)


def contract_rows(left, right):
    return lax.dot_general(
        left, right, (((0,), (0,)), ((), ())), preferred_element_type=jnp.float32
    )


def contract_cols(left, right):
    return lax.dot_general(
        left, right, (((1,), (1,)), ((), ())), preferred_element_type=jnp.float32
    )


def swap(values, axis, step):
    count = lax.axis_size(axis)
    return lax.ppermute(values, axis, [(i, i ^ step) for i in range(count)])


def butterfly(values, axis):
    step = 1
    while step < lax.axis_size(axis):
        values = values + swap(values, axis, step)
        step *= 2
    return values


def dp_total(values):
    step = 1
    total = values.astype(jnp.float32)
    while step < lax.axis_size("dp"):
        held = total.astype(jnp.bfloat16)
        total = held.astype(jnp.float32) + swap(held, "dp", step).astype(jnp.float32)
        step *= 2
    return total


def attend_kernel(key_seg, query_seg, query, key, value_t, out_t, log_total):
    scores = contract_cols(key[...], query[...]) * score_scale
    scores = jnp.where(key_seg[:, :1] == query_seg[...], scores, negative)
    peak = jnp.max(scores, axis=0, keepdims=True)
    weights = jnp.exp(scores - peak)
    total = jnp.sum(weights, axis=0, keepdims=True)
    out_t[...] = (mm(value_t[...], weights.astype(jnp.bfloat16)) / total).T.astype(out_t.dtype)
    log_total[...] = peak + jnp.log(total)


def attend(key_seg, query_seg, query, key, value_t):
    count = query.shape[0]
    whole = lambda i: (0, 0)
    return pl.pallas_call(
        attend_kernel,
        grid=(count // query_block,),
        in_specs=[
            pl.BlockSpec((count, HEAD_DIM), whole),
            pl.BlockSpec((1, query_block), lambda i: (0, i)),
            pl.BlockSpec((query_block, HEAD_DIM), lambda i: (i, 0)),
            pl.BlockSpec((count, HEAD_DIM), whole),
            pl.BlockSpec((HEAD_DIM, count), whole),
        ],
        out_specs=[
            pl.BlockSpec((query_block, HEAD_DIM), lambda i: (i, 0)),
            pl.BlockSpec((1, query_block), lambda i: (0, i)),
        ],
        out_shape=[
            jax.ShapeDtypeStruct((count, HEAD_DIM), jnp.bfloat16),
            jax.ShapeDtypeStruct((1, count), jnp.float32),
        ],
        cost_estimate=pl.CostEstimate(
            flops=4 * count * count * HEAD_DIM,
            bytes_accessed=count * HEAD_DIM * 10,
            transcendentals=count * count,
        ),
        name="attend",
    )(key_seg, query_seg, query, key, value_t)


def attend_back_kernel(
    key_seg, query_seg, log_total, query, upstream, key, key_t, value, dquery, dkey, dvalue
):
    @pl.when(pl.program_id(0) == 0)
    def _():
        dkey[...] = jnp.zeros_like(dkey)
        dvalue[...] = jnp.zeros_like(dvalue)

    scores = contract_cols(key[...], query[...]) * score_scale
    probs = jnp.where(
        key_seg[:, :1] == query_seg[...], jnp.exp(scores - log_total[...]), 0.0
    )
    dvalue[...] += mm(probs.astype(jnp.bfloat16), upstream[...])
    dprobs = contract_cols(value[...], upstream[...])
    delta = jnp.sum(probs * dprobs, axis=0, keepdims=True)
    dscores = (probs * (dprobs - delta)).astype(jnp.bfloat16)
    dkey[...] += mm(dscores, query[...]) * score_scale
    dquery[...] = (mm(key_t[...], dscores) * score_scale).T


def attend_back(key_seg, query_seg, log_total, query, upstream, key, key_t, value):
    count = query.shape[0]
    whole = lambda i: (0, 0)
    return pl.pallas_call(
        attend_back_kernel,
        grid=(count // query_block,),
        in_specs=[
            pl.BlockSpec((count, HEAD_DIM), whole),
            pl.BlockSpec((1, query_block), lambda i: (0, i)),
            pl.BlockSpec((1, query_block), lambda i: (0, i)),
            pl.BlockSpec((query_block, HEAD_DIM), lambda i: (i, 0)),
            pl.BlockSpec((query_block, HEAD_DIM), lambda i: (i, 0)),
            pl.BlockSpec((count, HEAD_DIM), whole),
            pl.BlockSpec((HEAD_DIM, count), whole),
            pl.BlockSpec((count, HEAD_DIM), whole),
        ],
        out_specs=[
            pl.BlockSpec((query_block, HEAD_DIM), lambda i: (i, 0)),
            pl.BlockSpec((count, HEAD_DIM), whole),
            pl.BlockSpec((count, HEAD_DIM), whole),
        ],
        out_shape=[jax.ShapeDtypeStruct((count, HEAD_DIM), jnp.float32)] * 3,
        cost_estimate=pl.CostEstimate(
            flops=10 * count * count * HEAD_DIM,
            bytes_accessed=count * HEAD_DIM * 20,
            transcendentals=count * count,
        ),
        name="attend_back",
    )(key_seg, query_seg, log_total, query, upstream, key, key_t, value)


def local(
    tokens,
    segments,
    routes,
    route_gates,
    attn_gain,
    query_gain,
    key_gain,
    ffn_gain,
    w_query,
    w_key,
    w_value,
    w_out,
    w_gate,
    w_up,
    w_down,
    cotangent,
):
    row_count, width = tokens.shape
    top_count = routes.shape[1]
    devices = lax.axis_size("expert")
    me = lax.axis_index("expert")
    seq_length = row_count * devices
    part = width // devices
    sharing = HEAD_DIM // part
    head = me // sharing
    sub = me % sharing
    w_rows = w_query.shape[0]

    def gather(values):
        return lax.all_gather(values, "expert", axis=0, tiled=True)

    def exchange(values):
        return lax.all_to_all(values, "expert", split_axis=0, concat_axis=0, tiled=True)

    def to_heads(rows):
        blocks = rows.reshape(rows.shape[0], HEADS, HEAD_DIM).transpose(1, 0, 2)
        return jnp.repeat(blocks, sharing, axis=0)

    def my_part(columns):
        return lax.dynamic_slice_in_dim(columns, sub * part, part, axis=columns.ndim - 1)

    resid_in = tokens.astype(jnp.float32)
    pre_in, normal_in, inverse_in = norm_rows(resid_in, attn_gain)
    normed_in = pre_in.astype(jnp.bfloat16)
    normed_all = gather(normed_in)

    head_w = exchange(
        jnp.concatenate([to_heads(w_query), to_heads(w_key), to_heads(w_value)], axis=2)
    ).reshape(width, 3 * HEAD_DIM)

    out_full = gather(w_out)
    cot_all = gather(cotangent)

    experts_all = devices * w_gate.shape[0]
    slots = min(row_count, row_count * top_count * 3 // (2 * experts_all))
    hits = routes[:, :, None] == jnp.arange(experts_all, dtype=jnp.int32)[None, None, :]
    gate_table = jnp.sum(jnp.where(hits, route_gates[:, :, None], 0.0), axis=1)
    gate_mine = exchange(gate_table.T.reshape(devices, 1, row_count)).reshape(devices, row_count)
    chosen = gate_mine > 0.0
    before = jnp.arange(row_count)[:, None] < jnp.arange(row_count)[None, :]
    rank = mm(chosen.astype(jnp.bfloat16), before.astype(jnp.bfloat16)).astype(jnp.int32)
    rank = jnp.where(chosen, rank, -1)
    picks = rank[:, None, :] == jnp.arange(slots, dtype=jnp.int32)[None, :, None]
    slot_gate = jnp.sum(jnp.where(picks, gate_mine[:, None, :], 0.0), axis=2).reshape(-1, 1)
    picks = picks.astype(jnp.bfloat16)

    def pick(rows):
        return jnp.einsum(
            "bst,btd->bsd",
            picks,
            rows.reshape(devices, row_count, width),
            preferred_element_type=jnp.bfloat16,
        ).reshape(devices * slots, width)

    def unpick(rows):
        return jnp.einsum(
            "bst,bsd->btd",
            picks,
            rows.reshape(devices, slots, width),
            preferred_element_type=jnp.bfloat16,
        ).reshape(seq_length, width)

    raw = mm(normed_all, head_w)
    query_raw, key_raw = raw[:, :HEAD_DIM], raw[:, HEAD_DIM : 2 * HEAD_DIM]
    value = raw[:, 2 * HEAD_DIM :].astype(jnp.bfloat16)
    squares = jnp.stack(
        [jnp.sum(jnp.square(my_part(query_raw)), axis=1), jnp.sum(jnp.square(my_part(key_raw)), axis=1)]
    )
    squares = butterfly(squares, "expert")
    inverse = lax.rsqrt(squares / width + eps)
    inverse_query, inverse_key = inverse[0][:, None], inverse[1][:, None]
    my_query_gain = lax.dynamic_slice_in_dim(query_gain, head * HEAD_DIM, HEAD_DIM)
    my_key_gain = lax.dynamic_slice_in_dim(key_gain, head * HEAD_DIM, HEAD_DIM)
    normal_query = query_raw * inverse_query
    normal_key = key_raw * inverse_key
    cosine, rope_sine = rope_tables(jnp.arange(seq_length, dtype=jnp.int32))
    query_rot = rotate(normal_query * my_query_gain, cosine, rope_sine).astype(jnp.bfloat16)
    key_rot = rotate(normal_key * my_key_gain, cosine, rope_sine).astype(jnp.bfloat16)

    key_seg = jnp.broadcast_to(segments[:, None], (seq_length, HEAD_DIM))
    query_seg = segments[None, :]
    attended, log_total = attend(key_seg, query_seg, query_rot, key_rot, value.T)

    attended_low = (
        exchange(my_part(attended).reshape(devices, row_count, part))
        .transpose(1, 0, 2)
        .reshape(row_count, width)
    )
    middle = resid_in + mm(attended_low, out_full)
    pre_mid, normal_mid, inverse_mid = norm_rows(middle, ffn_gain)
    normed_mid = pre_mid.astype(jnp.bfloat16)

    rows_in = pick(gather(normed_mid))
    grad_eo = (pick(cot_all).astype(jnp.float32) * slot_gate).astype(jnp.bfloat16)
    gate_in = mm(rows_in, w_gate[0])
    up_in = mm(rows_in, w_up[0])
    sigmoid_in = jax.nn.sigmoid(gate_in)
    silu_in = gate_in * sigmoid_in
    hidden = (silu_in * up_in).astype(jnp.bfloat16)
    grad_hidden = contract_cols(grad_eo, w_down[0])
    grad_up_pre = (grad_hidden * silu_in).astype(jnp.bfloat16)
    grad_gate_pre = (
        grad_hidden * up_in * sigmoid_in * (1.0 + gate_in * (1.0 - sigmoid_in))
    ).astype(jnp.bfloat16)
    grad_rows = (
        contract_cols(grad_gate_pre, w_gate[0]) + contract_cols(grad_up_pre, w_up[0])
    ).astype(jnp.bfloat16)

    def scatter(rows):
        return lax.psum_scatter(rows, "expert", scatter_dimension=0, tiled=True)

    grad_normed_mid = scatter(unpick(grad_rows)).astype(jnp.float32)
    down_total = dp_total(contract_rows(hidden, grad_eo).astype(jnp.bfloat16))[None]
    gate_total = dp_total(contract_rows(rows_in, grad_gate_pre).astype(jnp.bfloat16))[None]
    up_total = dp_total(contract_rows(rows_in, grad_up_pre).astype(jnp.bfloat16))[None]
    expert_out = (mm(hidden, w_down[0]) * slot_gate).astype(jnp.bfloat16)
    mixed = scatter(unpick(expert_out)).astype(jnp.float32)
    activations = (middle + mixed).astype(jnp.bfloat16)

    grad_out = cotangent.astype(jnp.float32)
    mid_back, grad_ffn_gain = norm_back(grad_normed_mid, normal_mid, inverse_mid, ffn_gain)
    grad_middle = grad_out + mid_back
    grad_branch = grad_middle.astype(jnp.bfloat16)
    grad_attended = exchange(
        to_heads(contract_cols(grad_branch, out_full).astype(jnp.bfloat16))
    ).reshape(seq_length, HEAD_DIM)
    branch_all = gather(grad_branch)
    out_part = contract_rows(my_part(attended), branch_all)

    grad_query_rot, grad_key_rot, grad_value = attend_back(
        key_seg, query_seg, log_total, query_rot, grad_attended, key_rot, key_rot.T, value
    )
    grad_value = grad_value.astype(jnp.bfloat16)
    grad_query_pre = rotate(grad_query_rot, cosine, -rope_sine)
    grad_key_pre = rotate(grad_key_rot, cosine, -rope_sine)
    weighted_query = grad_query_pre * my_query_gain
    weighted_key = grad_key_pre * my_key_gain
    inner = jnp.stack(
        [
            jnp.sum(my_part(weighted_query * normal_query), axis=1),
            jnp.sum(my_part(weighted_key * normal_key), axis=1),
        ]
    )
    inner = butterfly(inner, "expert") / width
    grad_query = (inverse_query * (weighted_query - normal_query * inner[0][:, None])).astype(
        jnp.bfloat16
    )
    grad_key = (inverse_key * (weighted_key - normal_key * inner[1][:, None])).astype(jnp.bfloat16)
    grad_query_gain = my_part(jnp.sum(grad_query_pre * normal_query, axis=0))
    grad_key_gain = my_part(jnp.sum(grad_key_pre * normal_key, axis=0))

    grad_raw = jnp.concatenate(
        [my_part(grad_query), my_part(grad_key), my_part(grad_value)], axis=1
    )
    part_w = jnp.concatenate(
        [my_part(head_w[:, i * HEAD_DIM : (i + 1) * HEAD_DIM]) for i in range(3)], axis=1
    )
    grad_normed_in = scatter(contract_cols(grad_raw, part_w).astype(jnp.bfloat16)).astype(
        jnp.float32
    )
    in_back, _ = norm_back(grad_normed_in, normal_in, inverse_in, attn_gain)
    input_grad = (grad_middle + in_back).astype(jnp.bfloat16)

    grad_w = contract_rows(normed_all, grad_raw)
    grad_attn_gain = jnp.sum(grad_w * part_w.astype(jnp.float32), axis=1) / attn_gain
    w_columns = exchange(grad_w.astype(jnp.bfloat16).reshape(devices, w_rows, 3 * part))
    dense = (
        w_columns.reshape(devices, w_rows, 3, part)
        .transpose(1, 2, 0, 3)
        .reshape(w_rows, 3 * width)
    )
    dense_total = dp_total(jnp.concatenate([dense, out_part.astype(jnp.bfloat16)], axis=1))

    def placed(values):
        return lax.dynamic_update_slice_in_dim(
            jnp.zeros((width,), jnp.float32), values, me * part, 0
        )

    gain_total = butterfly(
        butterfly(
            jnp.stack(
                [grad_attn_gain, placed(grad_query_gain), placed(grad_key_gain), grad_ffn_gain]
            ),
            "expert",
        ),
        "dp",
    )
    return (
        activations,
        input_grad,
        gain_total[0],
        gain_total[1],
        gain_total[2],
        gain_total[3],
        dense_total[:, :width],
        dense_total[:, width : 2 * width],
        dense_total[:, 2 * width : 3 * width],
        dense_total[:, 3 * width :],
        gate_total,
        up_total,
        down_total,
    )


def solution(mesh):
    in_specs = (
        P(("dp", "expert"), None),
        P("dp"),
        P(("dp", "expert"), None),
        P(("dp", "expert"), None),
        P(),
        P(),
        P(),
        P(),
        P("expert", None),
        P("expert", None),
        P("expert", None),
        P("expert", None),
        P("expert", None, None),
        P("expert", None, None),
        P("expert", None, None),
        P(("dp", "expert"), None),
    )
    out_specs = (
        P(("dp", "expert"), None),
        P(("dp", "expert"), None),
        P(),
        P(),
        P(),
        P(),
        P("expert", None),
        P("expert", None),
        P("expert", None),
        P("expert", None),
        P("expert", None, None),
        P("expert", None, None),
        P("expert", None, None),
    )
    return jax.shard_map(local, mesh=mesh, in_specs=in_specs, out_specs=out_specs, check_vma=False)
```

```python
import functools

import jax
import jax.numpy as jnp
from jax import lax
from jax.experimental import pallas as pl
from jax.experimental.pallas import tpu as pltpu
from jax.sharding import PartitionSpec as P

HEADS = 16
HEAD_DIM = 128


eps = 1e-05
rope_base = 50000.0
negative = -1e30
score_scale = HEAD_DIM ** (-0.5)
query_block = 256


def norm_rows(values, norm_gain):
    inverse = lax.rsqrt(jnp.mean(values * values, axis=-1, keepdims=True) + eps)
    normal = values * inverse
    return (normal * norm_gain, normal, inverse)


def norm_back(upstream, normal, inverse, norm_gain):
    weighted = upstream * norm_gain
    inner_mean = jnp.mean(weighted * normal, axis=-1, keepdims=True)
    return (inverse * (weighted - normal * inner_mean), jnp.sum(upstream * normal, axis=0))


def rope_tables(positions):
    half_dim = HEAD_DIM // 2
    frequency = rope_base ** (-(jnp.arange(half_dim, dtype=jnp.float32) * 2.0 / HEAD_DIM))
    theta = frequency[:, None] * positions.astype(jnp.float32)[None, :]
    return (jnp.cos(theta), jnp.sin(theta))


def mm(left, right):
    return jnp.dot(left, right, preferred_element_type=jnp.float32)


def contract_rows(left, right):
    return lax.dot_general(
        left, right, (((0,), (0,)), ((), ())), preferred_element_type=jnp.float32
    )


def contract_cols(left, right):
    return lax.dot_general(
        left, right, (((1,), (1,)), ((), ())), preferred_element_type=jnp.float32
    )


def swap(values, axis, step):
    count = lax.axis_size(axis)
    return lax.ppermute(values, axis, [(i, i ^ step) for i in range(count)])


def together(*values):
    return lax.optimization_barrier(values)


def after(values, *others):
    return lax.optimization_barrier((values,) + others)[0]


def butterfly(values, axis):
    step = 1
    while step < lax.axis_size(axis):
        values = values + swap(values, axis, step)
        step *= 2
    return values


near_order = ((0, 1, 2, 3), (1, 0, 2, 3), (2, 3, 1, 0), (3, 2, 1, 0))


def moves(target):
    pairs = []
    for index in range(16):
        far = target(index // 4)
        if far is not None:
            pairs.append((index, far * 4 + index % 4))
    return pairs


swap_near = moves(lambda z: z ^ 1)
swap_middle = moves(lambda z: {1: 2, 2: 1}.get(z))
move_out = moves(lambda z: {1: 0, 2: 3}.get(z))
move_in = moves(lambda z: {0: 1, 3: 2}.get(z))
swap_row = [(i, i ^ 2) for i in range(16)]
swap_core = [(i, i ^ 1) for i in range(16)]


def send(values, pairs):
    return lax.ppermute(values, "expert", pairs)


def arrival_order(me):
    near = jnp.asarray(near_order, jnp.int32)[me // 4] * 4
    row, core = (me // 2) % 2, me % 2
    return jnp.concatenate(
        [near + (row ^ j) * 2 + (core ^ i) for i in (0, 1) for j in (0, 1)]
    ).astype(jnp.int32)


class Rounds:
    def __init__(self, steps):
        self.steps = steps
        self.result = None
        self.over = False
        self.sent = ()
        self._go(None)

    def _go(self, arrived):
        try:
            self.sent = self.steps.send(arrived)
        except StopIteration as stop:
            self.result, self.sent, self.over = stop.value, (), True

    def step(self, *others):
        values = together(*self.sent, *others) if self.sent or others else ()
        count = len(self.sent)
        if not self.over:
            self._go(values[:count])
        return values[count:]

    def finish(self):
        while not self.over:
            self.step()
        return self.result


def gather_rounds(block):
    at = lax.axis_index("expert") // 4
    outer = (at == 0) | (at == 3)
    first, second, row = yield (
        send(block, swap_near),
        send(block, swap_middle),
        send(block, swap_row),
    )
    third, second_out, row_first, core = yield (
        send(first, swap_middle),
        send(second, move_out),
        send(first, swap_row),
        send(block, swap_core),
    )
    second = jnp.where(outer, second_out, second)
    third_out, row_second, core_first, core_row = yield (
        send(third, move_out),
        send(second, swap_row),
        send(first, swap_core),
        send(row, swap_core),
    )
    third = jnp.where(outer, third_out, third)
    row_third, core_second, core_third, core_row_first, core_row_second = yield (
        send(third, swap_row),
        send(second, swap_core),
        send(third, swap_core),
        send(row_first, swap_core),
        send(row_second, swap_core),
    )
    (core_row_third,) = yield (send(row_third, swap_core),)
    return [
        block,
        first,
        second,
        third,
        row,
        row_first,
        row_second,
        row_third,
        core,
        core_first,
        core_second,
        core_third,
        core_row,
        core_row_first,
        core_row_second,
        core_row_third,
    ]


def gather_whole(block):
    yield ()
    return list(lax.all_gather(block, "expert", axis=0))


def add_low(left, right):
    return (left.astype(jnp.float32) + right.astype(jnp.float32)).astype(jnp.bfloat16)


def scatter_rounds(make, count):
    (far,) = yield (send(make(count // 2, count // 2), swap_core),)
    close = make(0, count // 2)
    rows = count // 16

    def both(j, k):
        here = slice((j * 4 + k) * rows, (j * 4 + k + 1) * rows)
        return add_low(close[here], far[here])

    (row,) = yield (send(both(1, 3), swap_row),)
    third = add_low(both(0, 3), row)
    row, third_in = yield (send(both(1, 2), swap_row), send(third, move_in))
    second = add_low(both(0, 2), row)
    third = add_low(third, third_in)
    row, second_in, third_in = yield (
        send(both(1, 1), swap_row),
        send(second, move_in),
        send(third, swap_middle),
    )
    first = add_low(add_low(both(0, 1), row), third_in)
    second = add_low(second, second_in)
    row, second_in, first_in = yield (
        send(both(1, 0), swap_row),
        send(second, swap_middle),
        send(first, swap_near),
    )
    return (
        both(0, 0).astype(jnp.float32)
        + row.astype(jnp.float32)
        + second_in.astype(jnp.float32)
        + first_in.astype(jnp.float32)
    )


def scatter_whole(make, count):
    yield ()
    return lax.psum_scatter(make(0, count), "expert", scatter_dimension=0, tiled=True).astype(
        jnp.float32
    )


def pick_kernel(picks, scale, *refs):
    *blocks, out = refs
    slots = picks.shape[1]
    for index, block in enumerate(blocks):
        here = slice(index * slots, (index + 1) * slots)
        out[here, :] = (mm(picks[index], block[...]) * scale[here, :]).astype(out.dtype)


def pick(picks, scale, blocks):
    count, slots, tokens = picks.shape
    width = blocks[0].shape[1]
    return pl.pallas_call(
        pick_kernel,
        out_shape=jax.ShapeDtypeStruct((count * slots, width), jnp.bfloat16),
        cost_estimate=pl.CostEstimate(
            flops=2 * count * tokens * slots * width,
            bytes_accessed=2 * count * (tokens + slots) * width,
            transcendentals=0,
        ),
        name="pick",
    )(picks, scale, *blocks)


def merge_kernel(*refs):
    *pairs, out = refs
    count = len(pairs) // 2
    for index in range(count):

        @pl.when(pl.program_id(0) == index)
        def _():
            out[...] = pairs[index][...].astype(jnp.float32) + pairs[count + index][...].astype(
                jnp.float32
            )


def merge(own, far):
    rows, width = own[0].shape
    return pl.pallas_call(
        merge_kernel,
        grid=(len(own),),
        in_specs=[pl.BlockSpec((rows, width), lambda i: (0, 0))] * (2 * len(own)),
        out_specs=pl.BlockSpec((rows, width), lambda i: (i, 0)),
        out_shape=jax.ShapeDtypeStruct((len(own) * rows, width), jnp.float32),
        cost_estimate=pl.CostEstimate(
            flops=len(own) * rows * width,
            bytes_accessed=8 * len(own) * rows * width,
            transcendentals=0,
        ),
        name="merge",
    )(*own, *far)


def project_kernel(order, left_t, left_next_t, right, out):
    left = jnp.concatenate([left_t[...].T, left_next_t[...].T], axis=0)
    out[...] = mm(left, right[...]).astype(out.dtype)


def project(order, left_t, right, rows, first, count):
    depth, width = right.shape
    begin = first // rows
    return pl.pallas_call(
        project_kernel,
        grid_spec=pltpu.PrefetchScalarGridSpec(
            num_scalar_prefetch=1,
            grid=(count // (2 * rows),),
            in_specs=[
                pl.BlockSpec((depth, rows), lambda i, order: (0, order[begin + 2 * i])),
                pl.BlockSpec((depth, rows), lambda i, order: (0, order[begin + 2 * i + 1])),
                pl.BlockSpec((depth, width), lambda i, order: (0, 0)),
            ],
            out_specs=pl.BlockSpec((2 * rows, width), lambda i, order: (i, 0)),
        ),
        out_shape=jax.ShapeDtypeStruct((count, width), jnp.bfloat16),
        cost_estimate=pl.CostEstimate(
            flops=2 * count * depth * width,
            bytes_accessed=2 * (count * (depth + width) + depth * width),
            transcendentals=0,
        ),
        name="project",
    )(order, left_t, left_t, right)


scalars = pl.BlockSpec(memory_space=pltpu.SMEM)
vectors = pl.BlockSpec(memory_space=pltpu.VMEM)


def lanes(order, index, rows):
    return pl.ds(pl.multiple_of(order[index] * rows, rows), rows)


def stack_kernel(rows, order, left_t, *refs):
    *blocks, out = refs
    for index in range(0, len(blocks), 4):
        four = range(index, index + 4)
        left = jnp.concatenate([left_t[:, lanes(order, i, rows)] for i in four], axis=1)
        right = jnp.concatenate([blocks[i][:rows] for i in four], axis=0)
        term = mm(left, right)
        if index == 0:
            out[...] = term
        else:
            out[...] += term


def stack_product(order, left_t, rows, blocks):
    width = blocks[0].shape[1]
    return pl.pallas_call(
        functools.partial(stack_kernel, rows),
        in_specs=[scalars, vectors] + [vectors] * len(blocks),
        out_specs=vectors,
        out_shape=jax.ShapeDtypeStruct((left_t.shape[0], width), jnp.float32),
        cost_estimate=pl.CostEstimate(
            flops=2 * left_t.size * width,
            bytes_accessed=2 * len(blocks) * rows * width,
            transcendentals=0,
        ),
        name="stack_product",
    )(order, left_t, *blocks)


def heads_kernel(rows, order, weight, *refs):
    *blocks, query_t, key_t, value, value_t, squares = refs
    for index in range(0, len(blocks), 4):
        four = range(index, index + 4)
        raw = mm(jnp.concatenate([blocks[i][:rows] for i in four], axis=0), weight[...])
        for i in four:
            own = raw[(i - index) * rows : (i - index + 1) * rows]
            here = lanes(order, i, rows)
            query = own[:, :HEAD_DIM].T
            key = own[:, HEAD_DIM : 2 * HEAD_DIM].T
            query_t[:, here] = query
            key_t[:, here] = key
            value[here, :] = own[:, 2 * HEAD_DIM :].astype(value.dtype)
            value_t[:, here] = own[:, 2 * HEAD_DIM :].T.astype(value.dtype)
            squares[0:1, here] = jnp.sum(query * query, axis=0, keepdims=True)
            squares[1:2, here] = jnp.sum(key * key, axis=0, keepdims=True)


def heads_in(order, weight, rows, blocks):
    width = blocks[0].shape[1]
    count = len(blocks) * rows
    return pl.pallas_call(
        functools.partial(heads_kernel, rows),
        in_specs=[scalars, vectors] + [vectors] * len(blocks),
        out_specs=[vectors] * 5,
        out_shape=[
            jax.ShapeDtypeStruct((HEAD_DIM, count), jnp.float32),
            jax.ShapeDtypeStruct((HEAD_DIM, count), jnp.float32),
            jax.ShapeDtypeStruct((count, HEAD_DIM), jnp.bfloat16),
            jax.ShapeDtypeStruct((HEAD_DIM, count), jnp.bfloat16),
            jax.ShapeDtypeStruct((2, count), jnp.float32),
        ],
        cost_estimate=pl.CostEstimate(
            flops=2 * count * width * 3 * HEAD_DIM,
            bytes_accessed=2 * count * width,
            transcendentals=0,
        ),
        name="heads_in",
    )(order, weight, *blocks)


def out_kernel(rows, where, attended, resid, gain, *refs):
    *blocks, far_one, far_two, cross, middle, normed = refs
    count = len(blocks)
    half = HEAD_DIM // 2
    first_group = where[count] == 0
    total = resid[...].astype(jnp.float32)
    far_rows = [far_one[...], far_two[...], cross[: 4 * half], cross[4 * half :]]
    for index in range(0, count, 4):
        near_left, far_left = [], []
        for i in range(index, index + 4):
            columns = attended[where[i]].astype(jnp.float32)
            low, high = columns[:, :half], columns[:, half:]
            near_left.append(jnp.where(first_group, low, high))
            far_left.append(jnp.where(first_group, high, low))
        near = jnp.concatenate([blocks[i][rows:] for i in range(index, index + 4)], axis=0)
        total += mm(jnp.concatenate(near_left, axis=1).astype(jnp.bfloat16), near)
        total += mm(jnp.concatenate(far_left, axis=1).astype(jnp.bfloat16), far_rows[index // 4])
    middle[...] = total
    inverse = lax.rsqrt(jnp.mean(total * total, axis=-1, keepdims=True) + eps)
    normed[...] = (total * inverse * gain[...]).astype(normed.dtype)


def out_project(where, attended, resid, gain, rows, blocks, far):
    width = resid.shape[1]
    return pl.pallas_call(
        functools.partial(out_kernel, rows),
        in_specs=[scalars] + [vectors] * (3 + len(blocks) + len(far)),
        out_specs=[vectors] * 2,
        out_shape=[
            jax.ShapeDtypeStruct((rows, width), jnp.float32),
            jax.ShapeDtypeStruct((rows, width), jnp.bfloat16),
        ],
        cost_estimate=pl.CostEstimate(
            flops=2 * rows * width * width,
            bytes_accessed=2 * width * width,
            transcendentals=0,
        ),
        name="out_project",
    )(where, attended, resid, gain, *blocks, *far)


def out_back_kernel(rows, where, branch, *refs):
    *blocks, far_one, far_two, cross, out = refs
    count = len(blocks)
    half = HEAD_DIM // 2
    first_group = where[count] == 0
    far_rows = [far_one[...], far_two[...], cross[: 4 * half], cross[4 * half :]]
    for index in range(0, count, 4):
        near = jnp.concatenate([blocks[i][rows:] for i in range(index, index + 4)], axis=0)
        near = contract_cols(branch[...], near)
        far = contract_cols(branch[...], far_rows[index // 4])
        for i in range(index, index + 4):
            here = slice((i - index) * half, (i - index + 1) * half)
            low = jnp.where(first_group, near[:, here], far[:, here])
            high = jnp.where(first_group, far[:, here], near[:, here])
            out[where[i]] = jnp.concatenate([low, high], axis=1).astype(out.dtype)


def out_project_back(where, branch, rows, blocks, far):
    width = branch.shape[1]
    return pl.pallas_call(
        functools.partial(out_back_kernel, rows),
        in_specs=[scalars] + [vectors] * (1 + len(blocks) + len(far)),
        out_specs=vectors,
        out_shape=jax.ShapeDtypeStruct((len(blocks), rows, HEAD_DIM), jnp.bfloat16),
        cost_estimate=pl.CostEstimate(
            flops=2 * rows * width * width,
            bytes_accessed=2 * width * width,
            transcendentals=0,
        ),
        name="out_project_back",
    )(where, branch, *blocks, *far)


def turn(values, cosine, rope_sine):
    half = HEAD_DIM // 2
    first, second = values[:half], values[half:]
    return jnp.concatenate(
        [first * cosine - second * rope_sine, second * cosine + first * rope_sine], axis=0
    )


def attend_kernel(
    query_raw,
    key_raw,
    value_t,
    inverse,
    inverse_all,
    gains,
    cosine,
    rope_sine,
    cosine_all,
    rope_sine_all,
    key_seg,
    query_seg,
    query_t,
    query,
    key_t,
    key,
    out,
    out_t,
    log_total,
):
    @pl.when(pl.program_id(0) == 0)
    def _():
        turned = turn(
            key_raw[...] * inverse_all[1:2, :] * gains[:, 1:2], cosine_all[...], rope_sine_all[...]
        ).astype(jnp.bfloat16)
        key_t[...] = turned
        key[...] = turned.T

    turned = turn(
        query_raw[...] * inverse[0:1, :] * gains[:, 0:1], cosine[...], rope_sine[...]
    ).astype(jnp.bfloat16)
    query_t[...] = turned
    query[...] = turned.T
    scores = mm(key[...], turned) * score_scale
    scores = jnp.where(key_seg[:, :1] == query_seg[...], scores, negative)
    peak = jnp.max(scores, axis=0, keepdims=True)
    weights = jnp.exp(scores - peak)
    total = jnp.sum(weights, axis=0, keepdims=True)
    result = mm(value_t[...], weights.astype(jnp.bfloat16)) / total
    out_t[...] = result.astype(out_t.dtype)
    out[...] = result.T.astype(out.dtype)
    log_total[...] = peak + jnp.log(total)


def attend(query_raw, key_raw, value_t, inverse, gains, cosine, rope_sine, key_seg, query_seg):
    count = query_raw.shape[1]
    whole = lambda i: (0, 0)
    across = lambda rows: pl.BlockSpec((rows, query_block), lambda i: (0, i))
    down = pl.BlockSpec((query_block, HEAD_DIM), lambda i: (i, 0))
    all_of = lambda rows: pl.BlockSpec((rows, count), whole)
    low, half = jnp.bfloat16, HEAD_DIM // 2
    return pl.pallas_call(
        attend_kernel,
        grid=(count // query_block,),
        in_specs=[
            across(HEAD_DIM),
            all_of(HEAD_DIM),
            all_of(HEAD_DIM),
            across(2),
            all_of(2),
            pl.BlockSpec((HEAD_DIM, 2), whole),
            across(half),
            across(half),
            all_of(half),
            all_of(half),
            pl.BlockSpec((count, HEAD_DIM), whole),
            across(1),
        ],
        out_specs=[
            across(HEAD_DIM),
            down,
            all_of(HEAD_DIM),
            pl.BlockSpec((count, HEAD_DIM), whole),
            down,
            across(HEAD_DIM),
            across(1),
        ],
        out_shape=[
            jax.ShapeDtypeStruct((HEAD_DIM, count), low),
            jax.ShapeDtypeStruct((count, HEAD_DIM), low),
            jax.ShapeDtypeStruct((HEAD_DIM, count), low),
            jax.ShapeDtypeStruct((count, HEAD_DIM), low),
            jax.ShapeDtypeStruct((count, HEAD_DIM), low),
            jax.ShapeDtypeStruct((HEAD_DIM, count), low),
            jax.ShapeDtypeStruct((1, count), jnp.float32),
        ],
        cost_estimate=pl.CostEstimate(
            flops=4 * count * count * HEAD_DIM,
            bytes_accessed=count * HEAD_DIM * 24,
            transcendentals=count * count,
        ),
        name="attend",
    )(
        query_raw,
        key_raw,
        value_t,
        inverse,
        inverse,
        gains,
        cosine,
        rope_sine,
        cosine,
        rope_sine,
        key_seg,
        query_seg,
    )


def attend_back_kernel(
    key_seg,
    query_seg,
    log_total,
    query_t,
    query,
    upstream,
    key,
    key_t,
    value,
    query_raw,
    key_raw,
    inverse,
    inverse_all,
    gains,
    cosine,
    rope_sine,
    cosine_all,
    rope_sine_all,
    weighted_query,
    weighted_key,
    dvalue_t,
    inner_query,
    inner_key,
    gain_sums,
    dkey,
    dvalue,
):
    step = pl.program_id(0)

    @pl.when(step == 0)
    def _():
        dkey[...] = jnp.zeros_like(dkey)
        dvalue[...] = jnp.zeros_like(dvalue)
        gain_sums[...] = jnp.zeros_like(gain_sums)

    scores = mm(key[...], query_t[...]) * score_scale
    probs = jnp.where(key_seg[:, :1] == query_seg[...], jnp.exp(scores - log_total[...]), 0.0)
    dvalue[...] += mm(probs.astype(jnp.bfloat16), upstream[...])
    dprobs = contract_cols(value[...], upstream[...])
    delta = jnp.sum(probs * dprobs, axis=0, keepdims=True)
    dscores = (probs * (dprobs - delta)).astype(jnp.bfloat16)
    dkey[...] += mm(dscores, query[...])
    turned = turn(mm(key_t[...], dscores) * score_scale, cosine[...], -rope_sine[...])
    product = turned * (query_raw[...] * inverse[0:1, :])
    weighted_query[...] = turned * gains[:, 0:1]
    inner_query[...] = jnp.sum(product * gains[:, 0:1], axis=0, keepdims=True)
    gain_sums[:, 0:1] += jnp.sum(product, axis=1, keepdims=True)

    @pl.when(step == pl.num_programs(0) - 1)
    def _():
        turned = turn(dkey[...].T * score_scale, cosine_all[...], -rope_sine_all[...])
        product = turned * (key_raw[...] * inverse_all[1:2, :])
        weighted_key[...] = turned * gains[:, 1:2]
        inner_key[...] = jnp.sum(product * gains[:, 1:2], axis=0, keepdims=True)
        gain_sums[:, 1:2] = jnp.sum(product, axis=1, keepdims=True)
        dvalue_t[...] = dvalue[...].T.astype(dvalue_t.dtype)


def attend_back(
    key_seg,
    query_seg,
    log_total,
    query_t,
    query,
    upstream,
    key,
    key_t,
    value,
    query_raw,
    key_raw,
    inverse,
    gains,
    cosine,
    rope_sine,
):
    count = query.shape[0]
    whole = lambda i: (0, 0)
    across = lambda rows: pl.BlockSpec((rows, query_block), lambda i: (0, i))
    down = pl.BlockSpec((query_block, HEAD_DIM), lambda i: (i, 0))
    all_of = lambda rows: pl.BlockSpec((rows, count), whole)
    tall = pl.BlockSpec((count, HEAD_DIM), whole)
    half = HEAD_DIM // 2
    return pl.pallas_call(
        attend_back_kernel,
        grid=(count // query_block,),
        in_specs=[
            tall,
            across(1),
            across(1),
            across(HEAD_DIM),
            down,
            down,
            tall,
            all_of(HEAD_DIM),
            tall,
            across(HEAD_DIM),
            all_of(HEAD_DIM),
            across(2),
            all_of(2),
            pl.BlockSpec((HEAD_DIM, 2), whole),
            across(half),
            across(half),
            all_of(half),
            all_of(half),
        ],
        out_specs=[
            across(HEAD_DIM),
            all_of(HEAD_DIM),
            all_of(HEAD_DIM),
            across(1),
            all_of(1),
            pl.BlockSpec((HEAD_DIM, 2), whole),
        ],
        out_shape=[
            jax.ShapeDtypeStruct((HEAD_DIM, count), jnp.float32),
            jax.ShapeDtypeStruct((HEAD_DIM, count), jnp.float32),
            jax.ShapeDtypeStruct((HEAD_DIM, count), jnp.bfloat16),
            jax.ShapeDtypeStruct((1, count), jnp.float32),
            jax.ShapeDtypeStruct((1, count), jnp.float32),
            jax.ShapeDtypeStruct((HEAD_DIM, 2), jnp.float32),
        ],
        scratch_shapes=[
            pltpu.VMEM((count, HEAD_DIM), jnp.float32),
            pltpu.VMEM((count, HEAD_DIM), jnp.float32),
        ],
        cost_estimate=pl.CostEstimate(
            flops=10 * count * count * HEAD_DIM,
            bytes_accessed=count * HEAD_DIM * 40,
            transcendentals=count * count,
        ),
        name="attend_back",
    )(
        key_seg,
        query_seg,
        log_total,
        query_t,
        query,
        upstream,
        key,
        key_t,
        value,
        query_raw,
        key_raw,
        inverse,
        inverse,
        gains,
        cosine,
        rope_sine,
        cosine,
        rope_sine,
    )


def local(
    tokens,
    segments,
    routes,
    route_gates,
    attn_gain,
    query_gain,
    key_gain,
    ffn_gain,
    w_query,
    w_key,
    w_value,
    w_out,
    w_gate,
    w_up,
    w_down,
    cotangent,
):
    row_count, width = tokens.shape
    top_count = routes.shape[1]
    devices = lax.axis_size("expert")
    groups = lax.axis_size("dp")
    me = lax.axis_index("expert")
    my_group = lax.axis_index("dp")
    seq_length = row_count * devices
    part = width // devices
    sharing = HEAD_DIM // part
    head = me // sharing
    sub = me % sharing
    w_rows = w_query.shape[0]
    w_half = w_rows // 2

    grouped = devices == 16 and groups == 2
    order = arrival_order(me) if grouped else jnp.arange(devices, dtype=jnp.int32)
    where = jnp.concatenate([order, my_group[None].astype(jnp.int32)])

    def gather(block):
        return Rounds(gather_rounds(block) if grouped else gather_whole(block))

    def scatter(make):
        return Rounds((scatter_rounds if grouped else scatter_whole)(make, seq_length))

    def exchange(values):
        return lax.all_to_all(values, "expert", split_axis=0, concat_axis=0, tiled=True)

    def to_heads(rows):
        blocks = rows.reshape(rows.shape[0], HEADS, HEAD_DIM).transpose(1, 0, 2)
        return jnp.repeat(blocks, sharing, axis=0)

    def my_part(columns, axis):
        if sharing == 1:
            return columns
        return lax.dynamic_slice_in_dim(columns, sub * part, part, axis=axis)

    def by_half(values, axis):
        return jnp.where(my_group == 0, values, jnp.flip(values, axis))

    def dp_start(values):
        return swap(values, "dp", 1) if groups == 2 else lax.psum(values, "dp")

    def dp_end(values, arrived):
        total = arrived.astype(jnp.float32)
        return total + values.astype(jnp.float32) if groups == 2 else total

    waiting = []

    def weight_grad(left, right):
        pieces = 4 if grouped else 1
        step = left.shape[1] // pieces
        own = [
            contract_rows(left[:, i * step : (i + 1) * step], right).astype(jnp.bfloat16)
            for i in range(pieces)
        ]
        far = [dp_start(values) for values in own]
        waiting.extend((far, i) for i in range(pieces))
        return own, far

    def weight_total(own, far):
        return (merge(own, far) if groups == 2 else far[0].astype(jnp.float32))[None]

    def cross(*others):
        if not (waiting and grouped):
            return others
        far, i = waiting.pop(0)
        *others, far[i] = together(*others, far[i])
        return others

    def ride(rounds, *others):
        if not (waiting and grouped):
            return rounds.step(*others)
        far, i = waiting.pop(0)
        *others, far[i] = rounds.step(*others, far[i])
        return others

    resid_in = tokens.astype(jnp.float32)
    pre_in, normal_in, inverse_in = norm_rows(resid_in, attn_gain)
    normed_in = pre_in.astype(jnp.bfloat16)

    experts_all = devices * w_gate.shape[0]
    slots = min(row_count, row_count * top_count * 3 // (2 * experts_all))
    hits = routes[:, :, None] == jnp.arange(experts_all, dtype=jnp.int32)[None, None, :]
    gate_table = jnp.sum(jnp.where(hits, route_gates[:, :, None], 0.0), axis=1).T
    gate_high = lax.reduce_precision(gate_table, exponent_bits=8, mantissa_bits=7)
    gate_rows = jnp.pad(
        jnp.stack([gate_high, gate_table - gate_high], axis=1).astype(jnp.bfloat16),
        ((0, 0), (0, 14), (0, 3 * HEAD_DIM - row_count)),
    )
    if grouped:
        take = lambda w: lax.dynamic_slice_in_dim(w, my_group * w_half, w_half)
    else:
        take = lambda w: w
    sent_w = jnp.concatenate([to_heads(take(w)) for w in (w_query, w_key, w_value)], axis=2)
    taken = sent_w.shape[1]
    arrived = exchange(jnp.concatenate([sent_w, gate_rows], axis=1))

    if grouped:
        rounds = gather(jnp.concatenate([normed_in, take(w_out)], axis=0))
        rounds.step()
        rounds.step()
        (arrived,) = rounds.step(arrived)
        head_w = arrived[:, :taken]
        head_w_far = swap(head_w, "dp", 1)
        (head_w_far,) = rounds.step(head_w_far)
        blocks = rounds.finish()
        head_w = by_half(jnp.stack([head_w, head_w_far], axis=1), 1).reshape(width, 3 * HEAD_DIM)
        out_far = [
            swap(jnp.concatenate([block[row_count:] for block in some], axis=0), "dp", 1)
            for some in (blocks[:4], blocks[4:8])
        ]
    else:
        blocks = gather(normed_in).finish()
        head_w = arrived[:, :taken].reshape(width, 3 * HEAD_DIM)
        out_full = lax.all_gather(w_out, "expert", axis=0, tiled=True)

    gate_pair = arrived[:, taken : taken + 2, :row_count].astype(jnp.float32)
    gate_mine = (gate_pair[:, 0] + gate_pair[:, 1])[order]
    chosen = gate_mine > 0.0
    before = jnp.arange(row_count)[:, None] < jnp.arange(row_count)[None, :]
    rank = mm(chosen.astype(jnp.bfloat16), before.astype(jnp.bfloat16)).astype(jnp.int32)
    rank = jnp.where(chosen, rank, -1)
    slot = jnp.arange(slots, dtype=jnp.int32)
    picks = rank[:, None, :] == slot[None, :, None]
    slot_gate = jnp.sum(jnp.where(picks, gate_mine[:, None, :], 0.0), axis=2).reshape(-1, 1)
    picks = picks.astype(jnp.bfloat16)
    unpicks = (rank[:, :, None] == slot[None, None, :]).astype(jnp.bfloat16)
    ones = jnp.ones_like(slot_gate)

    key_seg = jnp.broadcast_to(segments[:, None], (seq_length, HEAD_DIM))
    query_seg = segments[None, :]
    cosine, rope_sine = rope_tables(jnp.arange(seq_length, dtype=jnp.int32))
    gains = jnp.stack(
        [
            lax.dynamic_slice_in_dim(query_gain, head * HEAD_DIM, HEAD_DIM),
            lax.dynamic_slice_in_dim(key_gain, head * HEAD_DIM, HEAD_DIM),
        ],
        axis=1,
    )

    cot_rounds = gather(cotangent)
    query_raw, key_raw, value, value_t, squares = heads_in(order, head_w, row_count, blocks)
    if sharing > 1:
        squares = jnp.stack(
            [jnp.sum(jnp.square(my_part(raw, 0)), axis=0) for raw in (query_raw, key_raw)]
        )
    (squares,) = cot_rounds.step(squares)
    squares = butterfly(squares, "expert")
    if grouped:
        squares, out_far[0] = cot_rounds.step(squares, out_far[0])
    inverse = lax.rsqrt(squares / width + eps)
    query_t, query, key_t, key, attended, attended_t, log_total = attend(
        query_raw, key_raw, value_t, inverse, gains, cosine, rope_sine, key_seg, query_seg
    )
    if grouped:
        attended, out_far[1] = cot_rounds.step(attended, out_far[1])
        out_cross = send(jnp.concatenate(out_far, axis=0), swap_core)

    attended_low = exchange(my_part(attended, 1).reshape(devices, row_count, part))
    (attended_low,) = cot_rounds.step(attended_low)
    if grouped:
        out_far.append(out_cross)
        middle, normed_mid = out_project(
            where, attended_low, tokens, ffn_gain[None, :], row_count, blocks, out_far
        )
    else:
        attended_low = attended_low.transpose(1, 0, 2).reshape(row_count, width)
        middle = resid_in + mm(attended_low, out_full)
        normed_mid = norm_rows(middle, ffn_gain)[0].astype(jnp.bfloat16)
    (normed_mid,) = cot_rounds.step(normed_mid)
    cot_blocks = cot_rounds.finish()

    mid_rounds = gather(normed_mid)
    grad_eo = pick(picks, slot_gate, cot_blocks)
    (grad_eo,) = mid_rounds.step(grad_eo)
    rows_in = pick(picks, ones, mid_rounds.finish())
    gate_in = mm(rows_in, w_gate[0])
    up_in = mm(rows_in, w_up[0])
    sigmoid_in = jax.nn.sigmoid(gate_in)
    silu_in = gate_in * sigmoid_in
    hidden = (silu_in * up_in).astype(jnp.bfloat16)
    grad_down, down_far = weight_grad(hidden, grad_eo)

    def give_back(rows):
        blocks = rows.reshape(devices, slots, width)

        def some(first, count):
            here = slice(first // row_count, (first + count) // row_count)
            return jnp.einsum(
                "bts,bsd->btd",
                unpicks[here],
                blocks[here],
                preferred_element_type=jnp.bfloat16,
            ).reshape(count, width)

        return some

    hidden_next, grad_eo_next = together(hidden, grad_eo, *grad_down)[:2]
    expert_out = (mm(hidden_next, w_down[0]) * slot_gate).astype(jnp.bfloat16)
    out_rounds = scatter(give_back(expert_out))
    grad_hidden = contract_cols(grad_eo_next, w_down[0])
    grad_up_pre = (grad_hidden * silu_in).astype(jnp.bfloat16)
    grad_gate_pre = (
        grad_hidden * up_in * sigmoid_in * (1.0 + gate_in * (1.0 - sigmoid_in))
    ).astype(jnp.bfloat16)
    grad_up_pre, grad_gate_pre = ride(out_rounds, grad_up_pre, grad_gate_pre)
    grad_rows = contract_cols(grad_gate_pre, w_gate[0])
    (grad_rows,) = out_rounds.step(grad_rows)
    grad_rows = (grad_rows + contract_cols(grad_up_pre, w_up[0])).astype(jnp.bfloat16)
    (grad_rows,) = ride(out_rounds, grad_rows)
    row_rounds = scatter(give_back(grad_rows))
    out_rounds.step()
    row_rounds.step()
    out_rounds.step()
    mixed = out_rounds.finish()
    activations = (middle + mixed).astype(jnp.bfloat16)

    grad_gate, gate_far = weight_grad(rows_in, grad_gate_pre)
    ride(row_rounds)
    row_rounds.step(*grad_gate)
    grad_up, up_far = weight_grad(rows_in, grad_up_pre)
    ride(row_rounds)
    row_rounds.step(*grad_up)
    grad_normed_mid = row_rounds.finish()

    grad_out = cotangent.astype(jnp.float32)
    _, normal_mid, inverse_mid = norm_rows(middle, ffn_gain)
    mid_back, grad_ffn_gain = norm_back(grad_normed_mid, normal_mid, inverse_mid, ffn_gain)
    grad_middle = grad_out + mid_back
    grad_branch = grad_middle.astype(jnp.bfloat16)
    (grad_branch,) = cross(grad_branch)
    if grouped:
        grad_columns = out_project_back(where, grad_branch, row_count, blocks, out_far)
    else:
        grad_columns = to_heads(contract_cols(grad_branch, out_full).astype(jnp.bfloat16))
    grad_attended = exchange(grad_columns).reshape(seq_length, HEAD_DIM)
    (grad_attended,) = cross(grad_attended)

    branch_rounds = gather(after(grad_branch, grad_attended))
    weighted_query, weighted_key, grad_value_t, inner_query, inner_key, gain_sums = attend_back(
        key_seg,
        query_seg,
        log_total,
        query_t,
        query,
        grad_attended,
        key,
        key_t,
        value,
        query_raw,
        key_raw,
        inverse,
        gains,
        cosine,
        rope_sine,
    )
    inner = jnp.concatenate([inner_query, inner_key], axis=0)
    if sharing > 1:
        inner = jnp.stack(
            [
                jnp.sum(my_part(weighted * raw * at, 0), axis=0)
                for weighted, raw, at in (
                    (weighted_query, query_raw, inverse[0:1]),
                    (weighted_key, key_raw, inverse[1:2]),
                )
            ]
        )
    (inner,) = ride(branch_rounds, inner)
    inner = butterfly(inner, "expert") / width
    (inner,) = branch_rounds.step(inner)
    grad_raw_t = jnp.concatenate(
        [
            my_part(
                (at * (weighted - raw * at * mean)).astype(jnp.bfloat16),
                0,
            )
            for weighted, raw, at, mean in (
                (weighted_query, query_raw, inverse[0:1], inner[0:1]),
                (weighted_key, key_raw, inverse[1:2], inner[1:2]),
            )
        ]
        + [my_part(grad_value_t, 0)],
        axis=0,
    )
    head_w_t = jnp.concatenate(
        [my_part(head_w[:, i * HEAD_DIM : (i + 1) * HEAD_DIM], 1).T for i in range(3)], axis=0
    )
    grad_w_t = stack_product(order, grad_raw_t, row_count, blocks)
    grad_attn_gain = jnp.sum(grad_w_t * head_w_t.astype(jnp.float32), axis=0) / attn_gain
    w_columns = exchange(
        grad_w_t.astype(jnp.bfloat16).reshape(3 * part, devices, w_rows).transpose(1, 0, 2)
    )
    (grad_raw_t,) = ride(branch_rounds, grad_raw_t)
    in_rounds = scatter(
        lambda first, count: project(order, grad_raw_t, head_w_t, row_count, first, count)
    )
    (w_columns,) = branch_rounds.step(w_columns)
    ride(in_rounds, *branch_rounds.sent)
    dense = [
        w_columns[:, i * part : (i + 1) * part].reshape(width, w_rows).T for i in range(3)
    ]
    branch_blocks = branch_rounds.finish()
    out_part = stack_product(
        order, my_part(attended_t, 0), row_count, branch_blocks
    ).astype(jnp.bfloat16)
    in_rounds.step()
    ride(in_rounds)
    out_part, *dense = in_rounds.step(out_part, *dense)
    dense_far = [dp_start(values) for values in dense]
    out_part_far = dp_start(out_part)
    ride(in_rounds)
    grad_normed_in = in_rounds.finish()
    in_back, _ = norm_back(grad_normed_in, normal_in, inverse_in, attn_gain)
    input_grad = (grad_middle + in_back).astype(jnp.bfloat16)

    def placed(values):
        return lax.dynamic_update_slice_in_dim(
            jnp.zeros((width,), jnp.float32), values, me * part, 0
        )

    gain_total = butterfly(
        butterfly(
            jnp.stack(
                [
                    grad_attn_gain,
                    placed(my_part(gain_sums[:, 0], 0)),
                    placed(my_part(gain_sums[:, 1], 0)),
                    grad_ffn_gain,
                ]
            ),
            "expert",
        ),
        "dp",
    )
    return (
        activations,
        input_grad,
        gain_total[0],
        gain_total[1],
        gain_total[2],
        gain_total[3],
        dp_end(dense[0], dense_far[0]),
        dp_end(dense[1], dense_far[1]),
        dp_end(dense[2], dense_far[2]),
        dp_end(out_part, out_part_far),
        weight_total(grad_gate, gate_far),
        weight_total(grad_up, up_far),
        weight_total(grad_down, down_far),
    )


def solution(mesh):
    in_specs = (
        P(("dp", "expert"), None),
        P("dp"),
        P(("dp", "expert"), None),
        P(("dp", "expert"), None),
        P(),
        P(),
        P(),
        P(),
        P("expert", None),
        P("expert", None),
        P("expert", None),
        P("expert", None),
        P("expert", None, None),
        P("expert", None, None),
        P("expert", None, None),
        P(("dp", "expert"), None),
    )
    out_specs = (
        P(("dp", "expert"), None),
        P(("dp", "expert"), None),
        P(),
        P(),
        P(),
        P(),
        P("expert", None),
        P("expert", None),
        P("expert", None),
        P("expert", None),
        P("expert", None, None),
        P("expert", None, None),
        P("expert", None, None),
    )
    return jax.shard_map(local, mesh=mesh, in_specs=in_specs, out_specs=out_specs, check_vma=False)
```

```python
import functools

import jax
import jax.numpy as jnp
from jax import lax
from jax.experimental import pallas as pl
from jax.experimental.pallas import tpu as pltpu
from jax.sharding import PartitionSpec as P

HEADS = 16
HEAD_DIM = 128


eps = 1e-05
rope_base = 50000.0
negative = -1e30
score_scale = HEAD_DIM ** (-0.5)
query_block = 256


def norm_rows(values, norm_gain):
    inverse = lax.rsqrt(jnp.mean(values * values, axis=-1, keepdims=True) + eps)
    normal = values * inverse
    return (normal * norm_gain, normal, inverse)


def norm_back(upstream, normal, inverse, norm_gain):
    weighted = upstream * norm_gain
    inner_mean = jnp.mean(weighted * normal, axis=-1, keepdims=True)
    return (inverse * (weighted - normal * inner_mean), jnp.sum(upstream * normal, axis=0))


def rope_tables(positions):
    half_dim = HEAD_DIM // 2
    frequency = rope_base ** (-(jnp.arange(half_dim, dtype=jnp.float32) * 2.0 / HEAD_DIM))
    theta = frequency[:, None] * positions.astype(jnp.float32)[None, :]
    return (jnp.cos(theta), jnp.sin(theta))


def mm(left, right):
    return jnp.dot(left, right, preferred_element_type=jnp.float32)


def contract_rows(left, right):
    return lax.dot_general(
        left, right, (((0,), (0,)), ((), ())), preferred_element_type=jnp.float32
    )


def contract_cols(left, right):
    return lax.dot_general(
        left, right, (((1,), (1,)), ((), ())), preferred_element_type=jnp.float32
    )


def swap(values, axis, step):
    count = lax.axis_size(axis)
    return lax.ppermute(values, axis, [(i, i ^ step) for i in range(count)])


def together(*values):
    return lax.optimization_barrier(values)


def after(values, *others):
    return lax.optimization_barrier((values,) + others)[0]


def butterfly(values, axis):
    step = 1
    while step < lax.axis_size(axis):
        values = values + swap(values, axis, step)
        step *= 2
    return values


near_order = ((0, 1, 2, 3), (1, 0, 2, 3), (2, 3, 1, 0), (3, 2, 1, 0))


def moves(target):
    pairs = []
    for index in range(16):
        far = target(index // 4)
        if far is not None:
            pairs.append((index, far * 4 + index % 4))
    return pairs


swap_near = moves(lambda z: z ^ 1)
swap_middle = moves(lambda z: {1: 2, 2: 1}.get(z))
move_out = moves(lambda z: {1: 0, 2: 3}.get(z))
move_in = moves(lambda z: {0: 1, 3: 2}.get(z))
swap_row = [(i, i ^ 2) for i in range(16)]
swap_core = [(i, i ^ 1) for i in range(16)]


def send(values, pairs):
    return lax.ppermute(values, "expert", pairs)


def arrival_order(me):
    near = jnp.asarray(near_order, jnp.int32)[me // 4] * 4
    row, core = (me // 2) % 2, me % 2
    return jnp.concatenate(
        [near + (row ^ j) * 2 + (core ^ i) for i in (0, 1) for j in (0, 1)]
    ).astype(jnp.int32)


class Rounds:
    def __init__(self, steps):
        self.steps = steps
        self.result = None
        self.over = False
        self.sent = ()
        self._go(None)

    def _go(self, arrived):
        try:
            self.sent = self.steps.send(arrived)
        except StopIteration as stop:
            self.result, self.sent, self.over = stop.value, (), True

    def step(self, *others):
        return step_all([self], *others)

    def finish(self):
        while not self.over:
            self.step()
        return self.result


def step_all(rounds, *others):
    sent = [values for one in rounds for values in one.sent]
    values = together(*sent, *others) if sent or others else ()
    at = 0
    for one in rounds:
        count = len(one.sent)
        if not one.over:
            one._go(values[at : at + count])
        at += count
    return values[at:]


def gather_rounds(block):
    at = lax.axis_index("expert") // 4
    outer = (at == 0) | (at == 3)
    first, second, row = yield (
        send(block, swap_near),
        send(block, swap_middle),
        send(block, swap_row),
    )
    third, second_out, row_first, core = yield (
        send(first, swap_middle),
        send(second, move_out),
        send(first, swap_row),
        send(block, swap_core),
    )
    second = jnp.where(outer, second_out, second)
    third_out, row_second, core_first, core_row = yield (
        send(third, move_out),
        send(second, swap_row),
        send(first, swap_core),
        send(row, swap_core),
    )
    third = jnp.where(outer, third_out, third)
    row_third, core_second, core_third, core_row_first, core_row_second = yield (
        send(third, swap_row),
        send(second, swap_core),
        send(third, swap_core),
        send(row_first, swap_core),
        send(row_second, swap_core),
    )
    (core_row_third,) = yield (send(row_third, swap_core),)
    return [
        block,
        first,
        second,
        third,
        row,
        row_first,
        row_second,
        row_third,
        core,
        core_first,
        core_second,
        core_third,
        core_row,
        core_row_first,
        core_row_second,
        core_row_third,
    ]


def gather_whole(block):
    yield ()
    return list(lax.all_gather(block, "expert", axis=0))


def add_low(left, right):
    return (left.astype(jnp.float32) + right.astype(jnp.float32)).astype(jnp.bfloat16)


def scatter_rounds(make, count, tie):
    (far,) = yield (send(tie(make(count // 2, count // 2)), swap_core),)
    close = make(0, count // 2)
    rows = count // 16

    def both(j, k):
        here = slice((j * 4 + k) * rows, (j * 4 + k + 1) * rows)
        return add_low(close[here], far[here])

    (row,) = yield (send(both(1, 3), swap_row),)
    third = add_low(both(0, 3), row)
    row, third_in = yield (send(both(1, 2), swap_row), send(third, move_in))
    second = add_low(both(0, 2), row)
    third = add_low(third, third_in)
    row, second_in, third_in = yield (
        send(both(1, 1), swap_row),
        send(second, move_in),
        send(third, swap_middle),
    )
    first = add_low(add_low(both(0, 1), row), third_in)
    second = add_low(second, second_in)
    row, second_in, first_in = yield (
        send(both(1, 0), swap_row),
        send(second, swap_middle),
        send(first, swap_near),
    )
    return (
        both(0, 0).astype(jnp.float32)
        + row.astype(jnp.float32)
        + second_in.astype(jnp.float32)
        + first_in.astype(jnp.float32)
    )


def scatter_whole(make, count, tie):
    yield ()
    return lax.psum_scatter(
        tie(make(0, count)), "expert", scatter_dimension=0, tiled=True
    ).astype(jnp.float32)


def pick_kernel(picks, scale, *refs):
    *blocks, out = refs
    slots = picks.shape[1]
    for index, block in enumerate(blocks):
        here = slice(index * slots, (index + 1) * slots)
        out[here, :] = (mm(picks[index], block[...]) * scale[here, :]).astype(out.dtype)


def pick(picks, scale, blocks):
    count, slots, tokens = picks.shape
    width = blocks[0].shape[1]
    return pl.pallas_call(
        pick_kernel,
        out_shape=jax.ShapeDtypeStruct((count * slots, width), jnp.bfloat16),
        cost_estimate=pl.CostEstimate(
            flops=2 * count * tokens * slots * width,
            bytes_accessed=2 * count * (tokens + slots) * width,
            transcendentals=0,
        ),
        name="pick",
    )(picks, scale, *blocks)


def merge_kernel(count, parts, *refs):
    pairs, outs = refs[: 2 * count], refs[-parts:]
    width = outs[0].shape[1]
    for index in range(count):

        @pl.when(pl.program_id(0) == index)
        def _():
            total = pairs[index][...].astype(jnp.float32) + pairs[count + index][...].astype(
                jnp.float32
            )
            for i, out in enumerate(outs):
                out[...] = total[:, i * width : (i + 1) * width]


def merge(own, far, parts, pieces=None, before=None):
    count = len(own)
    begin = pieces if before else 0
    before = before or []
    pieces = begin + count if before else pieces or count
    rows, width = own[0].shape
    return pl.pallas_call(
        functools.partial(merge_kernel, count, parts),
        grid=(count,),
        in_specs=[pl.BlockSpec((rows, width), lambda i: (0, 0))] * (2 * count)
        + [pl.BlockSpec(memory_space=pl.ANY)] * len(before),
        out_specs=[pl.BlockSpec((rows, width // parts), lambda i: (begin + i, 0))] * parts,
        out_shape=[jax.ShapeDtypeStruct((pieces * rows, width // parts), jnp.float32)] * parts,
        input_output_aliases={2 * count + i: i for i in range(len(before))},
        cost_estimate=pl.CostEstimate(
            flops=count * rows * width,
            bytes_accessed=8 * count * rows * width,
            transcendentals=0,
        ),
        name="merge",
    )(*own, *far, *before)


def project_kernel(order, left_t, left_next_t, right, out):
    left = jnp.concatenate([left_t[...].T, left_next_t[...].T], axis=0)
    out[...] = mm(left, right[...]).astype(out.dtype)


def project(order, left_t, right, rows, first, count):
    depth, width = right.shape
    begin = first // rows
    return pl.pallas_call(
        project_kernel,
        grid_spec=pltpu.PrefetchScalarGridSpec(
            num_scalar_prefetch=1,
            grid=(count // (2 * rows),),
            in_specs=[
                pl.BlockSpec((depth, rows), lambda i, order: (0, order[begin + 2 * i])),
                pl.BlockSpec((depth, rows), lambda i, order: (0, order[begin + 2 * i + 1])),
                pl.BlockSpec((depth, width), lambda i, order: (0, 0)),
            ],
            out_specs=pl.BlockSpec((2 * rows, width), lambda i, order: (i, 0)),
        ),
        out_shape=jax.ShapeDtypeStruct((count, width), jnp.bfloat16),
        cost_estimate=pl.CostEstimate(
            flops=2 * count * depth * width,
            bytes_accessed=2 * (count * (depth + width) + depth * width),
            transcendentals=0,
        ),
        name="project",
    )(order, left_t, left_t, right)


scalars = pl.BlockSpec(memory_space=pltpu.SMEM)
vectors = pl.BlockSpec(memory_space=pltpu.VMEM)


def lanes(order, index, rows):
    return pl.ds(pl.multiple_of(order[index] * rows, rows), rows)


def stack_kernel(rows, order, left_t, *refs):
    *blocks, out = refs
    for index in range(0, len(blocks), 4):
        four = range(index, index + 4)
        left = jnp.concatenate([left_t[:, lanes(order, i, rows)] for i in four], axis=1)
        right = jnp.concatenate([blocks[i][:rows] for i in four], axis=0)
        term = mm(left, right)
        if index == 0:
            out[...] = term
        else:
            out[...] += term


def stack_product(order, left_t, rows, blocks):
    width = blocks[0].shape[1]
    return pl.pallas_call(
        functools.partial(stack_kernel, rows),
        in_specs=[scalars, vectors] + [vectors] * len(blocks),
        out_specs=vectors,
        out_shape=jax.ShapeDtypeStruct((left_t.shape[0], width), jnp.float32),
        cost_estimate=pl.CostEstimate(
            flops=2 * left_t.size * width,
            bytes_accessed=2 * len(blocks) * rows * width,
            transcendentals=0,
        ),
        name="stack_product",
    )(order, left_t, *blocks)


def heads_kernel(rows, order, weight, *refs):
    *blocks, query_t, key_t, value, value_t, squares = refs
    for index in range(0, len(blocks), 4):
        four = range(index, index + 4)
        raw = mm(jnp.concatenate([blocks[i][:rows] for i in four], axis=0), weight[...])
        for i in four:
            own = raw[(i - index) * rows : (i - index + 1) * rows]
            here = lanes(order, i, rows)
            query = own[:, :HEAD_DIM].T
            key = own[:, HEAD_DIM : 2 * HEAD_DIM].T
            query_t[:, here] = query
            key_t[:, here] = key
            value[here, :] = own[:, 2 * HEAD_DIM :].astype(value.dtype)
            value_t[:, here] = own[:, 2 * HEAD_DIM :].T.astype(value.dtype)
            squares[0:1, here] = jnp.sum(query * query, axis=0, keepdims=True)
            squares[1:2, here] = jnp.sum(key * key, axis=0, keepdims=True)


def heads_in(order, weight, rows, blocks):
    width = blocks[0].shape[1]
    count = len(blocks) * rows
    return pl.pallas_call(
        functools.partial(heads_kernel, rows),
        in_specs=[scalars, vectors] + [vectors] * len(blocks),
        out_specs=[vectors] * 5,
        out_shape=[
            jax.ShapeDtypeStruct((HEAD_DIM, count), jnp.float32),
            jax.ShapeDtypeStruct((HEAD_DIM, count), jnp.float32),
            jax.ShapeDtypeStruct((count, HEAD_DIM), jnp.bfloat16),
            jax.ShapeDtypeStruct((HEAD_DIM, count), jnp.bfloat16),
            jax.ShapeDtypeStruct((2, count), jnp.float32),
        ],
        cost_estimate=pl.CostEstimate(
            flops=2 * count * width * 3 * HEAD_DIM,
            bytes_accessed=2 * count * width,
            transcendentals=0,
        ),
        name="heads_in",
    )(order, weight, *blocks)


def tail_kernel(*refs):
    *blocks, out = refs
    rows = blocks[0].shape[0]
    for index, block in enumerate(blocks):
        out[index * rows : (index + 1) * rows, :] = block[...]


def tail_specs(blocks, rows, tail):
    width = blocks[0].shape[1]
    return [pl.BlockSpec((tail, width), lambda i: (rows // tail, 0))] * len(blocks)


def tails(blocks, rows, tail):
    width = blocks[0].shape[1]
    return pl.pallas_call(
        tail_kernel,
        grid=(1,),
        in_specs=tail_specs(blocks, rows, tail),
        out_specs=pl.BlockSpec((len(blocks) * tail, width), lambda i: (0, 0)),
        out_shape=jax.ShapeDtypeStruct((len(blocks) * tail, width), jnp.bfloat16),
        name="tails",
    )(*blocks)


def four(refs, index):
    return jnp.concatenate([ref[...] for ref in refs[index : index + 4]], axis=0)


def far_four(far, cross, index):
    rows = far.shape[0] // 2
    ref, at = (far, index // 4) if index < 8 else (cross, index // 4 - 2)
    return ref[at * rows : (at + 1) * rows, :]


def out_kernel(where, attended, resid, gain, *refs):
    *near, far, cross, middle, normed = refs
    count = len(near)
    half = HEAD_DIM // 2
    first_group = where[count] == 0
    total = resid[...].astype(jnp.float32)
    for index in range(0, count, 4):
        near_left, far_left = [], []
        for i in range(index, index + 4):
            columns = attended[where[i]].astype(jnp.float32)
            low, high = columns[:, :half], columns[:, half:]
            near_left.append(jnp.where(first_group, low, high))
            far_left.append(jnp.where(first_group, high, low))
        total += mm(jnp.concatenate(near_left, axis=1).astype(jnp.bfloat16), four(near, index))
        total += mm(
            jnp.concatenate(far_left, axis=1).astype(jnp.bfloat16), far_four(far, cross, index)
        )
    middle[...] = total
    inverse = lax.rsqrt(jnp.mean(total * total, axis=-1, keepdims=True) + eps)
    normed[...] = (total * inverse * gain[...]).astype(normed.dtype)


def whole_specs(*arrays):
    return [pl.BlockSpec(array.shape, lambda i, rank=array.ndim: (0,) * rank) for array in arrays]


def out_project(where, attended, resid, gain, blocks, far, cross):
    rows, width = resid.shape
    tail = blocks[0].shape[0] - rows
    return pl.pallas_call(
        out_kernel,
        grid=(1,),
        in_specs=[scalars]
        + whole_specs(attended, resid, gain)
        + tail_specs(blocks, rows, tail)
        + whole_specs(far, cross),
        out_specs=whole_specs(resid, resid),
        out_shape=[
            jax.ShapeDtypeStruct((rows, width), jnp.float32),
            jax.ShapeDtypeStruct((rows, width), jnp.bfloat16),
        ],
        cost_estimate=pl.CostEstimate(
            flops=2 * rows * width * width,
            bytes_accessed=2 * width * width,
            transcendentals=0,
        ),
        name="out_project",
    )(where, attended, resid, gain, *blocks, far, cross)


def out_back_kernel(where, branch, *refs):
    *near_refs, far_ref, cross, out = refs
    count = len(near_refs)
    half = HEAD_DIM // 2
    first_group = where[count] == 0
    for index in range(0, count, 4):
        near = contract_cols(branch[...], four(near_refs, index))
        far = contract_cols(branch[...], far_four(far_ref, cross, index))
        for i in range(index, index + 4):
            here = slice((i - index) * half, (i - index + 1) * half)
            low = jnp.where(first_group, near[:, here], far[:, here])
            high = jnp.where(first_group, far[:, here], near[:, here])
            out[where[i]] = jnp.concatenate([low, high], axis=1).astype(out.dtype)


def out_project_back(where, branch, blocks, far, cross):
    rows, width = branch.shape
    tail = blocks[0].shape[0] - rows
    shape = (len(blocks), rows, HEAD_DIM)
    return pl.pallas_call(
        out_back_kernel,
        grid=(1,),
        in_specs=[scalars]
        + whole_specs(branch)
        + tail_specs(blocks, rows, tail)
        + whole_specs(far, cross),
        out_specs=pl.BlockSpec(shape, lambda i: (0, 0, 0)),
        out_shape=jax.ShapeDtypeStruct(shape, jnp.bfloat16),
        cost_estimate=pl.CostEstimate(
            flops=2 * rows * width * width,
            bytes_accessed=2 * width * width,
            transcendentals=0,
        ),
        name="out_project_back",
    )(where, branch, *blocks, far, cross)


def turn(values, cosine, rope_sine):
    half = HEAD_DIM // 2
    first, second = values[:half], values[half:]
    return jnp.concatenate(
        [first * cosine - second * rope_sine, second * cosine + first * rope_sine], axis=0
    )


def attend_kernel(
    query_raw,
    key_raw,
    value_t,
    inverse,
    inverse_all,
    gains,
    cosine,
    rope_sine,
    cosine_all,
    rope_sine_all,
    key_seg,
    query_seg,
    query_t,
    query,
    key_t,
    key,
    out,
    out_t,
    log_total,
):
    @pl.when(pl.program_id(0) == 0)
    def _():
        turned = turn(
            key_raw[...] * inverse_all[1:2, :] * gains[:, 1:2], cosine_all[...], rope_sine_all[...]
        ).astype(jnp.bfloat16)
        key_t[...] = turned
        key[...] = turned.T

    turned = turn(
        query_raw[...] * inverse[0:1, :] * gains[:, 0:1], cosine[...], rope_sine[...]
    ).astype(jnp.bfloat16)
    query_t[...] = turned
    query[...] = turned.T
    scores = mm(key[...], turned) * score_scale
    scores = jnp.where(key_seg[:, :1] == query_seg[...], scores, negative)
    peak = jnp.max(scores, axis=0, keepdims=True)
    weights = jnp.exp(scores - peak)
    total = jnp.sum(weights, axis=0, keepdims=True)
    result = mm(value_t[...], weights.astype(jnp.bfloat16)) / total
    out_t[...] = result.astype(out_t.dtype)
    out[...] = result.T.astype(out.dtype)
    log_total[...] = peak + jnp.log(total)


def attend(query_raw, key_raw, value_t, inverse, gains, cosine, rope_sine, key_seg, query_seg):
    count = query_raw.shape[1]
    whole = lambda i: (0, 0)
    across = lambda rows: pl.BlockSpec((rows, query_block), lambda i: (0, i))
    down = pl.BlockSpec((query_block, HEAD_DIM), lambda i: (i, 0))
    all_of = lambda rows: pl.BlockSpec((rows, count), whole)
    low, half = jnp.bfloat16, HEAD_DIM // 2
    return pl.pallas_call(
        attend_kernel,
        grid=(count // query_block,),
        in_specs=[
            across(HEAD_DIM),
            all_of(HEAD_DIM),
            all_of(HEAD_DIM),
            across(2),
            all_of(2),
            pl.BlockSpec((HEAD_DIM, 2), whole),
            across(half),
            across(half),
            all_of(half),
            all_of(half),
            pl.BlockSpec((count, HEAD_DIM), whole),
            across(1),
        ],
        out_specs=[
            across(HEAD_DIM),
            down,
            all_of(HEAD_DIM),
            pl.BlockSpec((count, HEAD_DIM), whole),
            down,
            across(HEAD_DIM),
            across(1),
        ],
        out_shape=[
            jax.ShapeDtypeStruct((HEAD_DIM, count), low),
            jax.ShapeDtypeStruct((count, HEAD_DIM), low),
            jax.ShapeDtypeStruct((HEAD_DIM, count), low),
            jax.ShapeDtypeStruct((count, HEAD_DIM), low),
            jax.ShapeDtypeStruct((count, HEAD_DIM), low),
            jax.ShapeDtypeStruct((HEAD_DIM, count), low),
            jax.ShapeDtypeStruct((1, count), jnp.float32),
        ],
        cost_estimate=pl.CostEstimate(
            flops=4 * count * count * HEAD_DIM,
            bytes_accessed=count * HEAD_DIM * 24,
            transcendentals=count * count,
        ),
        name="attend",
    )(
        query_raw,
        key_raw,
        value_t,
        inverse,
        inverse,
        gains,
        cosine,
        rope_sine,
        cosine,
        rope_sine,
        key_seg,
        query_seg,
    )


def attend_back_kernel(
    key_seg,
    query_seg,
    log_total,
    query_t,
    query,
    upstream,
    key,
    key_t,
    value,
    query_raw,
    key_raw,
    inverse,
    inverse_all,
    gains,
    cosine,
    rope_sine,
    cosine_all,
    rope_sine_all,
    weighted_query,
    weighted_key,
    dvalue_t,
    inner_query,
    inner_key,
    gain_sums,
    dkey,
    dvalue,
):
    step = pl.program_id(0)

    @pl.when(step == 0)
    def _():
        dkey[...] = jnp.zeros_like(dkey)
        dvalue[...] = jnp.zeros_like(dvalue)
        gain_sums[...] = jnp.zeros_like(gain_sums)

    scores = mm(key[...], query_t[...]) * score_scale
    probs = jnp.where(key_seg[:, :1] == query_seg[...], jnp.exp(scores - log_total[...]), 0.0)
    dvalue[...] += mm(probs.astype(jnp.bfloat16), upstream[...])
    dprobs = contract_cols(value[...], upstream[...])
    delta = jnp.sum(probs * dprobs, axis=0, keepdims=True)
    dscores = (probs * (dprobs - delta)).astype(jnp.bfloat16)
    dkey[...] += mm(dscores, query[...])
    turned = turn(mm(key_t[...], dscores) * score_scale, cosine[...], -rope_sine[...])
    product = turned * (query_raw[...] * inverse[0:1, :])
    weighted_query[...] = turned * gains[:, 0:1]
    inner_query[...] = jnp.sum(product * gains[:, 0:1], axis=0, keepdims=True)
    gain_sums[:, 0:1] += jnp.sum(product, axis=1, keepdims=True)

    @pl.when(step == pl.num_programs(0) - 1)
    def _():
        turned = turn(dkey[...].T * score_scale, cosine_all[...], -rope_sine_all[...])
        product = turned * (key_raw[...] * inverse_all[1:2, :])
        weighted_key[...] = turned * gains[:, 1:2]
        inner_key[...] = jnp.sum(product * gains[:, 1:2], axis=0, keepdims=True)
        gain_sums[:, 1:2] = jnp.sum(product, axis=1, keepdims=True)
        dvalue_t[...] = dvalue[...].T.astype(dvalue_t.dtype)


def attend_back(
    key_seg,
    query_seg,
    log_total,
    query_t,
    query,
    upstream,
    key,
    key_t,
    value,
    query_raw,
    key_raw,
    inverse,
    gains,
    cosine,
    rope_sine,
):
    count = query.shape[0]
    whole = lambda i: (0, 0)
    across = lambda rows: pl.BlockSpec((rows, query_block), lambda i: (0, i))
    down = pl.BlockSpec((query_block, HEAD_DIM), lambda i: (i, 0))
    all_of = lambda rows: pl.BlockSpec((rows, count), whole)
    tall = pl.BlockSpec((count, HEAD_DIM), whole)
    half = HEAD_DIM // 2
    return pl.pallas_call(
        attend_back_kernel,
        grid=(count // query_block,),
        in_specs=[
            tall,
            across(1),
            across(1),
            across(HEAD_DIM),
            down,
            down,
            tall,
            all_of(HEAD_DIM),
            tall,
            across(HEAD_DIM),
            all_of(HEAD_DIM),
            across(2),
            all_of(2),
            pl.BlockSpec((HEAD_DIM, 2), whole),
            across(half),
            across(half),
            all_of(half),
            all_of(half),
        ],
        out_specs=[
            across(HEAD_DIM),
            all_of(HEAD_DIM),
            all_of(HEAD_DIM),
            across(1),
            all_of(1),
            pl.BlockSpec((HEAD_DIM, 2), whole),
        ],
        out_shape=[
            jax.ShapeDtypeStruct((HEAD_DIM, count), jnp.float32),
            jax.ShapeDtypeStruct((HEAD_DIM, count), jnp.float32),
            jax.ShapeDtypeStruct((HEAD_DIM, count), jnp.bfloat16),
            jax.ShapeDtypeStruct((1, count), jnp.float32),
            jax.ShapeDtypeStruct((1, count), jnp.float32),
            jax.ShapeDtypeStruct((HEAD_DIM, 2), jnp.float32),
        ],
        scratch_shapes=[
            pltpu.VMEM((count, HEAD_DIM), jnp.float32),
            pltpu.VMEM((count, HEAD_DIM), jnp.float32),
        ],
        cost_estimate=pl.CostEstimate(
            flops=10 * count * count * HEAD_DIM,
            bytes_accessed=count * HEAD_DIM * 40,
            transcendentals=count * count,
        ),
        name="attend_back",
    )(
        key_seg,
        query_seg,
        log_total,
        query_t,
        query,
        upstream,
        key,
        key_t,
        value,
        query_raw,
        key_raw,
        inverse,
        inverse,
        gains,
        cosine,
        rope_sine,
        cosine,
        rope_sine,
    )


def local(
    tokens,
    segments,
    routes,
    route_gates,
    attn_gain,
    query_gain,
    key_gain,
    ffn_gain,
    w_query,
    w_key,
    w_value,
    w_out,
    w_gate,
    w_up,
    w_down,
    cotangent,
):
    row_count, width = tokens.shape
    top_count = routes.shape[1]
    devices = lax.axis_size("expert")
    groups = lax.axis_size("dp")
    me = lax.axis_index("expert")
    my_group = lax.axis_index("dp")
    seq_length = row_count * devices
    part = width // devices
    sharing = HEAD_DIM // part
    head = me // sharing
    sub = me % sharing
    w_rows = w_query.shape[0]
    w_half = w_rows // 2

    grouped = devices == 16 and groups == 2
    order = arrival_order(me) if grouped else jnp.arange(devices, dtype=jnp.int32)
    where = jnp.concatenate([order, my_group[None].astype(jnp.int32)])

    def gather(block):
        return Rounds(gather_rounds(block) if grouped else gather_whole(block))

    def scatter(make, tie=lambda addends: addends):
        return Rounds((scatter_rounds if grouped else scatter_whole)(make, seq_length, tie))

    def exchange(values):
        return lax.all_to_all(values, "expert", split_axis=0, concat_axis=0, tiled=True)

    def to_heads(rows):
        blocks = rows.reshape(rows.shape[0], HEADS, HEAD_DIM).transpose(1, 0, 2)
        return jnp.repeat(blocks, sharing, axis=0)

    def my_part(columns, axis):
        if sharing == 1:
            return columns
        return lax.dynamic_slice_in_dim(columns, sub * part, part, axis=axis)

    def by_half(values, axis):
        return jnp.where(my_group == 0, values, jnp.flip(values, axis))

    def dp_start(values):
        return swap(values, "dp", 1) if groups == 2 else lax.psum(values, "dp")

    def dp_end(values, arrived):
        total = arrived.astype(jnp.float32)
        return total + values.astype(jnp.float32) if groups == 2 else total

    waiting = []

    def weight_grad(left, right):
        pieces = left.shape[1] // 256 if grouped else 1
        step = left.shape[1] // pieces
        own = [
            contract_rows(left[:, i * step : (i + 1) * step], right).astype(jnp.bfloat16)
            for i in range(pieces)
        ]
        far = [dp_start(values) for values in own]
        waiting.extend((far, i) for i in range(pieces))
        return own, far

    def cross(*others):
        if not (waiting and grouped):
            return others
        far, i = waiting.pop(0)
        *others, far[i] = together(*others, far[i])
        return others

    def ride(rounds, *others):
        if not (waiting and grouped):
            return rounds.step(*others)
        far, i = waiting.pop(0)
        *others, far[i] = rounds.step(*others, far[i])
        return others

    resid_in = tokens.astype(jnp.float32)
    pre_in, normal_in, inverse_in = norm_rows(resid_in, attn_gain)
    normed_in = pre_in.astype(jnp.bfloat16)

    experts_all = devices * w_gate.shape[0]
    slots = min(row_count, row_count * top_count * 3 // (2 * experts_all))
    hits = routes[:, :, None] == jnp.arange(experts_all, dtype=jnp.int32)[None, None, :]
    gate_table = jnp.sum(jnp.where(hits, route_gates[:, :, None], 0.0), axis=1).T
    gate_high = lax.reduce_precision(gate_table, exponent_bits=8, mantissa_bits=7)
    gate_rows = jnp.pad(
        jnp.stack([gate_high, gate_table - gate_high], axis=1).astype(jnp.bfloat16),
        ((0, 0), (0, 14), (0, 3 * HEAD_DIM - row_count)),
    )
    if grouped:
        take = lambda w: lax.dynamic_slice_in_dim(w, my_group * w_half, w_half)
    else:
        take = lambda w: w
    sent_w = jnp.concatenate([to_heads(take(w)) for w in (w_query, w_key, w_value)], axis=2)
    taken = sent_w.shape[1]
    arrived = exchange(jnp.concatenate([sent_w, gate_rows], axis=1))

    key_seg = jnp.broadcast_to(segments[:, None], (seq_length, HEAD_DIM))
    query_seg = segments[None, :]
    cosine, rope_sine = rope_tables(jnp.arange(seq_length, dtype=jnp.int32))
    gains = jnp.stack(
        [
            lax.dynamic_slice_in_dim(query_gain, head * HEAD_DIM, HEAD_DIM),
            lax.dynamic_slice_in_dim(key_gain, head * HEAD_DIM, HEAD_DIM),
        ],
        axis=1,
    )
    if grouped:
        rounds = gather(jnp.concatenate([normed_in, take(w_out)], axis=0))
        rounds.step()
        (arrived,) = rounds.step(arrived)
        head_w = arrived[:, :taken]
        head_w_far = swap(head_w, "dp", 1)
        rounds.step(key_seg, cosine, rope_sine, gains)
        (head_w_far,) = rounds.step(head_w_far)
        blocks = rounds.finish()
        head_w = by_half(jnp.stack([head_w, head_w_far], axis=1), 1).reshape(width, 3 * HEAD_DIM)
        out_far = swap(tails(blocks[: devices // 2], row_count, w_half), "dp", 1)
    else:
        blocks = gather(normed_in).finish()
        head_w = arrived[:, :taken].reshape(width, 3 * HEAD_DIM)
        out_full = lax.all_gather(w_out, "expert", axis=0, tiled=True)

    gate_pair = arrived[:, taken : taken + 2, :row_count].astype(jnp.float32)
    gate_mine = (gate_pair[:, 0] + gate_pair[:, 1])[order]
    chosen = gate_mine > 0.0
    before = jnp.arange(row_count)[:, None] < jnp.arange(row_count)[None, :]
    rank = mm(chosen.astype(jnp.bfloat16), before.astype(jnp.bfloat16)).astype(jnp.int32)
    rank = jnp.where(chosen, rank, -1)
    slot = jnp.arange(slots, dtype=jnp.int32)
    picks = rank[:, None, :] == slot[None, :, None]
    slot_gate = jnp.sum(jnp.where(picks, gate_mine[:, None, :], 0.0), axis=2).reshape(-1, 1)
    picks = picks.astype(jnp.bfloat16)
    unpicks = (rank[:, :, None] == slot[None, None, :]).astype(jnp.bfloat16)
    ones = jnp.ones_like(slot_gate)
    ff = w_gate.shape[2]
    w_both = jnp.concatenate([w_gate[0], w_up[0]], axis=1)

    cot_rounds = gather(cotangent)
    query_raw, key_raw, value, value_t, squares = heads_in(order, head_w, row_count, blocks)
    if sharing > 1:
        squares = jnp.stack(
            [jnp.sum(jnp.square(my_part(raw, 0)), axis=0) for raw in (query_raw, key_raw)]
        )
    (squares,) = cot_rounds.step(squares)
    squares = butterfly(squares, "expert")
    (squares,) = cot_rounds.step(squares)
    inverse = lax.rsqrt(squares / width + eps)
    query_t, query, key_t, key, attended, attended_t, log_total = attend(
        query_raw, key_raw, value_t, inverse, gains, cosine, rope_sine, key_seg, query_seg
    )
    if grouped:
        attended, out_far = cot_rounds.step(attended, out_far)
        out_cross = send(out_far, swap_core)

    attended_low = exchange(my_part(attended, 1).reshape(devices, row_count, part))
    (attended_low,) = cot_rounds.step(attended_low)
    if grouped:
        middle, normed_mid = out_project(
            where, attended_low, tokens, ffn_gain[None, :], blocks, out_far, out_cross
        )
    else:
        attended_low = attended_low.transpose(1, 0, 2).reshape(row_count, width)
        middle = resid_in + mm(attended_low, out_full)
        normed_mid = norm_rows(middle, ffn_gain)[0].astype(jnp.bfloat16)
    (normed_mid,) = cot_rounds.step(normed_mid)
    cot_blocks = cot_rounds.finish()

    mid_rounds = gather(normed_mid)
    grad_eo = pick(picks, slot_gate, cot_blocks)
    head_w_t = jnp.concatenate(
        [my_part(head_w[:, i * HEAD_DIM : (i + 1) * HEAD_DIM], 1).T for i in range(3)], axis=0
    )
    grad_eo, head_w_t = mid_rounds.step(grad_eo, head_w_t)
    rows_in = pick(picks, ones, mid_rounds.finish())
    gate_up = mm(rows_in, w_both)
    gate_in, up_in = gate_up[:, :ff], gate_up[:, ff:]
    sigmoid_in = jax.nn.sigmoid(gate_in)
    silu_in = gate_in * sigmoid_in
    hidden = (silu_in * up_in).astype(jnp.bfloat16)
    grad_down, down_far = weight_grad(hidden, grad_eo)

    def give_back(produce):
        def some(first, count):
            here = slice(first // row_count, (first + count) // row_count)
            rows = produce(slice(here.start * slots, here.stop * slots))
            return jnp.einsum(
                "bts,bsd->btd",
                unpicks[here],
                rows.astype(jnp.bfloat16).reshape(-1, slots, width),
                preferred_element_type=jnp.bfloat16,
            ).reshape(count, width)

        return some

    hidden_next, grad_eo_next = together(hidden, grad_eo, *grad_down)[:2]
    mix_rounds = scatter(
        give_back(lambda some: mm(hidden_next[some], w_down[0]) * slot_gate[some])
    )
    grad_hidden = contract_cols(grad_eo_next, w_down[0])
    grad_pre = jnp.concatenate(
        [
            (
                grad_hidden * up_in * sigmoid_in * (1.0 + gate_in * (1.0 - sigmoid_in))
            ).astype(jnp.bfloat16),
            (grad_hidden * silu_in).astype(jnp.bfloat16),
        ],
        axis=1,
    )
    (grad_pre,) = ride(mix_rounds, grad_pre)
    row_rounds = scatter(
        give_back(lambda some: contract_cols(grad_pre[some], w_both)),
        lambda addends: ride(mix_rounds, addends)[0],
    )
    grad_both, both_far = weight_grad(rows_in, grad_pre)
    far, i = waiting.pop(0) if grouped else (None, 0)
    if grouped:
        (far[i], *_) = step_all([row_rounds, mix_rounds], far[i], *grad_both[:1])
    else:
        row_rounds.step()
    ride(row_rounds, *mix_rounds.sent, *grad_both[1:2])
    row_rounds.step(*grad_both[2:4])
    ride(row_rounds, *grad_both[4:5])
    ride(row_rounds, *grad_both[5:6])
    grad_normed_mid = row_rounds.finish()

    grad_out = cotangent.astype(jnp.float32)
    _, normal_mid, inverse_mid = norm_rows(middle, ffn_gain)
    mid_back, grad_ffn_gain = norm_back(grad_normed_mid, normal_mid, inverse_mid, ffn_gain)
    grad_middle = grad_out + mid_back
    grad_branch = grad_middle.astype(jnp.bfloat16)
    if grouped:
        grad_columns = out_project_back(where, grad_branch, blocks, out_far, out_cross)
        (grad_columns,) = ride(mix_rounds, grad_columns)
    else:
        grad_columns = to_heads(contract_cols(grad_branch, out_full).astype(jnp.bfloat16))
    grad_attended = exchange(grad_columns).reshape(seq_length, HEAD_DIM)
    if groups == 2:
        (down_total,) = merge(grad_down, down_far, 1)
        grad_attended, down_total, *_ = cross(grad_attended, down_total, *grad_both[6:])
    else:
        down_total = down_far[0].astype(jnp.float32)
    mixed = mix_rounds.finish()
    activations = (middle + mixed).astype(jnp.bfloat16)
    branch_all = lax.all_gather(
        after(grad_branch, grad_attended), "expert", axis=0, tiled=True
    )

    weighted_query, weighted_key, grad_value_t, inner_query, inner_key, gain_sums = attend_back(
        key_seg,
        query_seg,
        log_total,
        query_t,
        query,
        grad_attended,
        key,
        key_t,
        value,
        query_raw,
        key_raw,
        inverse,
        gains,
        cosine,
        rope_sine,
    )
    inner = jnp.concatenate([inner_query, inner_key], axis=0)
    if sharing > 1:
        inner = jnp.stack(
            [
                jnp.sum(my_part(weighted * raw * at, 0), axis=0)
                for weighted, raw, at in (
                    (weighted_query, query_raw, inverse[0:1]),
                    (weighted_key, key_raw, inverse[1:2]),
                )
            ]
        )
    (inner,) = cross(inner)
    inner = butterfly(inner, "expert") / width
    (inner,) = cross(inner)
    grad_raw_t = jnp.concatenate(
        [
            my_part(
                (at * (weighted - raw * at * mean)).astype(jnp.bfloat16),
                0,
            )
            for weighted, raw, at, mean in (
                (weighted_query, query_raw, inverse[0:1], inner[0:1]),
                (weighted_key, key_raw, inverse[1:2], inner[1:2]),
            )
        ]
        + [my_part(grad_value_t, 0)],
        axis=0,
    )
    in_rounds = scatter(
        lambda first, count: project(order, grad_raw_t, head_w_t, row_count, first, count)
    )
    grad_w_t = stack_product(order, grad_raw_t, row_count, blocks)
    grad_attn_gain = jnp.sum(grad_w_t * head_w_t.astype(jnp.float32), axis=0) / attn_gain
    w_columns = exchange(
        grad_w_t.astype(jnp.bfloat16).reshape(3 * part, devices, w_rows).transpose(1, 0, 2)
    )
    ride(in_rounds)

    def placed(values):
        return lax.dynamic_update_slice_in_dim(
            jnp.zeros((width,), jnp.float32), values, me * part, 0
        )

    gain_parts = jnp.stack(
        [
            grad_attn_gain,
            placed(my_part(gain_sums[:, 0], 0)),
            placed(my_part(gain_sums[:, 1], 0)),
            grad_ffn_gain,
        ]
    )
    out_part = mm(my_part(attended_t, 0), branch_all).astype(jnp.bfloat16)
    gain_parts, out_part = ride(in_rounds, gain_parts, out_part)
    out_part_far = dp_start(out_part)
    if groups == 2:
        both_total = merge(grad_both[:4], both_far[:4], 2, len(grad_both))
        w_columns, *both_total = in_rounds.step(w_columns, *both_total)
    else:
        in_rounds.step()
    dense = [
        w_columns[:, i * part : (i + 1) * part].reshape(width, w_rows).T for i in range(3)
    ]
    dense = in_rounds.step(*dense)
    dense_far = [dp_start(values) for values in dense]
    if groups == 2:
        both_total = merge(grad_both[4:], both_far[4:], 2, 4, both_total)
        gate_total, up_total = in_rounds.step(*both_total)
    else:
        in_rounds.step()
        both_total = both_far[0].astype(jnp.float32)
        gate_total, up_total = both_total[:, :ff], both_total[:, ff:]
    grad_normed_in = in_rounds.finish()
    grad_normed_in, gain_parts = together(grad_normed_in, gain_parts)
    gain_total = butterfly(butterfly(gain_parts, "expert"), "dp")
    in_back, _ = norm_back(grad_normed_in, normal_in, inverse_in, attn_gain)
    input_grad = (grad_middle + in_back).astype(jnp.bfloat16)

    return (
        activations,
        input_grad,
        gain_total[0],
        gain_total[1],
        gain_total[2],
        gain_total[3],
        dp_end(dense[0], dense_far[0]),
        dp_end(dense[1], dense_far[1]),
        dp_end(dense[2], dense_far[2]),
        dp_end(out_part, out_part_far),
        gate_total[None],
        up_total[None],
        down_total[None],
    )


def solution(mesh):
    in_specs = (
        P(("dp", "expert"), None),
        P("dp"),
        P(("dp", "expert"), None),
        P(("dp", "expert"), None),
        P(),
        P(),
        P(),
        P(),
        P("expert", None),
        P("expert", None),
        P("expert", None),
        P("expert", None),
        P("expert", None, None),
        P("expert", None, None),
        P("expert", None, None),
        P(("dp", "expert"), None),
    )
    out_specs = (
        P(("dp", "expert"), None),
        P(("dp", "expert"), None),
        P(),
        P(),
        P(),
        P(),
        P("expert", None),
        P("expert", None),
        P("expert", None),
        P("expert", None),
        P("expert", None, None),
        P("expert", None, None),
        P("expert", None, None),
    )
    return jax.shard_map(local, mesh=mesh, in_specs=in_specs, out_specs=out_specs, check_vma=False)
```

```python
import functools

import jax
import jax.numpy as jnp
from jax import lax
from jax.experimental import pallas as pl
from jax.experimental.pallas import tpu as pltpu
from jax.sharding import PartitionSpec as P

HEADS = 16
HEAD_DIM = 128


eps = 1e-05
rope_base = 50000.0
negative = -1e30
score_scale = HEAD_DIM ** (-0.5)
query_block = 256


def norm_rows(values, norm_gain):
    inverse = lax.rsqrt(jnp.mean(values * values, axis=-1, keepdims=True) + eps)
    normal = values * inverse
    return (normal * norm_gain, normal, inverse)


def norm_back(upstream, normal, inverse, norm_gain):
    weighted = upstream * norm_gain
    inner_mean = jnp.mean(weighted * normal, axis=-1, keepdims=True)
    return (inverse * (weighted - normal * inner_mean), jnp.sum(upstream * normal, axis=0))


def rope_tables(positions):
    half_dim = HEAD_DIM // 2
    frequency = rope_base ** (-(jnp.arange(half_dim, dtype=jnp.float32) * 2.0 / HEAD_DIM))
    theta = frequency[:, None] * positions.astype(jnp.float32)[None, :]
    return (jnp.cos(theta), jnp.sin(theta))


def mm(left, right):
    return jnp.dot(left, right, preferred_element_type=jnp.float32)


def contract_rows(left, right):
    return lax.dot_general(
        left, right, (((0,), (0,)), ((), ())), preferred_element_type=jnp.float32
    )


def contract_cols(left, right):
    return lax.dot_general(
        left, right, (((1,), (1,)), ((), ())), preferred_element_type=jnp.float32
    )


def swap(values, axis, step):
    count = lax.axis_size(axis)
    return lax.ppermute(values, axis, [(i, i ^ step) for i in range(count)])


def together(*values):
    return lax.optimization_barrier(values)


def after(values, *others):
    return lax.optimization_barrier((values,) + others)[0]


def butterfly(values, axis):
    step = 1
    while step < lax.axis_size(axis):
        values = values + swap(values, axis, step)
        step *= 2
    return values


near_order = ((0, 1, 2, 3), (1, 0, 2, 3), (2, 3, 1, 0), (3, 2, 1, 0))


def moves(target):
    pairs = []
    for index in range(16):
        far = target(index // 4)
        if far is not None:
            pairs.append((index, far * 4 + index % 4))
    return pairs


swap_near = moves(lambda z: z ^ 1)
swap_middle = moves(lambda z: {1: 2, 2: 1}.get(z))
move_out = moves(lambda z: {1: 0, 2: 3}.get(z))
move_in = moves(lambda z: {0: 1, 3: 2}.get(z))
swap_row = [(i, i ^ 2) for i in range(16)]
swap_core = [(i, i ^ 1) for i in range(16)]


def send(values, pairs):
    return lax.ppermute(values, "expert", pairs)


def arrival_order(me):
    near = jnp.asarray(near_order, jnp.int32)[me // 4] * 4
    row, core = (me // 2) % 2, me % 2
    return jnp.concatenate(
        [near + (row ^ j) * 2 + (core ^ i) for i in (0, 1) for j in (0, 1)]
    ).astype(jnp.int32)


class Rounds:
    def __init__(self, steps):
        self.steps = steps
        self.result = None
        self.over = False
        self.sent = ()
        self._go(None)

    def _go(self, arrived):
        try:
            self.sent = self.steps.send(arrived)
        except StopIteration as stop:
            self.result, self.sent, self.over = stop.value, (), True

    def step(self, *others):
        return step_all([self], *others)

    def finish(self):
        while not self.over:
            self.step()
        return self.result


def step_all(rounds, *others):
    sent = [values for one in rounds for values in one.sent]
    values = together(*sent, *others) if sent or others else ()
    at = 0
    for one in rounds:
        count = len(one.sent)
        if not one.over:
            one._go(values[at : at + count])
        at += count
    return values[at:]


def gather_rounds(block):
    at = lax.axis_index("expert") // 4
    outer = (at == 0) | (at == 3)
    first, second, row = yield (
        send(block, swap_near),
        send(block, swap_middle),
        send(block, swap_row),
    )
    third, second_out, row_first, core = yield (
        send(first, swap_middle),
        send(second, move_out),
        send(first, swap_row),
        send(block, swap_core),
    )
    second = jnp.where(outer, second_out, second)
    third_out, row_second, core_first, core_row = yield (
        send(third, move_out),
        send(second, swap_row),
        send(first, swap_core),
        send(row, swap_core),
    )
    third = jnp.where(outer, third_out, third)
    row_third, core_second, core_third, core_row_first, core_row_second = yield (
        send(third, swap_row),
        send(second, swap_core),
        send(third, swap_core),
        send(row_first, swap_core),
        send(row_second, swap_core),
    )
    (core_row_third,) = yield (send(row_third, swap_core),)
    return [
        block,
        first,
        second,
        third,
        row,
        row_first,
        row_second,
        row_third,
        core,
        core_first,
        core_second,
        core_third,
        core_row,
        core_row_first,
        core_row_second,
        core_row_third,
    ]


def gather_whole(block):
    yield ()
    return list(lax.all_gather(block, "expert", axis=0))


def add_low(left, right):
    return (left.astype(jnp.float32) + right.astype(jnp.float32)).astype(jnp.bfloat16)


def scatter_rounds(make, count, tie):
    (far,) = yield (send(tie(make(count // 2, count // 2)), swap_core),)
    close = make(0, count // 2)
    rows = count // 16

    def both(j, k):
        here = slice((j * 4 + k) * rows, (j * 4 + k + 1) * rows)
        return add_low(close[here], far[here])

    (row,) = yield (send(both(1, 3), swap_row),)
    third = add_low(both(0, 3), row)
    row, third_in = yield (send(both(1, 2), swap_row), send(third, move_in))
    second = add_low(both(0, 2), row)
    third = add_low(third, third_in)
    row, second_in, third_in = yield (
        send(both(1, 1), swap_row),
        send(second, move_in),
        send(third, swap_middle),
    )
    first = add_low(add_low(both(0, 1), row), third_in)
    second = add_low(second, second_in)
    row, second_in, first_in = yield (
        send(both(1, 0), swap_row),
        send(second, swap_middle),
        send(first, swap_near),
    )
    return (
        both(0, 0).astype(jnp.float32)
        + row.astype(jnp.float32)
        + second_in.astype(jnp.float32)
        + first_in.astype(jnp.float32)
    )


def scatter_whole(make, count, tie):
    yield ()
    return lax.psum_scatter(
        tie(make(0, count)), "expert", scatter_dimension=0, tiled=True
    ).astype(jnp.float32)


def pick_kernel(picks, scale, *refs):
    *blocks, out = refs
    slots = picks.shape[1]
    for index, block in enumerate(blocks):
        here = slice(index * slots, (index + 1) * slots)
        out[here, :] = (mm(picks[index], block[...]) * scale[here, :]).astype(out.dtype)


def pick(picks, scale, blocks):
    count, slots, tokens = picks.shape
    width = blocks[0].shape[1]
    return pl.pallas_call(
        pick_kernel,
        out_shape=jax.ShapeDtypeStruct((count * slots, width), jnp.bfloat16),
        cost_estimate=pl.CostEstimate(
            flops=2 * count * tokens * slots * width,
            bytes_accessed=2 * count * (tokens + slots) * width,
            transcendentals=0,
        ),
        name="pick",
    )(picks, scale, *blocks)


def merge_kernel(count, parts, *refs):
    pairs, outs = refs[: 2 * count], refs[-parts:]
    width = outs[0].shape[1]
    for index in range(count):

        @pl.when(pl.program_id(0) == index)
        def _():
            total = pairs[index][...].astype(jnp.float32) + pairs[count + index][...].astype(
                jnp.float32
            )
            for i, out in enumerate(outs):
                out[...] = total[:, i * width : (i + 1) * width]


def merge(own, far, parts, pieces=None, before=None):
    count = len(own)
    begin = pieces if before else 0
    before = before or []
    pieces = begin + count if before else pieces or count
    rows, width = own[0].shape
    return pl.pallas_call(
        functools.partial(merge_kernel, count, parts),
        grid=(count,),
        in_specs=[pl.BlockSpec((rows, width), lambda i: (0, 0))] * (2 * count)
        + [pl.BlockSpec(memory_space=pl.ANY)] * len(before),
        out_specs=[pl.BlockSpec((rows, width // parts), lambda i: (begin + i, 0))] * parts,
        out_shape=[jax.ShapeDtypeStruct((pieces * rows, width // parts), jnp.float32)] * parts,
        input_output_aliases={2 * count + i: i for i in range(len(before))},
        cost_estimate=pl.CostEstimate(
            flops=count * rows * width,
            bytes_accessed=8 * count * rows * width,
            transcendentals=0,
        ),
        compiler_params=pltpu.CompilerParams(vmem_limit_bytes=28 * 2**20),
        name="merge",
    )(*own, *far, *before)


def project_kernel(order, left_t, left_next_t, right, out):
    left = jnp.concatenate([left_t[...].T, left_next_t[...].T], axis=0)
    out[...] = mm(left, right[...]).astype(out.dtype)


def project(order, left_t, right, rows, first, count):
    depth, width = right.shape
    begin = first // rows
    return pl.pallas_call(
        project_kernel,
        grid_spec=pltpu.PrefetchScalarGridSpec(
            num_scalar_prefetch=1,
            grid=(count // (2 * rows),),
            in_specs=[
                pl.BlockSpec((depth, rows), lambda i, order: (0, order[begin + 2 * i])),
                pl.BlockSpec((depth, rows), lambda i, order: (0, order[begin + 2 * i + 1])),
                pl.BlockSpec((depth, width), lambda i, order: (0, 0)),
            ],
            out_specs=pl.BlockSpec((2 * rows, width), lambda i, order: (i, 0)),
        ),
        out_shape=jax.ShapeDtypeStruct((count, width), jnp.bfloat16),
        cost_estimate=pl.CostEstimate(
            flops=2 * count * depth * width,
            bytes_accessed=2 * (count * (depth + width) + depth * width),
            transcendentals=0,
        ),
        compiler_params=pltpu.CompilerParams(vmem_limit_bytes=28 * 2**20),
        name="project",
    )(order, left_t, left_t, right)


scalars = pl.BlockSpec(memory_space=pltpu.SMEM)
vectors = pl.BlockSpec(memory_space=pltpu.VMEM)


def lanes(order, index, rows):
    return pl.ds(pl.multiple_of(order[index] * rows, rows), rows)


def stack_kernel(rows, order, left_t, *refs):
    *blocks, out = refs
    for index in range(0, len(blocks), 4):
        four = range(index, index + 4)
        left = jnp.concatenate([left_t[:, lanes(order, i, rows)] for i in four], axis=1)
        right = jnp.concatenate([blocks[i][:rows] for i in four], axis=0)
        term = mm(left, right)
        if index == 0:
            out[...] = term
        else:
            out[...] += term


def stack_product(order, left_t, rows, blocks):
    width = blocks[0].shape[1]
    return pl.pallas_call(
        functools.partial(stack_kernel, rows),
        in_specs=[scalars, vectors] + [vectors] * len(blocks),
        out_specs=vectors,
        out_shape=jax.ShapeDtypeStruct((left_t.shape[0], width), jnp.float32),
        cost_estimate=pl.CostEstimate(
            flops=2 * left_t.size * width,
            bytes_accessed=2 * len(blocks) * rows * width,
            transcendentals=0,
        ),
        compiler_params=pltpu.CompilerParams(vmem_limit_bytes=28 * 2**20),
        name="stack_product",
    )(order, left_t, *blocks)


def heads_kernel(rows, order, weight, *refs):
    *blocks, query_t, key_t, value, value_t, squares = refs
    for index in range(0, len(blocks), 4):
        four = range(index, index + 4)
        raw = mm(jnp.concatenate([blocks[i][:rows] for i in four], axis=0), weight[...])
        for i in four:
            own = raw[(i - index) * rows : (i - index + 1) * rows]
            here = lanes(order, i, rows)
            query = own[:, :HEAD_DIM].T
            key = own[:, HEAD_DIM : 2 * HEAD_DIM].T
            query_t[:, here] = query
            key_t[:, here] = key
            value[here, :] = own[:, 2 * HEAD_DIM :].astype(value.dtype)
            value_t[:, here] = own[:, 2 * HEAD_DIM :].T.astype(value.dtype)
            squares[0:1, here] = jnp.sum(query * query, axis=0, keepdims=True)
            squares[1:2, here] = jnp.sum(key * key, axis=0, keepdims=True)


def heads_in(order, weight, rows, blocks):
    width = blocks[0].shape[1]
    count = len(blocks) * rows
    return pl.pallas_call(
        functools.partial(heads_kernel, rows),
        in_specs=[scalars, vectors] + [vectors] * len(blocks),
        out_specs=[vectors] * 5,
        out_shape=[
            jax.ShapeDtypeStruct((HEAD_DIM, count), jnp.float32),
            jax.ShapeDtypeStruct((HEAD_DIM, count), jnp.float32),
            jax.ShapeDtypeStruct((count, HEAD_DIM), jnp.bfloat16),
            jax.ShapeDtypeStruct((HEAD_DIM, count), jnp.bfloat16),
            jax.ShapeDtypeStruct((2, count), jnp.float32),
        ],
        cost_estimate=pl.CostEstimate(
            flops=2 * count * width * 3 * HEAD_DIM,
            bytes_accessed=2 * count * width,
            transcendentals=0,
        ),
        name="heads_in",
    )(order, weight, *blocks)


def tail_kernel(*refs):
    *blocks, out = refs
    rows = blocks[0].shape[0]
    for index, block in enumerate(blocks):
        out[index * rows : (index + 1) * rows, :] = block[...]


def tail_specs(blocks, rows, tail):
    width = blocks[0].shape[1]
    return [pl.BlockSpec((tail, width), lambda i: (rows // tail, 0))] * len(blocks)


def tails(blocks, rows, tail):
    width = blocks[0].shape[1]
    return pl.pallas_call(
        tail_kernel,
        grid=(1,),
        in_specs=tail_specs(blocks, rows, tail),
        out_specs=pl.BlockSpec((len(blocks) * tail, width), lambda i: (0, 0)),
        out_shape=jax.ShapeDtypeStruct((len(blocks) * tail, width), jnp.bfloat16),
        name="tails",
    )(*blocks)


def four(refs, index):
    return jnp.concatenate([ref[...] for ref in refs[index : index + 4]], axis=0)


def far_four(far, cross, index):
    rows = far.shape[0] // 2
    ref, at = (far, index // 4) if index < 8 else (cross, index // 4 - 2)
    return ref[at * rows : (at + 1) * rows, :]


def out_kernel(where, attended, resid, gain, *refs):
    *near, far, cross, middle, normed = refs
    count = len(near)
    half = HEAD_DIM // 2
    first_group = where[count] == 0
    total = resid[...].astype(jnp.float32)
    for index in range(0, count, 4):
        near_left, far_left = [], []
        for i in range(index, index + 4):
            columns = attended[where[i]].astype(jnp.float32)
            low, high = columns[:, :half], columns[:, half:]
            near_left.append(jnp.where(first_group, low, high))
            far_left.append(jnp.where(first_group, high, low))
        total += mm(jnp.concatenate(near_left, axis=1).astype(jnp.bfloat16), four(near, index))
        total += mm(
            jnp.concatenate(far_left, axis=1).astype(jnp.bfloat16), far_four(far, cross, index)
        )
    middle[...] = total
    inverse = lax.rsqrt(jnp.mean(total * total, axis=-1, keepdims=True) + eps)
    normed[...] = (total * inverse * gain[...]).astype(normed.dtype)


def whole_specs(*arrays):
    return [pl.BlockSpec(array.shape, lambda i, rank=array.ndim: (0,) * rank) for array in arrays]


def out_project(where, attended, resid, gain, blocks, far, cross):
    rows, width = resid.shape
    tail = blocks[0].shape[0] - rows
    return pl.pallas_call(
        out_kernel,
        grid=(1,),
        in_specs=[scalars]
        + whole_specs(attended, resid, gain)
        + tail_specs(blocks, rows, tail)
        + whole_specs(far, cross),
        out_specs=whole_specs(resid, resid),
        out_shape=[
            jax.ShapeDtypeStruct((rows, width), jnp.float32),
            jax.ShapeDtypeStruct((rows, width), jnp.bfloat16),
        ],
        cost_estimate=pl.CostEstimate(
            flops=2 * rows * width * width,
            bytes_accessed=2 * width * width,
            transcendentals=0,
        ),
        name="out_project",
    )(where, attended, resid, gain, *blocks, far, cross)


def out_back_kernel(where, branch, *refs):
    *near_refs, far_ref, cross, out = refs
    count = len(near_refs)
    half = HEAD_DIM // 2
    first_group = where[count] == 0
    for index in range(0, count, 4):
        near = contract_cols(branch[...], four(near_refs, index))
        far = contract_cols(branch[...], far_four(far_ref, cross, index))
        for i in range(index, index + 4):
            here = slice((i - index) * half, (i - index + 1) * half)
            low = jnp.where(first_group, near[:, here], far[:, here])
            high = jnp.where(first_group, far[:, here], near[:, here])
            out[where[i]] = jnp.concatenate([low, high], axis=1).astype(out.dtype)


def out_project_back(where, branch, blocks, far, cross):
    rows, width = branch.shape
    tail = blocks[0].shape[0] - rows
    shape = (len(blocks), rows, HEAD_DIM)
    return pl.pallas_call(
        out_back_kernel,
        grid=(1,),
        in_specs=[scalars]
        + whole_specs(branch)
        + tail_specs(blocks, rows, tail)
        + whole_specs(far, cross),
        out_specs=pl.BlockSpec(shape, lambda i: (0, 0, 0)),
        out_shape=jax.ShapeDtypeStruct(shape, jnp.bfloat16),
        cost_estimate=pl.CostEstimate(
            flops=2 * rows * width * width,
            bytes_accessed=2 * width * width,
            transcendentals=0,
        ),
        name="out_project_back",
    )(where, branch, *blocks, far, cross)


def turn(values, cosine, rope_sine):
    half = HEAD_DIM // 2
    first, second = values[:half], values[half:]
    return jnp.concatenate(
        [first * cosine - second * rope_sine, second * cosine + first * rope_sine], axis=0
    )


def attend_kernel(
    query_raw,
    key_raw,
    value_t,
    inverse,
    inverse_all,
    gains,
    cosine,
    rope_sine,
    cosine_all,
    rope_sine_all,
    key_seg,
    query_seg,
    query_t,
    query,
    key_t,
    key,
    out,
    out_t,
    log_total,
):
    @pl.when(pl.program_id(0) == 0)
    def _():
        turned = turn(
            key_raw[...] * inverse_all[1:2, :] * gains[:, 1:2], cosine_all[...], rope_sine_all[...]
        ).astype(jnp.bfloat16)
        key_t[...] = turned
        key[...] = turned.T

    turned = turn(
        query_raw[...] * inverse[0:1, :] * gains[:, 0:1], cosine[...], rope_sine[...]
    ).astype(jnp.bfloat16)
    query_t[...] = turned
    query[...] = turned.T
    scores = mm(key[...], turned) * score_scale
    scores = jnp.where(key_seg[:, :1] == query_seg[...], scores, negative)
    peak = jnp.max(scores, axis=0, keepdims=True)
    weights = jnp.exp(scores - peak)
    total = jnp.sum(weights, axis=0, keepdims=True)
    result = mm(value_t[...], weights.astype(jnp.bfloat16)) / total
    out_t[...] = result.astype(out_t.dtype)
    out[...] = result.T.astype(out.dtype)
    log_total[...] = peak + jnp.log(total)


def attend(query_raw, key_raw, value_t, inverse, gains, cosine, rope_sine, key_seg, query_seg):
    count = query_raw.shape[1]
    whole = lambda i: (0, 0)
    across = lambda rows: pl.BlockSpec((rows, query_block), lambda i: (0, i))
    down = pl.BlockSpec((query_block, HEAD_DIM), lambda i: (i, 0))
    all_of = lambda rows: pl.BlockSpec((rows, count), whole)
    low, half = jnp.bfloat16, HEAD_DIM // 2
    return pl.pallas_call(
        attend_kernel,
        grid=(count // query_block,),
        in_specs=[
            across(HEAD_DIM),
            all_of(HEAD_DIM),
            all_of(HEAD_DIM),
            across(2),
            all_of(2),
            pl.BlockSpec((HEAD_DIM, 2), whole),
            across(half),
            across(half),
            all_of(half),
            all_of(half),
            pl.BlockSpec((count, HEAD_DIM), whole),
            across(1),
        ],
        out_specs=[
            across(HEAD_DIM),
            down,
            all_of(HEAD_DIM),
            pl.BlockSpec((count, HEAD_DIM), whole),
            down,
            across(HEAD_DIM),
            across(1),
        ],
        out_shape=[
            jax.ShapeDtypeStruct((HEAD_DIM, count), low),
            jax.ShapeDtypeStruct((count, HEAD_DIM), low),
            jax.ShapeDtypeStruct((HEAD_DIM, count), low),
            jax.ShapeDtypeStruct((count, HEAD_DIM), low),
            jax.ShapeDtypeStruct((count, HEAD_DIM), low),
            jax.ShapeDtypeStruct((HEAD_DIM, count), low),
            jax.ShapeDtypeStruct((1, count), jnp.float32),
        ],
        cost_estimate=pl.CostEstimate(
            flops=4 * count * count * HEAD_DIM,
            bytes_accessed=count * HEAD_DIM * 24,
            transcendentals=count * count,
        ),
        name="attend",
    )(
        query_raw,
        key_raw,
        value_t,
        inverse,
        inverse,
        gains,
        cosine,
        rope_sine,
        cosine,
        rope_sine,
        key_seg,
        query_seg,
    )


def attend_back_kernel(
    key_seg,
    query_seg,
    log_total,
    query_t,
    query,
    upstream,
    key,
    key_t,
    value,
    query_raw,
    key_raw,
    inverse,
    inverse_all,
    gains,
    cosine,
    rope_sine,
    cosine_all,
    rope_sine_all,
    weighted_query,
    weighted_key,
    dvalue_t,
    inner_query,
    inner_key,
    gain_sums,
    dkey,
    dvalue,
):
    step = pl.program_id(0)

    @pl.when(step == 0)
    def _():
        dkey[...] = jnp.zeros_like(dkey)
        dvalue[...] = jnp.zeros_like(dvalue)
        gain_sums[...] = jnp.zeros_like(gain_sums)

    scores = mm(key[...], query_t[...]) * score_scale
    probs = jnp.where(key_seg[:, :1] == query_seg[...], jnp.exp(scores - log_total[...]), 0.0)
    dvalue[...] += mm(probs.astype(jnp.bfloat16), upstream[...])
    dprobs = contract_cols(value[...], upstream[...])
    delta = jnp.sum(probs * dprobs, axis=0, keepdims=True)
    dscores = (probs * (dprobs - delta)).astype(jnp.bfloat16)
    dkey[...] += mm(dscores, query[...])
    turned = turn(mm(key_t[...], dscores) * score_scale, cosine[...], -rope_sine[...])
    product = turned * (query_raw[...] * inverse[0:1, :])
    weighted_query[...] = turned * gains[:, 0:1]
    inner_query[...] = jnp.sum(product * gains[:, 0:1], axis=0, keepdims=True)
    gain_sums[:, 0:1] += jnp.sum(product, axis=1, keepdims=True)

    @pl.when(step == pl.num_programs(0) - 1)
    def _():
        turned = turn(dkey[...].T * score_scale, cosine_all[...], -rope_sine_all[...])
        product = turned * (key_raw[...] * inverse_all[1:2, :])
        weighted_key[...] = turned * gains[:, 1:2]
        inner_key[...] = jnp.sum(product * gains[:, 1:2], axis=0, keepdims=True)
        gain_sums[:, 1:2] = jnp.sum(product, axis=1, keepdims=True)
        dvalue_t[...] = dvalue[...].T.astype(dvalue_t.dtype)


def attend_back(
    key_seg,
    query_seg,
    log_total,
    query_t,
    query,
    upstream,
    key,
    key_t,
    value,
    query_raw,
    key_raw,
    inverse,
    gains,
    cosine,
    rope_sine,
):
    count = query.shape[0]
    whole = lambda i: (0, 0)
    across = lambda rows: pl.BlockSpec((rows, query_block), lambda i: (0, i))
    down = pl.BlockSpec((query_block, HEAD_DIM), lambda i: (i, 0))
    all_of = lambda rows: pl.BlockSpec((rows, count), whole)
    tall = pl.BlockSpec((count, HEAD_DIM), whole)
    half = HEAD_DIM // 2
    return pl.pallas_call(
        attend_back_kernel,
        grid=(count // query_block,),
        in_specs=[
            tall,
            across(1),
            across(1),
            across(HEAD_DIM),
            down,
            down,
            tall,
            all_of(HEAD_DIM),
            tall,
            across(HEAD_DIM),
            all_of(HEAD_DIM),
            across(2),
            all_of(2),
            pl.BlockSpec((HEAD_DIM, 2), whole),
            across(half),
            across(half),
            all_of(half),
            all_of(half),
        ],
        out_specs=[
            across(HEAD_DIM),
            all_of(HEAD_DIM),
            all_of(HEAD_DIM),
            across(1),
            all_of(1),
            pl.BlockSpec((HEAD_DIM, 2), whole),
        ],
        out_shape=[
            jax.ShapeDtypeStruct((HEAD_DIM, count), jnp.float32),
            jax.ShapeDtypeStruct((HEAD_DIM, count), jnp.float32),
            jax.ShapeDtypeStruct((HEAD_DIM, count), jnp.bfloat16),
            jax.ShapeDtypeStruct((1, count), jnp.float32),
            jax.ShapeDtypeStruct((1, count), jnp.float32),
            jax.ShapeDtypeStruct((HEAD_DIM, 2), jnp.float32),
        ],
        scratch_shapes=[
            pltpu.VMEM((count, HEAD_DIM), jnp.float32),
            pltpu.VMEM((count, HEAD_DIM), jnp.float32),
        ],
        cost_estimate=pl.CostEstimate(
            flops=10 * count * count * HEAD_DIM,
            bytes_accessed=count * HEAD_DIM * 40,
            transcendentals=count * count,
        ),
        name="attend_back",
    )(
        key_seg,
        query_seg,
        log_total,
        query_t,
        query,
        upstream,
        key,
        key_t,
        value,
        query_raw,
        key_raw,
        inverse,
        inverse,
        gains,
        cosine,
        rope_sine,
        cosine,
        rope_sine,
    )


def local(
    tokens,
    segments,
    routes,
    route_gates,
    attn_gain,
    query_gain,
    key_gain,
    ffn_gain,
    w_query,
    w_key,
    w_value,
    w_out,
    w_gate,
    w_up,
    w_down,
    cotangent,
):
    row_count, width = tokens.shape
    top_count = routes.shape[1]
    devices = lax.axis_size("expert")
    groups = lax.axis_size("dp")
    me = lax.axis_index("expert")
    my_group = lax.axis_index("dp")
    seq_length = row_count * devices
    part = width // devices
    sharing = HEAD_DIM // part
    head = me // sharing
    sub = me % sharing
    w_rows = w_query.shape[0]
    w_half = w_rows // 2

    grouped = devices == 16 and groups == 2
    order = arrival_order(me) if grouped else jnp.arange(devices, dtype=jnp.int32)
    where = jnp.concatenate([order, my_group[None].astype(jnp.int32)])

    def gather(block):
        return Rounds(gather_rounds(block) if grouped else gather_whole(block))

    def scatter(make, tie=lambda addends: addends):
        return Rounds((scatter_rounds if grouped else scatter_whole)(make, seq_length, tie))

    def exchange(values):
        return lax.all_to_all(values, "expert", split_axis=0, concat_axis=0, tiled=True)

    def to_heads(rows):
        blocks = rows.reshape(rows.shape[0], HEADS, HEAD_DIM).transpose(1, 0, 2)
        return jnp.repeat(blocks, sharing, axis=0)

    def my_part(columns, axis):
        if sharing == 1:
            return columns
        return lax.dynamic_slice_in_dim(columns, sub * part, part, axis=axis)

    def by_half(values, axis):
        return jnp.where(my_group == 0, values, jnp.flip(values, axis))

    def dp_start(values):
        return swap(values, "dp", 1) if groups == 2 else lax.psum(values, "dp")

    def dp_end(values, arrived):
        total = arrived.astype(jnp.float32)
        return total + values.astype(jnp.float32) if groups == 2 else total

    waiting = []

    def weight_grad(left, right):
        pieces = left.shape[1] // 256 if grouped else 1
        step = left.shape[1] // pieces
        own = [
            contract_rows(left[:, i * step : (i + 1) * step], right).astype(jnp.bfloat16)
            for i in range(pieces)
        ]
        far = [dp_start(values) for values in own]
        waiting.extend((far, i) for i in range(pieces))
        return own, far

    def cross(*others):
        if not (waiting and grouped):
            return others
        far, i = waiting.pop(0)
        *others, far[i] = together(*others, far[i])
        return others

    def ride(rounds, *others):
        if not (waiting and grouped):
            return rounds.step(*others)
        far, i = waiting.pop(0)
        *others, far[i] = rounds.step(*others, far[i])
        return others

    resid_in = tokens.astype(jnp.float32)
    pre_in, normal_in, inverse_in = norm_rows(resid_in, attn_gain)
    normed_in = pre_in.astype(jnp.bfloat16)

    experts_all = devices * w_gate.shape[0]
    slots = min(row_count, row_count * top_count * 3 // (2 * experts_all))
    hits = routes[:, :, None] == jnp.arange(experts_all, dtype=jnp.int32)[None, None, :]
    gate_table = jnp.sum(jnp.where(hits, route_gates[:, :, None], 0.0), axis=1).T
    gate_high = lax.reduce_precision(gate_table, exponent_bits=8, mantissa_bits=7)
    gate_rows = jnp.pad(
        jnp.stack([gate_high, gate_table - gate_high], axis=1).astype(jnp.bfloat16),
        ((0, 0), (0, 14), (0, 3 * HEAD_DIM - row_count)),
    )
    if grouped:
        take = lambda w: lax.dynamic_slice_in_dim(w, my_group * w_half, w_half)
    else:
        take = lambda w: w
    sent_w = jnp.concatenate([to_heads(take(w)) for w in (w_query, w_key, w_value)], axis=2)
    taken = sent_w.shape[1]
    arrived = exchange(jnp.concatenate([sent_w, gate_rows], axis=1))

    key_seg = jnp.broadcast_to(segments[:, None], (seq_length, HEAD_DIM))
    query_seg = segments[None, :]
    cosine, rope_sine = rope_tables(jnp.arange(seq_length, dtype=jnp.int32))
    gains = jnp.stack(
        [
            lax.dynamic_slice_in_dim(query_gain, head * HEAD_DIM, HEAD_DIM),
            lax.dynamic_slice_in_dim(key_gain, head * HEAD_DIM, HEAD_DIM),
        ],
        axis=1,
    )
    if grouped:
        rounds = gather(jnp.concatenate([normed_in, take(w_out)], axis=0))
        rounds.step()
        rounds.step(key_seg, cosine, rope_sine, gains)
        (arrived,) = rounds.step(arrived)
        head_w = arrived[:, :taken]
        head_w_far = swap(head_w, "dp", 1)
        rounds.step()
        blocks = rounds.finish()
        head_w = by_half(jnp.stack([head_w, head_w_far], axis=1), 1).reshape(width, 3 * HEAD_DIM)
        out_far = swap(tails(blocks[: devices // 2], row_count, w_half), "dp", 1)
    else:
        blocks = gather(normed_in).finish()
        head_w = arrived[:, :taken].reshape(width, 3 * HEAD_DIM)
        out_full = lax.all_gather(w_out, "expert", axis=0, tiled=True)

    gate_pair = arrived[:, taken : taken + 2, :row_count].astype(jnp.float32)
    gate_mine = (gate_pair[:, 0] + gate_pair[:, 1])[order]
    chosen = gate_mine > 0.0
    before = jnp.arange(row_count)[:, None] < jnp.arange(row_count)[None, :]
    rank = mm(chosen.astype(jnp.bfloat16), before.astype(jnp.bfloat16)).astype(jnp.int32)
    rank = jnp.where(chosen, rank, -1)
    slot = jnp.arange(slots, dtype=jnp.int32)
    picks = rank[:, None, :] == slot[None, :, None]
    slot_gate = jnp.sum(jnp.where(picks, gate_mine[:, None, :], 0.0), axis=2).reshape(-1, 1)
    picks = picks.astype(jnp.bfloat16)
    unpicks = (rank[:, :, None] == slot[None, None, :]).astype(jnp.bfloat16)
    ones = jnp.ones_like(slot_gate)
    ff = w_gate.shape[2]
    w_both = jnp.concatenate([w_gate[0], w_up[0]], axis=1)

    cot_rounds = gather(cotangent)
    query_raw, key_raw, value, value_t, squares = heads_in(order, head_w, row_count, blocks)
    if sharing > 1:
        squares = jnp.stack(
            [jnp.sum(jnp.square(my_part(raw, 0)), axis=0) for raw in (query_raw, key_raw)]
        )
    (squares,) = cot_rounds.step(squares)
    squares = butterfly(squares, "expert")
    inverse = lax.rsqrt(squares / width + eps)
    query_t, query, key_t, key, attended, attended_t, log_total = attend(
        query_raw, key_raw, value_t, inverse, gains, cosine, rope_sine, key_seg, query_seg
    )
    if grouped:
        attended, out_far = cot_rounds.step(attended, out_far)
        out_cross = send(out_far, swap_core)

    attended_low = exchange(my_part(attended, 1).reshape(devices, row_count, part))
    if grouped:
        middle, normed_mid = out_project(
            where, attended_low, tokens, ffn_gain[None, :], blocks, out_far, out_cross
        )
    else:
        attended_low = attended_low.transpose(1, 0, 2).reshape(row_count, width)
        middle = resid_in + mm(attended_low, out_full)
        normed_mid = norm_rows(middle, ffn_gain)[0].astype(jnp.bfloat16)
    (normed_mid,) = cot_rounds.step(normed_mid)

    mid_rounds = gather(normed_mid)
    head_w_t = jnp.concatenate(
        [my_part(head_w[:, i * HEAD_DIM : (i + 1) * HEAD_DIM], 1).T for i in range(3)], axis=0
    )
    (head_w_t,) = mid_rounds.step(head_w_t)
    rows_in = pick(picks, ones, mid_rounds.finish())
    (rows_in,) = cot_rounds.step(rows_in)
    grad_eo = pick(picks, slot_gate, cot_rounds.finish())
    gate_up = mm(rows_in, w_both)
    gate_in, up_in = gate_up[:, :ff], gate_up[:, ff:]
    sigmoid_in = jax.nn.sigmoid(gate_in)
    silu_in = gate_in * sigmoid_in
    hidden = (silu_in * up_in).astype(jnp.bfloat16)
    grad_down, down_far = weight_grad(hidden, grad_eo)

    def give_back(produce):
        def some(first, count):
            here = slice(first // row_count, (first + count) // row_count)
            rows = produce(slice(here.start * slots, here.stop * slots))
            return jnp.einsum(
                "bts,bsd->btd",
                unpicks[here],
                rows.astype(jnp.bfloat16).reshape(-1, slots, width),
                preferred_element_type=jnp.bfloat16,
            ).reshape(count, width)

        return some

    hidden_next, grad_eo_next = together(hidden, grad_eo, *grad_down)[:2]
    mix_rounds = scatter(
        give_back(lambda some: mm(hidden_next[some], w_down[0]) * slot_gate[some])
    )
    grad_hidden = contract_cols(grad_eo_next, w_down[0])
    grad_pre = jnp.concatenate(
        [
            (
                grad_hidden * up_in * sigmoid_in * (1.0 + gate_in * (1.0 - sigmoid_in))
            ).astype(jnp.bfloat16),
            (grad_hidden * silu_in).astype(jnp.bfloat16),
        ],
        axis=1,
    )
    (grad_pre,) = ride(mix_rounds, grad_pre)
    row_rounds = scatter(
        give_back(lambda some: contract_cols(grad_pre[some], w_both)),
        lambda addends: ride(mix_rounds, addends)[0],
    )
    grad_both, both_far = weight_grad(rows_in, grad_pre)
    far, i = waiting.pop(0) if grouped else (None, 0)
    if grouped:
        (far[i], *_) = step_all([row_rounds, mix_rounds], far[i], *grad_both[:1])
    else:
        row_rounds.step()
    ride(row_rounds, *mix_rounds.sent, *grad_both[1:2])
    row_rounds.step(*grad_both[2:4])
    ride(row_rounds, *grad_both[4:5])
    ride(row_rounds, *grad_both[5:6])
    grad_normed_mid = row_rounds.finish()

    grad_out = cotangent.astype(jnp.float32)
    _, normal_mid, inverse_mid = norm_rows(middle, ffn_gain)
    mid_back, grad_ffn_gain = norm_back(grad_normed_mid, normal_mid, inverse_mid, ffn_gain)
    grad_middle = grad_out + mid_back
    grad_branch = grad_middle.astype(jnp.bfloat16)
    if grouped:
        grad_columns = out_project_back(where, grad_branch, blocks, out_far, out_cross)
        (grad_columns,) = ride(mix_rounds, grad_columns)
    else:
        grad_columns = to_heads(contract_cols(grad_branch, out_full).astype(jnp.bfloat16))
    grad_attended = exchange(grad_columns).reshape(seq_length, HEAD_DIM)
    if groups == 2:
        (down_total,) = merge(grad_down, down_far, 1)
        grad_attended, down_total, *_ = cross(grad_attended, down_total, *grad_both[6:])
    else:
        down_total = down_far[0].astype(jnp.float32)
    mixed = mix_rounds.finish()
    activations = (middle + mixed).astype(jnp.bfloat16)
    branch_all = lax.all_gather(
        after(grad_branch, grad_attended), "expert", axis=0, tiled=True
    )

    weighted_query, weighted_key, grad_value_t, inner_query, inner_key, gain_sums = attend_back(
        key_seg,
        query_seg,
        log_total,
        query_t,
        query,
        grad_attended,
        key,
        key_t,
        value,
        query_raw,
        key_raw,
        inverse,
        gains,
        cosine,
        rope_sine,
    )
    inner = jnp.concatenate([inner_query, inner_key], axis=0)
    if sharing > 1:
        inner = jnp.stack(
            [
                jnp.sum(my_part(weighted * raw * at, 0), axis=0)
                for weighted, raw, at in (
                    (weighted_query, query_raw, inverse[0:1]),
                    (weighted_key, key_raw, inverse[1:2]),
                )
            ]
        )
    (inner,) = cross(inner)
    inner = butterfly(inner, "expert") / width
    (inner,) = cross(inner)
    grad_raw_t = jnp.concatenate(
        [
            my_part(
                (at * (weighted - raw * at * mean)).astype(jnp.bfloat16),
                0,
            )
            for weighted, raw, at, mean in (
                (weighted_query, query_raw, inverse[0:1], inner[0:1]),
                (weighted_key, key_raw, inverse[1:2], inner[1:2]),
            )
        ]
        + [my_part(grad_value_t, 0)],
        axis=0,
    )
    in_rounds = scatter(
        lambda first, count: project(order, grad_raw_t, head_w_t, row_count, first, count)
    )
    grad_w_t = stack_product(order, grad_raw_t, row_count, blocks)
    grad_attn_gain = jnp.sum(grad_w_t * head_w_t.astype(jnp.float32), axis=0) / attn_gain
    w_columns = exchange(
        grad_w_t.astype(jnp.bfloat16).reshape(3 * part, devices, w_rows).transpose(1, 0, 2)
    )
    ride(in_rounds)

    def placed(values):
        return lax.dynamic_update_slice_in_dim(
            jnp.zeros((width,), jnp.float32), values, me * part, 0
        )

    gain_parts = jnp.stack(
        [
            grad_attn_gain,
            placed(my_part(gain_sums[:, 0], 0)),
            placed(my_part(gain_sums[:, 1], 0)),
            grad_ffn_gain,
        ]
    )
    out_part = mm(my_part(attended_t, 0), branch_all).astype(jnp.bfloat16)
    out_part, w_columns = in_rounds.step(out_part, w_columns)
    out_part_far = dp_start(out_part)
    dense = [
        w_columns[:, i * part : (i + 1) * part].reshape(width, w_rows).T for i in range(3)
    ]
    dense_far = [dp_start(values) for values in dense]
    if groups == 2:
        both_total = merge(grad_both[:4], both_far[:4], 2, len(grad_both))
        gain_parts, *both_total = ride(in_rounds, gain_parts, *both_total)
        both_total = merge(grad_both[4:], both_far[4:], 2, 4, both_total)
    else:
        in_rounds.step()
        both_total = both_far[0].astype(jnp.float32)
        both_total = (both_total[:, :ff], both_total[:, ff:])
    out_part_far, dense_far[0] = in_rounds.step(out_part_far, dense_far[0])
    dense_far[1], *both_total = in_rounds.step(dense_far[1], *both_total)
    gate_total, up_total = both_total
    grad_normed_in = in_rounds.finish()
    grad_normed_in, gain_parts = together(grad_normed_in, gain_parts)
    gain_parts = butterfly(gain_parts, "expert")
    gain_parts, dense_far[2], gate_total = together(gain_parts, dense_far[2], gate_total)
    gain_total = butterfly(gain_parts, "dp")
    in_back, _ = norm_back(grad_normed_in, normal_in, inverse_in, attn_gain)
    input_grad = (grad_middle + in_back).astype(jnp.bfloat16)

    return (
        activations,
        input_grad,
        gain_total[0],
        gain_total[1],
        gain_total[2],
        gain_total[3],
        dp_end(dense[0], dense_far[0]),
        dp_end(dense[1], dense_far[1]),
        dp_end(dense[2], dense_far[2]),
        dp_end(out_part, out_part_far),
        gate_total[None],
        up_total[None],
        down_total[None],
    )


def solution(mesh):
    in_specs = (
        P(("dp", "expert"), None),
        P("dp"),
        P(("dp", "expert"), None),
        P(("dp", "expert"), None),
        P(),
        P(),
        P(),
        P(),
        P("expert", None),
        P("expert", None),
        P("expert", None),
        P("expert", None),
        P("expert", None, None),
        P("expert", None, None),
        P("expert", None, None),
        P(("dp", "expert"), None),
    )
    out_specs = (
        P(("dp", "expert"), None),
        P(("dp", "expert"), None),
        P(),
        P(),
        P(),
        P(),
        P("expert", None),
        P("expert", None),
        P("expert", None),
        P("expert", None),
        P("expert", None, None),
        P("expert", None, None),
        P("expert", None, None),
    )
    return jax.shard_map(local, mesh=mesh, in_specs=in_specs, out_specs=out_specs, check_vma=False)
```

```python
import functools

import jax
import jax.numpy as jnp
from jax import lax
from jax.experimental import pallas as pl
from jax.experimental.pallas import tpu as pltpu
from jax.sharding import PartitionSpec as P

HEADS = 16
HEAD_DIM = 128


eps = 1e-05
rope_base = 50000.0
negative = -1e30
score_scale = HEAD_DIM ** (-0.5)
query_block = 256


def norm_rows(values, norm_gain):
    inverse = lax.rsqrt(jnp.mean(values * values, axis=-1, keepdims=True) + eps)
    normal = values * inverse
    return (normal * norm_gain, normal, inverse)


def norm_back(upstream, normal, inverse, norm_gain):
    weighted = upstream * norm_gain
    inner_mean = jnp.mean(weighted * normal, axis=-1, keepdims=True)
    return (inverse * (weighted - normal * inner_mean), jnp.sum(upstream * normal, axis=0))


def rope_tables(positions):
    half_dim = HEAD_DIM // 2
    frequency = rope_base ** (-(jnp.arange(half_dim, dtype=jnp.float32) * 2.0 / HEAD_DIM))
    theta = frequency[:, None] * positions.astype(jnp.float32)[None, :]
    return (jnp.cos(theta), jnp.sin(theta))


def mm(left, right):
    return jnp.dot(left, right, preferred_element_type=jnp.float32)


def contract_rows(left, right):
    return lax.dot_general(
        left, right, (((0,), (0,)), ((), ())), preferred_element_type=jnp.float32
    )


def contract_cols(left, right):
    return lax.dot_general(
        left, right, (((1,), (1,)), ((), ())), preferred_element_type=jnp.float32
    )


def swap(values, axis, step):
    count = lax.axis_size(axis)
    return lax.ppermute(values, axis, [(i, i ^ step) for i in range(count)])


def together(*values):
    return lax.optimization_barrier(values)


def after(values, *others):
    return lax.optimization_barrier((values,) + others)[0]


def butterfly(values, axis):
    step = 1
    while step < lax.axis_size(axis):
        if 2 * step < lax.axis_size(axis):
            one, two, three = [swap(values, axis, times * step) for times in (1, 2, 3)]
            values = (values + one) + (two + three)
            step *= 4
        else:
            values = values + swap(values, axis, step)
            step *= 2
    return values


near_order = ((0, 1, 2, 3), (1, 0, 2, 3), (2, 3, 1, 0), (3, 2, 1, 0))


def moves(target):
    pairs = []
    for index in range(16):
        far = target(index // 4)
        if far is not None:
            pairs.append((index, far * 4 + index % 4))
    return pairs


swap_near = moves(lambda z: z ^ 1)
swap_middle = moves(lambda z: {1: 2, 2: 1}.get(z))
move_out = moves(lambda z: {1: 0, 2: 3}.get(z))
move_in = moves(lambda z: {0: 1, 3: 2}.get(z))
swap_row = [(i, i ^ 2) for i in range(16)]
swap_core = [(i, i ^ 1) for i in range(16)]


def send(values, pairs):
    return lax.ppermute(values, "expert", pairs)


def arrival_order(me):
    near = jnp.asarray(near_order, jnp.int32)[me // 4] * 4
    row, core = (me // 2) % 2, me % 2
    return jnp.concatenate(
        [near + (row ^ j) * 2 + (core ^ i) for i in (0, 1) for j in (0, 1)]
    ).astype(jnp.int32)


class Rounds:
    def __init__(self, steps):
        self.steps = steps
        self.result = None
        self.over = False
        self.sent = ()
        self._go(None)

    def _go(self, arrived):
        try:
            self.sent = self.steps.send(arrived)
        except StopIteration as stop:
            self.result, self.sent, self.over = stop.value, (), True

    def step(self, *others):
        return step_all([self], *others)

    def finish(self):
        while not self.over:
            self.step()
        return self.result


def step_all(rounds, *others):
    sent = [values for one in rounds for values in one.sent]
    values = together(*sent, *others) if sent or others else ()
    at = 0
    for one in rounds:
        count = len(one.sent)
        if not one.over:
            one._go(values[at : at + count])
        at += count
    return values[at:]


def gather_rounds(block):
    at = lax.axis_index("expert") // 4
    outer = (at == 0) | (at == 3)
    first, second, row = yield (
        send(block, swap_near),
        send(block, swap_middle),
        send(block, swap_row),
    )
    third, second_out, row_first, core = yield (
        send(first, swap_middle),
        send(second, move_out),
        send(first, swap_row),
        send(block, swap_core),
    )
    second = jnp.where(outer, second_out, second)
    third_out, row_second, core_first, core_row = yield (
        send(third, move_out),
        send(second, swap_row),
        send(first, swap_core),
        send(row, swap_core),
    )
    third = jnp.where(outer, third_out, third)
    row_third, core_second, core_third, core_row_first, core_row_second = yield (
        send(third, swap_row),
        send(second, swap_core),
        send(third, swap_core),
        send(row_first, swap_core),
        send(row_second, swap_core),
    )
    (core_row_third,) = yield (send(row_third, swap_core),)
    return [
        block,
        first,
        second,
        third,
        row,
        row_first,
        row_second,
        row_third,
        core,
        core_first,
        core_second,
        core_third,
        core_row,
        core_row_first,
        core_row_second,
        core_row_third,
    ]


def gather_whole(block):
    yield ()
    return list(lax.all_gather(block, "expert", axis=0))


def add_low(left, right):
    return (left.astype(jnp.float32) + right.astype(jnp.float32)).astype(jnp.bfloat16)


def scatter_rounds(make, count, tie, both_first):
    far = send(tie(make(count // 2, count // 2)), swap_core)
    if both_first:
        far, close = yield (far, make(0, count // 2))
    else:
        (far,) = yield (far,)
        close = make(0, count // 2)
    rows = count // 16

    def both(j, k):
        here = slice((j * 4 + k) * rows, (j * 4 + k + 1) * rows)
        return add_low(close[here], far[here])

    (row,) = yield (send(both(1, 3), swap_row),)
    third = add_low(both(0, 3), row)
    row, third_in = yield (send(both(1, 2), swap_row), send(third, move_in))
    second = add_low(both(0, 2), row)
    third = add_low(third, third_in)
    row, second_in, third_in = yield (
        send(both(1, 1), swap_row),
        send(second, move_in),
        send(third, swap_middle),
    )
    first = add_low(add_low(both(0, 1), row), third_in)
    second = add_low(second, second_in)
    row, second_in, first_in = yield (
        send(both(1, 0), swap_row),
        send(second, swap_middle),
        send(first, swap_near),
    )
    return (
        both(0, 0).astype(jnp.float32)
        + row.astype(jnp.float32)
        + second_in.astype(jnp.float32)
        + first_in.astype(jnp.float32)
    )


def scatter_whole(make, count, tie, both_first):
    yield ()
    return lax.psum_scatter(
        tie(make(0, count)), "expert", scatter_dimension=0, tiled=True
    ).astype(jnp.float32)


def pick_kernel(picks, scale, *refs):
    *blocks, out = refs
    slots = picks.shape[1]
    for index, block in enumerate(blocks):
        here = slice(index * slots, (index + 1) * slots)
        out[here, :] = (mm(picks[index], block[...]) * scale[here, :]).astype(out.dtype)


def pick(picks, scale, blocks):
    count, slots, tokens = picks.shape
    width = blocks[0].shape[1]
    return pl.pallas_call(
        pick_kernel,
        out_shape=jax.ShapeDtypeStruct((count * slots, width), jnp.bfloat16),
        cost_estimate=pl.CostEstimate(
            flops=2 * count * tokens * slots * width,
            bytes_accessed=2 * count * (tokens + slots) * width,
            transcendentals=0,
        ),
        name="pick",
    )(picks, scale, *blocks)


def merge_kernel(count, parts, *refs):
    pairs, outs = refs[: 2 * count], refs[-parts:]
    width = outs[0].shape[1]
    for index in range(count):

        @pl.when(pl.program_id(0) == index)
        def _():
            total = pairs[index][...].astype(jnp.float32) + pairs[count + index][...].astype(
                jnp.float32
            )
            for i, out in enumerate(outs):
                out[...] = total[:, i * width : (i + 1) * width]


def merge(own, far, parts, pieces=None, before=None):
    count = len(own)
    begin = pieces if before else 0
    before = before or []
    pieces = begin + count if before else pieces or count
    rows, width = own[0].shape
    return pl.pallas_call(
        functools.partial(merge_kernel, count, parts),
        grid=(count,),
        in_specs=[pl.BlockSpec((rows, width), lambda i: (0, 0))] * (2 * count)
        + [pl.BlockSpec(memory_space=pl.ANY)] * len(before),
        out_specs=[pl.BlockSpec((rows, width // parts), lambda i: (begin + i, 0))] * parts,
        out_shape=[jax.ShapeDtypeStruct((pieces * rows, width // parts), jnp.float32)] * parts,
        input_output_aliases={2 * count + i: i for i in range(len(before))},
        cost_estimate=pl.CostEstimate(
            flops=count * rows * width,
            bytes_accessed=8 * count * rows * width,
            transcendentals=0,
        ),
        compiler_params=pltpu.CompilerParams(vmem_limit_bytes=28 * 2**20),
        name="merge",
    )(*own, *far, *before)


def project_kernel(order, left_t, left_next_t, right, out):
    left = jnp.concatenate([left_t[...].T, left_next_t[...].T], axis=0)
    out[...] = mm(left, right[...]).astype(out.dtype)


def project(order, left_t, right, rows, first, count):
    depth, width = right.shape
    begin = first // rows
    return pl.pallas_call(
        project_kernel,
        grid_spec=pltpu.PrefetchScalarGridSpec(
            num_scalar_prefetch=1,
            grid=(count // (2 * rows),),
            in_specs=[
                pl.BlockSpec((depth, rows), lambda i, order: (0, order[begin + 2 * i])),
                pl.BlockSpec((depth, rows), lambda i, order: (0, order[begin + 2 * i + 1])),
                pl.BlockSpec((depth, width), lambda i, order: (0, 0)),
            ],
            out_specs=pl.BlockSpec((2 * rows, width), lambda i, order: (i, 0)),
        ),
        out_shape=jax.ShapeDtypeStruct((count, width), jnp.bfloat16),
        cost_estimate=pl.CostEstimate(
            flops=2 * count * depth * width,
            bytes_accessed=2 * (count * (depth + width) + depth * width),
            transcendentals=0,
        ),
        compiler_params=pltpu.CompilerParams(vmem_limit_bytes=28 * 2**20),
        name="project",
    )(order, left_t, left_t, right)


scalars = pl.BlockSpec(memory_space=pltpu.SMEM)
vectors = pl.BlockSpec(memory_space=pltpu.VMEM)


def lanes(order, index, rows):
    return pl.ds(pl.multiple_of(order[index] * rows, rows), rows)


def stack_kernel(rows, order, left_t, *refs):
    *blocks, out = refs
    for index in range(0, len(blocks), 4):
        four = range(index, index + 4)
        left = jnp.concatenate([left_t[:, lanes(order, i, rows)] for i in four], axis=1)
        right = jnp.concatenate([blocks[i][:rows] for i in four], axis=0)
        term = mm(left, right)
        if index == 0:
            out[...] = term
        else:
            out[...] += term


def stack_product(order, left_t, rows, blocks):
    width = blocks[0].shape[1]
    return pl.pallas_call(
        functools.partial(stack_kernel, rows),
        in_specs=[scalars, vectors] + [vectors] * len(blocks),
        out_specs=vectors,
        out_shape=jax.ShapeDtypeStruct((left_t.shape[0], width), jnp.float32),
        cost_estimate=pl.CostEstimate(
            flops=2 * left_t.size * width,
            bytes_accessed=2 * len(blocks) * rows * width,
            transcendentals=0,
        ),
        compiler_params=pltpu.CompilerParams(vmem_limit_bytes=28 * 2**20),
        name="stack_product",
    )(order, left_t, *blocks)


def heads_kernel(rows, order, weight, *refs):
    *blocks, query_t, key_t, value, value_t, squares = refs
    for index in range(0, len(blocks), 4):
        four = range(index, index + 4)
        raw = mm(jnp.concatenate([blocks[i][:rows] for i in four], axis=0), weight[...])
        for i in four:
            own = raw[(i - index) * rows : (i - index + 1) * rows]
            here = lanes(order, i, rows)
            query = own[:, :HEAD_DIM].T
            key = own[:, HEAD_DIM : 2 * HEAD_DIM].T
            query_t[:, here] = query
            key_t[:, here] = key
            value[here, :] = own[:, 2 * HEAD_DIM :].astype(value.dtype)
            value_t[:, here] = own[:, 2 * HEAD_DIM :].T.astype(value.dtype)
            squares[0:1, here] = jnp.sum(query * query, axis=0, keepdims=True)
            squares[1:2, here] = jnp.sum(key * key, axis=0, keepdims=True)


def heads_in(order, weight, rows, blocks):
    width = blocks[0].shape[1]
    count = len(blocks) * rows
    return pl.pallas_call(
        functools.partial(heads_kernel, rows),
        in_specs=[scalars, vectors] + [vectors] * len(blocks),
        out_specs=[vectors] * 5,
        out_shape=[
            jax.ShapeDtypeStruct((HEAD_DIM, count), jnp.float32),
            jax.ShapeDtypeStruct((HEAD_DIM, count), jnp.float32),
            jax.ShapeDtypeStruct((count, HEAD_DIM), jnp.bfloat16),
            jax.ShapeDtypeStruct((HEAD_DIM, count), jnp.bfloat16),
            jax.ShapeDtypeStruct((2, count), jnp.float32),
        ],
        cost_estimate=pl.CostEstimate(
            flops=2 * count * width * 3 * HEAD_DIM,
            bytes_accessed=2 * count * width,
            transcendentals=0,
        ),
        name="heads_in",
    )(order, weight, *blocks)


def tail_kernel(*refs):
    *blocks, out = refs
    rows = blocks[0].shape[0]
    for index, block in enumerate(blocks):
        out[index * rows : (index + 1) * rows, :] = block[...]


def tail_specs(blocks, rows, tail):
    width = blocks[0].shape[1]
    return [pl.BlockSpec((tail, width), lambda i: (rows // tail, 0))] * len(blocks)


def tails(blocks, rows, tail):
    width = blocks[0].shape[1]
    return pl.pallas_call(
        tail_kernel,
        grid=(1,),
        in_specs=tail_specs(blocks, rows, tail),
        out_specs=pl.BlockSpec((len(blocks) * tail, width), lambda i: (0, 0)),
        out_shape=jax.ShapeDtypeStruct((len(blocks) * tail, width), jnp.bfloat16),
        name="tails",
    )(*blocks)


def four(refs, index):
    return jnp.concatenate([ref[...] for ref in refs[index : index + 4]], axis=0)


def far_four(far, cross, index):
    rows = far.shape[0] // 2
    ref, at = (far, index // 4) if index < 8 else (cross, index // 4 - 2)
    return ref[at * rows : (at + 1) * rows, :]


def out_kernel(where, attended, resid, gain, *refs):
    *near, far, cross, middle, normed = refs
    count = len(near)
    half = HEAD_DIM // 2
    first_group = where[count] == 0
    total = resid[...].astype(jnp.float32)
    for index in range(0, count, 4):
        near_left, far_left = [], []
        for i in range(index, index + 4):
            columns = attended[where[i]].astype(jnp.float32)
            low, high = columns[:, :half], columns[:, half:]
            near_left.append(jnp.where(first_group, low, high))
            far_left.append(jnp.where(first_group, high, low))
        total += mm(jnp.concatenate(near_left, axis=1).astype(jnp.bfloat16), four(near, index))
        total += mm(
            jnp.concatenate(far_left, axis=1).astype(jnp.bfloat16), far_four(far, cross, index)
        )
    middle[...] = total
    inverse = lax.rsqrt(jnp.mean(total * total, axis=-1, keepdims=True) + eps)
    normed[...] = (total * inverse * gain[...]).astype(normed.dtype)


def whole_specs(*arrays):
    return [pl.BlockSpec(array.shape, lambda i, rank=array.ndim: (0,) * rank) for array in arrays]


def out_project(where, attended, resid, gain, blocks, far, cross):
    rows, width = resid.shape
    tail = blocks[0].shape[0] - rows
    return pl.pallas_call(
        out_kernel,
        grid=(1,),
        in_specs=[scalars]
        + whole_specs(attended, resid, gain)
        + tail_specs(blocks, rows, tail)
        + whole_specs(far, cross),
        out_specs=whole_specs(resid, resid),
        out_shape=[
            jax.ShapeDtypeStruct((rows, width), jnp.float32),
            jax.ShapeDtypeStruct((rows, width), jnp.bfloat16),
        ],
        cost_estimate=pl.CostEstimate(
            flops=2 * rows * width * width,
            bytes_accessed=2 * width * width,
            transcendentals=0,
        ),
        name="out_project",
    )(where, attended, resid, gain, *blocks, far, cross)


def out_back_kernel(where, branch, *refs):
    *near_refs, far_ref, cross, out = refs
    count = len(near_refs)
    half = HEAD_DIM // 2
    first_group = where[count] == 0
    for index in range(0, count, 4):
        near = contract_cols(branch[...], four(near_refs, index))
        far = contract_cols(branch[...], far_four(far_ref, cross, index))
        for i in range(index, index + 4):
            here = slice((i - index) * half, (i - index + 1) * half)
            low = jnp.where(first_group, near[:, here], far[:, here])
            high = jnp.where(first_group, far[:, here], near[:, here])
            out[where[i]] = jnp.concatenate([low, high], axis=1).astype(out.dtype)


def out_project_back(where, branch, blocks, far, cross):
    rows, width = branch.shape
    tail = blocks[0].shape[0] - rows
    shape = (len(blocks), rows, HEAD_DIM)
    return pl.pallas_call(
        out_back_kernel,
        grid=(1,),
        in_specs=[scalars]
        + whole_specs(branch)
        + tail_specs(blocks, rows, tail)
        + whole_specs(far, cross),
        out_specs=pl.BlockSpec(shape, lambda i: (0, 0, 0)),
        out_shape=jax.ShapeDtypeStruct(shape, jnp.bfloat16),
        cost_estimate=pl.CostEstimate(
            flops=2 * rows * width * width,
            bytes_accessed=2 * width * width,
            transcendentals=0,
        ),
        name="out_project_back",
    )(where, branch, *blocks, far, cross)


def turn(values, cosine, rope_sine):
    half = HEAD_DIM // 2
    first, second = values[:half], values[half:]
    return jnp.concatenate(
        [first * cosine - second * rope_sine, second * cosine + first * rope_sine], axis=0
    )


def attend_kernel(
    query_raw,
    key_raw,
    value_t,
    inverse,
    inverse_all,
    gains,
    cosine,
    rope_sine,
    cosine_all,
    rope_sine_all,
    key_seg,
    query_seg,
    query_t,
    query,
    key_t,
    key,
    out,
    out_t,
    log_total,
):
    @pl.when(pl.program_id(0) == 0)
    def _():
        turned = turn(
            key_raw[...] * inverse_all[1:2, :] * gains[:, 1:2], cosine_all[...], rope_sine_all[...]
        ).astype(jnp.bfloat16)
        key_t[...] = turned
        key[...] = turned.T

    turned = turn(
        query_raw[...] * inverse[0:1, :] * gains[:, 0:1], cosine[...], rope_sine[...]
    ).astype(jnp.bfloat16)
    query_t[...] = turned
    query[...] = turned.T
    scores = mm(key[...], turned) * score_scale
    scores = jnp.where(key_seg[:, :1] == query_seg[...], scores, negative)
    peak = jnp.max(scores, axis=0, keepdims=True)
    weights = jnp.exp(scores - peak)
    total = jnp.sum(weights, axis=0, keepdims=True)
    result = mm(value_t[...], weights.astype(jnp.bfloat16)) / total
    out_t[...] = result.astype(out_t.dtype)
    out[...] = result.T.astype(out.dtype)
    log_total[...] = peak + jnp.log(total)


def attend(query_raw, key_raw, value_t, inverse, gains, cosine, rope_sine, key_seg, query_seg):
    count = query_raw.shape[1]
    whole = lambda i: (0, 0)
    across = lambda rows: pl.BlockSpec((rows, query_block), lambda i: (0, i))
    down = pl.BlockSpec((query_block, HEAD_DIM), lambda i: (i, 0))
    all_of = lambda rows: pl.BlockSpec((rows, count), whole)
    low, half = jnp.bfloat16, HEAD_DIM // 2
    return pl.pallas_call(
        attend_kernel,
        grid=(count // query_block,),
        in_specs=[
            across(HEAD_DIM),
            all_of(HEAD_DIM),
            all_of(HEAD_DIM),
            across(2),
            all_of(2),
            pl.BlockSpec((HEAD_DIM, 2), whole),
            across(half),
            across(half),
            all_of(half),
            all_of(half),
            pl.BlockSpec((count, HEAD_DIM), whole),
            across(1),
        ],
        out_specs=[
            across(HEAD_DIM),
            down,
            all_of(HEAD_DIM),
            pl.BlockSpec((count, HEAD_DIM), whole),
            down,
            across(HEAD_DIM),
            across(1),
        ],
        out_shape=[
            jax.ShapeDtypeStruct((HEAD_DIM, count), low),
            jax.ShapeDtypeStruct((count, HEAD_DIM), low),
            jax.ShapeDtypeStruct((HEAD_DIM, count), low),
            jax.ShapeDtypeStruct((count, HEAD_DIM), low),
            jax.ShapeDtypeStruct((count, HEAD_DIM), low),
            jax.ShapeDtypeStruct((HEAD_DIM, count), low),
            jax.ShapeDtypeStruct((1, count), jnp.float32),
        ],
        cost_estimate=pl.CostEstimate(
            flops=4 * count * count * HEAD_DIM,
            bytes_accessed=count * HEAD_DIM * 24,
            transcendentals=count * count,
        ),
        name="attend",
    )(
        query_raw,
        key_raw,
        value_t,
        inverse,
        inverse,
        gains,
        cosine,
        rope_sine,
        cosine,
        rope_sine,
        key_seg,
        query_seg,
    )


def attend_back_kernel(
    key_seg,
    query_seg,
    log_total,
    query_t,
    query,
    upstream,
    key,
    key_t,
    value,
    query_raw,
    key_raw,
    inverse,
    inverse_all,
    gains,
    cosine,
    rope_sine,
    cosine_all,
    rope_sine_all,
    weighted_query,
    weighted_key,
    dvalue_t,
    inner_query,
    inner_key,
    gain_sums,
    dkey,
    dvalue,
):
    step = pl.program_id(0)

    @pl.when(step == 0)
    def _():
        dkey[...] = jnp.zeros_like(dkey)
        dvalue[...] = jnp.zeros_like(dvalue)
        gain_sums[...] = jnp.zeros_like(gain_sums)

    scores = mm(key[...], query_t[...]) * score_scale
    probs = jnp.where(key_seg[:, :1] == query_seg[...], jnp.exp(scores - log_total[...]), 0.0)
    dvalue[...] += mm(probs.astype(jnp.bfloat16), upstream[...])
    dprobs = contract_cols(value[...], upstream[...])
    delta = jnp.sum(probs * dprobs, axis=0, keepdims=True)
    dscores = (probs * (dprobs - delta)).astype(jnp.bfloat16)
    dkey[...] += mm(dscores, query[...])
    turned = turn(mm(key_t[...], dscores) * score_scale, cosine[...], -rope_sine[...])
    product = turned * (query_raw[...] * inverse[0:1, :])
    weighted_query[...] = turned * gains[:, 0:1]
    inner_query[...] = jnp.sum(product * gains[:, 0:1], axis=0, keepdims=True)
    gain_sums[:, 0:1] += jnp.sum(product, axis=1, keepdims=True)

    @pl.when(step == pl.num_programs(0) - 1)
    def _():
        turned = turn(dkey[...].T * score_scale, cosine_all[...], -rope_sine_all[...])
        product = turned * (key_raw[...] * inverse_all[1:2, :])
        weighted_key[...] = turned * gains[:, 1:2]
        inner_key[...] = jnp.sum(product * gains[:, 1:2], axis=0, keepdims=True)
        gain_sums[:, 1:2] = jnp.sum(product, axis=1, keepdims=True)
        dvalue_t[...] = dvalue[...].T.astype(dvalue_t.dtype)


def attend_back(
    key_seg,
    query_seg,
    log_total,
    query_t,
    query,
    upstream,
    key,
    key_t,
    value,
    query_raw,
    key_raw,
    inverse,
    gains,
    cosine,
    rope_sine,
):
    count = query.shape[0]
    whole = lambda i: (0, 0)
    across = lambda rows: pl.BlockSpec((rows, query_block), lambda i: (0, i))
    down = pl.BlockSpec((query_block, HEAD_DIM), lambda i: (i, 0))
    all_of = lambda rows: pl.BlockSpec((rows, count), whole)
    tall = pl.BlockSpec((count, HEAD_DIM), whole)
    half = HEAD_DIM // 2
    return pl.pallas_call(
        attend_back_kernel,
        grid=(count // query_block,),
        in_specs=[
            tall,
            across(1),
            across(1),
            across(HEAD_DIM),
            down,
            down,
            tall,
            all_of(HEAD_DIM),
            tall,
            across(HEAD_DIM),
            all_of(HEAD_DIM),
            across(2),
            all_of(2),
            pl.BlockSpec((HEAD_DIM, 2), whole),
            across(half),
            across(half),
            all_of(half),
            all_of(half),
        ],
        out_specs=[
            across(HEAD_DIM),
            all_of(HEAD_DIM),
            all_of(HEAD_DIM),
            across(1),
            all_of(1),
            pl.BlockSpec((HEAD_DIM, 2), whole),
        ],
        out_shape=[
            jax.ShapeDtypeStruct((HEAD_DIM, count), jnp.float32),
            jax.ShapeDtypeStruct((HEAD_DIM, count), jnp.float32),
            jax.ShapeDtypeStruct((HEAD_DIM, count), jnp.bfloat16),
            jax.ShapeDtypeStruct((1, count), jnp.float32),
            jax.ShapeDtypeStruct((1, count), jnp.float32),
            jax.ShapeDtypeStruct((HEAD_DIM, 2), jnp.float32),
        ],
        scratch_shapes=[
            pltpu.VMEM((count, HEAD_DIM), jnp.float32),
            pltpu.VMEM((count, HEAD_DIM), jnp.float32),
        ],
        cost_estimate=pl.CostEstimate(
            flops=10 * count * count * HEAD_DIM,
            bytes_accessed=count * HEAD_DIM * 40,
            transcendentals=count * count,
        ),
        name="attend_back",
    )(
        key_seg,
        query_seg,
        log_total,
        query_t,
        query,
        upstream,
        key,
        key_t,
        value,
        query_raw,
        key_raw,
        inverse,
        inverse,
        gains,
        cosine,
        rope_sine,
        cosine,
        rope_sine,
    )


def local(
    tokens,
    segments,
    routes,
    route_gates,
    attn_gain,
    query_gain,
    key_gain,
    ffn_gain,
    w_query,
    w_key,
    w_value,
    w_out,
    w_gate,
    w_up,
    w_down,
    cotangent,
):
    row_count, width = tokens.shape
    top_count = routes.shape[1]
    devices = lax.axis_size("expert")
    groups = lax.axis_size("dp")
    me = lax.axis_index("expert")
    my_group = lax.axis_index("dp")
    seq_length = row_count * devices
    part = width // devices
    sharing = HEAD_DIM // part
    head = me // sharing
    sub = me % sharing
    w_rows = w_query.shape[0]
    w_half = w_rows // 2

    grouped = devices == 16 and groups == 2
    order = arrival_order(me) if grouped else jnp.arange(devices, dtype=jnp.int32)
    where = jnp.concatenate([order, my_group[None].astype(jnp.int32)])

    def gather(block):
        return Rounds(gather_rounds(block) if grouped else gather_whole(block))

    def scatter(make, tie=lambda addends: addends, both_first=False):
        kind = scatter_rounds if grouped else scatter_whole
        return Rounds(kind(make, seq_length, tie, both_first))

    def exchange(values):
        return lax.all_to_all(values, "expert", split_axis=0, concat_axis=0, tiled=True)

    def to_heads(rows):
        blocks = rows.reshape(rows.shape[0], HEADS, HEAD_DIM).transpose(1, 0, 2)
        return jnp.repeat(blocks, sharing, axis=0)

    def my_part(columns, axis):
        if sharing == 1:
            return columns
        return lax.dynamic_slice_in_dim(columns, sub * part, part, axis=axis)

    def by_half(values, axis):
        return jnp.where(my_group == 0, values, jnp.flip(values, axis))

    def dp_start(values):
        return swap(values, "dp", 1) if groups == 2 else lax.psum(values, "dp")

    def dp_end(values, arrived):
        total = arrived.astype(jnp.float32)
        return total + values.astype(jnp.float32) if groups == 2 else total

    waiting = []

    def weight_grad(left, right):
        pieces = left.shape[1] // 256 if grouped else 1
        step = left.shape[1] // pieces
        own = [
            contract_rows(left[:, i * step : (i + 1) * step], right).astype(jnp.bfloat16)
            for i in range(pieces)
        ]
        far = [dp_start(values) for values in own]
        waiting.extend((far, i) for i in range(pieces))
        return own, far

    def cross(*others):
        if not (waiting and grouped):
            return others
        far, i = waiting.pop(0)
        *others, far[i] = together(*others, far[i])
        return others

    def ride(rounds, *others):
        if not (waiting and grouped):
            return rounds.step(*others)
        far, i = waiting.pop(0)
        *others, far[i] = rounds.step(*others, far[i])
        return others

    resid_in = tokens.astype(jnp.float32)
    pre_in, normal_in, inverse_in = norm_rows(resid_in, attn_gain)
    normed_in = pre_in.astype(jnp.bfloat16)

    experts_all = devices * w_gate.shape[0]
    slots = min(row_count, row_count * top_count * 3 // (2 * experts_all))
    hits = routes[:, :, None] == jnp.arange(experts_all, dtype=jnp.int32)[None, None, :]
    gate_table = jnp.sum(jnp.where(hits, route_gates[:, :, None], 0.0), axis=1).T
    gate_high = lax.reduce_precision(gate_table, exponent_bits=8, mantissa_bits=7)
    gate_rows = jnp.pad(
        jnp.stack([gate_high, gate_table - gate_high], axis=1).astype(jnp.bfloat16),
        ((0, 0), (0, 14), (0, 3 * HEAD_DIM - row_count)),
    )
    if grouped:
        take = lambda w: lax.dynamic_slice_in_dim(w, my_group * w_half, w_half)
    else:
        take = lambda w: w
    sent_w = jnp.concatenate([to_heads(take(w)) for w in (w_query, w_key, w_value)], axis=2)
    taken = sent_w.shape[1]
    arrived = exchange(jnp.concatenate([sent_w, gate_rows], axis=1))

    key_seg = jnp.broadcast_to(segments[:, None], (seq_length, HEAD_DIM))
    query_seg = segments[None, :]
    cosine, rope_sine = rope_tables(jnp.arange(seq_length, dtype=jnp.int32))
    gains = jnp.stack(
        [
            lax.dynamic_slice_in_dim(query_gain, head * HEAD_DIM, HEAD_DIM),
            lax.dynamic_slice_in_dim(key_gain, head * HEAD_DIM, HEAD_DIM),
        ],
        axis=1,
    )
    if grouped:
        rounds = gather(jnp.concatenate([normed_in, take(w_out)], axis=0))
        rounds.step()
        rounds.step(key_seg, cosine, rope_sine, gains)
        (arrived,) = rounds.step(arrived)
        head_w = arrived[:, :taken]
        head_w_far = swap(head_w, "dp", 1)
        rounds.step()
        blocks = rounds.finish()
        head_w = by_half(jnp.stack([head_w, head_w_far], axis=1), 1).reshape(width, 3 * HEAD_DIM)
        out_far = swap(tails(blocks[: devices // 2], row_count, w_half), "dp", 1)
    else:
        blocks = gather(normed_in).finish()
        head_w = arrived[:, :taken].reshape(width, 3 * HEAD_DIM)
        out_full = lax.all_gather(w_out, "expert", axis=0, tiled=True)

    gate_pair = arrived[:, taken : taken + 2, :row_count].astype(jnp.float32)
    gate_mine = (gate_pair[:, 0] + gate_pair[:, 1])[order]
    chosen = gate_mine > 0.0
    before = jnp.arange(row_count)[:, None] < jnp.arange(row_count)[None, :]
    rank = mm(chosen.astype(jnp.bfloat16), before.astype(jnp.bfloat16)).astype(jnp.int32)
    rank = jnp.where(chosen, rank, -1)
    slot = jnp.arange(slots, dtype=jnp.int32)
    picks = rank[:, None, :] == slot[None, :, None]
    slot_gate = jnp.sum(jnp.where(picks, gate_mine[:, None, :], 0.0), axis=2).reshape(-1, 1)
    picks = picks.astype(jnp.bfloat16)
    unpicks = (rank[:, :, None] == slot[None, None, :]).astype(jnp.bfloat16)
    ones = jnp.ones_like(slot_gate)
    ff = w_gate.shape[2]
    w_both = jnp.concatenate([w_gate[0], w_up[0]], axis=1)

    cot_rounds = gather(cotangent)
    query_raw, key_raw, value, value_t, squares = heads_in(order, head_w, row_count, blocks)
    if sharing > 1:
        squares = jnp.stack(
            [jnp.sum(jnp.square(my_part(raw, 0)), axis=0) for raw in (query_raw, key_raw)]
        )
    (squares,) = cot_rounds.step(squares)
    squares = butterfly(squares, "expert")
    inverse = lax.rsqrt(squares / width + eps)
    query_t, query, key_t, key, attended, attended_t, log_total = attend(
        query_raw, key_raw, value_t, inverse, gains, cosine, rope_sine, key_seg, query_seg
    )
    if grouped:
        attended, out_far = cot_rounds.step(attended, out_far)
        out_cross = send(out_far, swap_core)

    attended_low = exchange(my_part(attended, 1).reshape(devices, row_count, part))
    if grouped:
        middle, normed_mid = out_project(
            where, attended_low, tokens, ffn_gain[None, :], blocks, out_far, out_cross
        )
    else:
        attended_low = attended_low.transpose(1, 0, 2).reshape(row_count, width)
        middle = resid_in + mm(attended_low, out_full)
        normed_mid = norm_rows(middle, ffn_gain)[0].astype(jnp.bfloat16)
    (normed_mid,) = cot_rounds.step(normed_mid)

    mid_rounds = gather(normed_mid)
    head_w_t = jnp.concatenate(
        [my_part(head_w[:, i * HEAD_DIM : (i + 1) * HEAD_DIM], 1).T for i in range(3)], axis=0
    )
    (head_w_t,) = mid_rounds.step(head_w_t)
    rows_in = pick(picks, ones, mid_rounds.finish())
    (rows_in,) = cot_rounds.step(rows_in)
    grad_eo = pick(picks, slot_gate, cot_rounds.finish())
    gate_up = mm(rows_in, w_both)
    gate_in, up_in = gate_up[:, :ff], gate_up[:, ff:]
    sigmoid_in = jax.nn.sigmoid(gate_in)
    silu_in = gate_in * sigmoid_in
    hidden = (silu_in * up_in).astype(jnp.bfloat16)
    grad_down, down_far = weight_grad(hidden, grad_eo)

    def give_back(produce):
        def some(first, count):
            here = slice(first // row_count, (first + count) // row_count)
            rows = produce(slice(here.start * slots, here.stop * slots))
            return jnp.einsum(
                "bts,bsd->btd",
                unpicks[here],
                rows.astype(jnp.bfloat16).reshape(-1, slots, width),
                preferred_element_type=jnp.bfloat16,
            ).reshape(count, width)

        return some

    hidden_next, grad_eo_next = together(hidden, grad_eo, *grad_down)[:2]
    mix_rounds = scatter(
        give_back(lambda some: mm(hidden_next[some], w_down[0]) * slot_gate[some])
    )
    grad_hidden = contract_cols(grad_eo_next, w_down[0])
    grad_pre = jnp.concatenate(
        [
            (
                grad_hidden * up_in * sigmoid_in * (1.0 + gate_in * (1.0 - sigmoid_in))
            ).astype(jnp.bfloat16),
            (grad_hidden * silu_in).astype(jnp.bfloat16),
        ],
        axis=1,
    )
    (grad_pre,) = ride(mix_rounds, grad_pre)
    row_rounds = scatter(
        give_back(lambda some: contract_cols(grad_pre[some], w_both)),
        lambda addends: ride(mix_rounds, addends)[0],
    )
    grad_both, both_far = weight_grad(rows_in, grad_pre)
    far, i = waiting.pop(0) if grouped else (None, 0)
    if grouped:
        (far[i], *_) = step_all([row_rounds, mix_rounds], far[i], *grad_both[:1])
    else:
        row_rounds.step()
    ride(row_rounds, *mix_rounds.sent, *grad_both[1:2])
    row_rounds.step(*grad_both[2:4])
    ride(row_rounds, *grad_both[4:5])
    ride(row_rounds, *grad_both[5:6])
    grad_normed_mid = row_rounds.finish()

    grad_out = cotangent.astype(jnp.float32)
    _, normal_mid, inverse_mid = norm_rows(middle, ffn_gain)
    mid_back, grad_ffn_gain = norm_back(grad_normed_mid, normal_mid, inverse_mid, ffn_gain)
    grad_middle = grad_out + mid_back
    grad_branch = grad_middle.astype(jnp.bfloat16)
    if grouped:
        grad_columns = out_project_back(where, grad_branch, blocks, out_far, out_cross)
        (grad_columns,) = ride(mix_rounds, grad_columns)
    else:
        grad_columns = to_heads(contract_cols(grad_branch, out_full).astype(jnp.bfloat16))
    grad_attended = exchange(grad_columns).reshape(seq_length, HEAD_DIM)
    if groups == 2:
        (down_total,) = merge(grad_down, down_far, 1)
        grad_attended, down_total, *_ = cross(grad_attended, down_total, *grad_both[6:])
    else:
        down_total = down_far[0].astype(jnp.float32)
    mixed = mix_rounds.finish()
    activations = (middle + mixed).astype(jnp.bfloat16)
    branch_all = lax.all_gather(
        after(grad_branch, grad_attended), "expert", axis=0, tiled=True
    )

    weighted_query, weighted_key, grad_value_t, inner_query, inner_key, gain_sums = attend_back(
        key_seg,
        query_seg,
        log_total,
        query_t,
        query,
        grad_attended,
        key,
        key_t,
        value,
        query_raw,
        key_raw,
        inverse,
        gains,
        cosine,
        rope_sine,
    )
    inner = jnp.concatenate([inner_query, inner_key], axis=0)
    if sharing > 1:
        inner = jnp.stack(
            [
                jnp.sum(my_part(weighted * raw * at, 0), axis=0)
                for weighted, raw, at in (
                    (weighted_query, query_raw, inverse[0:1]),
                    (weighted_key, key_raw, inverse[1:2]),
                )
            ]
        )
    (inner,) = cross(inner)
    inner = butterfly(inner, "expert") / width
    grad_raw_t = jnp.concatenate(
        [
            my_part(
                (at * (weighted - raw * at * mean)).astype(jnp.bfloat16),
                0,
            )
            for weighted, raw, at, mean in (
                (weighted_query, query_raw, inverse[0:1], inner[0:1]),
                (weighted_key, key_raw, inverse[1:2], inner[1:2]),
            )
        ]
        + [my_part(grad_value_t, 0)],
        axis=0,
    )
    in_rounds = scatter(
        lambda first, count: project(order, grad_raw_t, head_w_t, row_count, first, count),
        both_first=True,
    )
    (grad_raw_t,) = in_rounds.step(grad_raw_t)
    grad_w_t = stack_product(order, grad_raw_t, row_count, blocks)
    grad_attn_gain = jnp.sum(grad_w_t * head_w_t.astype(jnp.float32), axis=0) / attn_gain
    (grad_w_t,) = ride(in_rounds, grad_w_t)
    w_columns = exchange(
        grad_w_t.astype(jnp.bfloat16).reshape(3 * part, devices, w_rows).transpose(1, 0, 2)
    )

    def placed(values):
        return lax.dynamic_update_slice_in_dim(
            jnp.zeros((width,), jnp.float32), values, me * part, 0
        )

    gain_parts = jnp.stack(
        [
            grad_attn_gain,
            placed(my_part(gain_sums[:, 0], 0)),
            placed(my_part(gain_sums[:, 1], 0)),
            grad_ffn_gain,
        ]
    )
    out_part = mm(my_part(attended_t, 0), branch_all).astype(jnp.bfloat16)
    out_part, w_columns = ride(in_rounds, out_part, w_columns)
    out_part_far = dp_start(out_part)
    dense = [
        w_columns[:, i * part : (i + 1) * part].reshape(width, w_rows).T for i in range(3)
    ]
    if groups == 2:
        both_total = list(merge(grad_both[:4], both_far[:4], 2, len(grad_both)))
        gain_parts, both_total[0], both_total[1], *dense = ride(
            in_rounds, gain_parts, *both_total, *dense
        )
        both_total = merge(grad_both[4:], both_far[4:], 2, 4, both_total)
    else:
        in_rounds.step()
        both_total = both_far[0].astype(jnp.float32)
        both_total = (both_total[:, :ff], both_total[:, ff:])
    dense_far = [dp_start(values) for values in dense]
    out_part_far, dense_far[0], *both_total = in_rounds.step(
        out_part_far, dense_far[0], *both_total
    )
    gate_total, up_total = both_total
    grad_normed_in = in_rounds.finish()
    grad_normed_in, gain_parts = together(grad_normed_in, gain_parts)
    gain_parts = butterfly(gain_parts, "expert")
    gain_parts, dense_far[2], gate_total = together(gain_parts, dense_far[2], gate_total)
    gain_total = butterfly(gain_parts, "dp")
    in_back, _ = norm_back(grad_normed_in, normal_in, inverse_in, attn_gain)
    input_grad = (grad_middle + in_back).astype(jnp.bfloat16)

    return (
        activations,
        input_grad,
        gain_total[0],
        gain_total[1],
        gain_total[2],
        gain_total[3],
        dp_end(dense[0], dense_far[0]),
        dp_end(dense[1], dense_far[1]),
        dp_end(dense[2], dense_far[2]),
        dp_end(out_part, out_part_far),
        gate_total[None],
        up_total[None],
        down_total[None],
    )


def solution(mesh):
    in_specs = (
        P(("dp", "expert"), None),
        P("dp"),
        P(("dp", "expert"), None),
        P(("dp", "expert"), None),
        P(),
        P(),
        P(),
        P(),
        P("expert", None),
        P("expert", None),
        P("expert", None),
        P("expert", None),
        P("expert", None, None),
        P("expert", None, None),
        P("expert", None, None),
        P(("dp", "expert"), None),
    )
    out_specs = (
        P(("dp", "expert"), None),
        P(("dp", "expert"), None),
        P(),
        P(),
        P(),
        P(),
        P("expert", None),
        P("expert", None),
        P("expert", None),
        P("expert", None),
        P("expert", None, None),
        P("expert", None, None),
        P("expert", None, None),
    )
    return jax.shard_map(local, mesh=mesh, in_specs=in_specs, out_specs=out_specs, check_vma=False)
```

```python
import functools

import jax
import jax.numpy as jnp
from jax import lax
from jax.experimental import pallas as pl
from jax.experimental.pallas import tpu as pltpu
from jax.sharding import PartitionSpec as P

HEADS = 16
HEAD_DIM = 128


eps = 1e-05
rope_base = 50000.0
negative = -1e30
score_scale = HEAD_DIM ** (-0.5)
query_block = 256


def norm_rows(values, norm_gain):
    inverse = lax.rsqrt(jnp.mean(values * values, axis=-1, keepdims=True) + eps)
    normal = values * inverse
    return (normal * norm_gain, normal, inverse)


def norm_back(upstream, normal, inverse, norm_gain):
    weighted = upstream * norm_gain
    inner_mean = jnp.mean(weighted * normal, axis=-1, keepdims=True)
    return (inverse * (weighted - normal * inner_mean), jnp.sum(upstream * normal, axis=0))


def rope_tables(positions):
    half_dim = HEAD_DIM // 2
    frequency = rope_base ** (-(jnp.arange(half_dim, dtype=jnp.float32) * 2.0 / HEAD_DIM))
    theta = frequency[:, None] * positions.astype(jnp.float32)[None, :]
    return (jnp.cos(theta), jnp.sin(theta))


def mm(left, right):
    return jnp.dot(left, right, preferred_element_type=jnp.float32)


def contract_rows(left, right):
    return lax.dot_general(
        left, right, (((0,), (0,)), ((), ())), preferred_element_type=jnp.float32
    )


def contract_cols(left, right):
    return lax.dot_general(
        left, right, (((1,), (1,)), ((), ())), preferred_element_type=jnp.float32
    )


def swap(values, axis, step):
    count = lax.axis_size(axis)
    return lax.ppermute(values, axis, [(i, i ^ step) for i in range(count)])


def together(*values):
    return lax.optimization_barrier(values)


def after(values, *others):
    return lax.optimization_barrier((values,) + others)[0]


def butterfly(values, axis):
    step = 1
    while step < lax.axis_size(axis):
        if 2 * step < lax.axis_size(axis):
            one, two, three = [swap(values, axis, times * step) for times in (1, 2, 3)]
            values = (values + one) + (two + three)
            step *= 4
        else:
            values = values + swap(values, axis, step)
            step *= 2
    return values


near_order = ((0, 1, 2, 3), (1, 0, 2, 3), (2, 3, 1, 0), (3, 2, 1, 0))


def moves(target):
    pairs = []
    for index in range(16):
        far = target(index // 4)
        if far is not None:
            pairs.append((index, far * 4 + index % 4))
    return pairs


swap_near = moves(lambda z: z ^ 1)
swap_middle = moves(lambda z: {1: 2, 2: 1}.get(z))
move_out = moves(lambda z: {1: 0, 2: 3}.get(z))
move_in = moves(lambda z: {0: 1, 3: 2}.get(z))
swap_row = [(i, i ^ 2) for i in range(16)]
swap_core = [(i, i ^ 1) for i in range(16)]


def send(values, pairs):
    return lax.ppermute(values, "expert", pairs)


def arrival_order(me):
    near = jnp.asarray(near_order, jnp.int32)[me // 4] * 4
    row, core = (me // 2) % 2, me % 2
    return jnp.concatenate(
        [near + (row ^ j) * 2 + (core ^ i) for i in (0, 1) for j in (0, 1)]
    ).astype(jnp.int32)


class Rounds:
    def __init__(self, steps):
        self.steps = steps
        self.result = None
        self.over = False
        self.sent = ()
        self._go(None)

    def _go(self, arrived):
        try:
            self.sent = self.steps.send(arrived)
        except StopIteration as stop:
            self.result, self.sent, self.over = stop.value, (), True

    def step(self, *others):
        return step_all([self], *others)

    def finish(self):
        while not self.over:
            self.step()
        return self.result


def step_all(rounds, *others):
    sent = [values for one in rounds for values in one.sent]
    values = together(*sent, *others) if sent or others else ()
    at = 0
    for one in rounds:
        count = len(one.sent)
        if not one.over:
            one._go(values[at : at + count])
        at += count
    return values[at:]


def gather_rounds(block):
    at = lax.axis_index("expert") // 4
    outer = (at == 0) | (at == 3)
    first, second, row = yield (
        send(block, swap_near),
        send(block, swap_middle),
        send(block, swap_row),
    )
    third, second_out, row_first, core = yield (
        send(first, swap_middle),
        send(second, move_out),
        send(first, swap_row),
        send(block, swap_core),
    )
    second = jnp.where(outer, second_out, second)
    third_out, row_second, core_first, core_row = yield (
        send(third, move_out),
        send(second, swap_row),
        send(first, swap_core),
        send(row, swap_core),
    )
    third = jnp.where(outer, third_out, third)
    row_third, core_second, core_third, core_row_first, core_row_second = yield (
        send(third, swap_row),
        send(second, swap_core),
        send(third, swap_core),
        send(row_first, swap_core),
        send(row_second, swap_core),
    )
    (core_row_third,) = yield (send(row_third, swap_core),)
    return [
        block,
        first,
        second,
        third,
        row,
        row_first,
        row_second,
        row_third,
        core,
        core_first,
        core_second,
        core_third,
        core_row,
        core_row_first,
        core_row_second,
        core_row_third,
    ]


def gather_whole(block):
    yield ()
    return list(lax.all_gather(block, "expert", axis=0))


def add_low(left, right):
    return (left.astype(jnp.float32) + right.astype(jnp.float32)).astype(jnp.bfloat16)


def scatter_rounds(make, count, tie, both_first):
    far = send(tie(make(count // 2, count // 2)), swap_core)
    if both_first:
        far, close = yield (far, make(0, count // 2))
    else:
        (far,) = yield (far,)
        close = make(0, count // 2)
    rows = count // 16

    def both(j, k):
        here = slice((j * 4 + k) * rows, (j * 4 + k + 1) * rows)
        return add_low(close[here], far[here])

    (row,) = yield (send(both(1, 3), swap_row),)
    third = add_low(both(0, 3), row)
    row, third_in = yield (send(both(1, 2), swap_row), send(third, move_in))
    second = add_low(both(0, 2), row)
    third = add_low(third, third_in)
    row, second_in, third_in = yield (
        send(both(1, 1), swap_row),
        send(second, move_in),
        send(third, swap_middle),
    )
    first = add_low(add_low(both(0, 1), row), third_in)
    second = add_low(second, second_in)
    row, second_in, first_in = yield (
        send(both(1, 0), swap_row),
        send(second, swap_middle),
        send(first, swap_near),
    )
    return (
        both(0, 0).astype(jnp.float32)
        + row.astype(jnp.float32)
        + second_in.astype(jnp.float32)
        + first_in.astype(jnp.float32)
    )


def scatter_whole(make, count, tie, both_first):
    yield ()
    return lax.psum_scatter(
        tie(make(0, count)), "expert", scatter_dimension=0, tiled=True
    ).astype(jnp.float32)


def pick_kernel(picks, scale, *refs):
    *blocks, out = refs
    slots = picks.shape[1]
    for index, block in enumerate(blocks):
        here = slice(index * slots, (index + 1) * slots)
        out[here, :] = (mm(picks[index], block[...]) * scale[here, :]).astype(out.dtype)


def pick(picks, scale, blocks):
    count, slots, tokens = picks.shape
    width = blocks[0].shape[1]
    return pl.pallas_call(
        pick_kernel,
        out_shape=jax.ShapeDtypeStruct((count * slots, width), jnp.bfloat16),
        cost_estimate=pl.CostEstimate(
            flops=2 * count * tokens * slots * width,
            bytes_accessed=2 * count * (tokens + slots) * width,
            transcendentals=0,
        ),
        name="pick",
    )(picks, scale, *blocks)


def merge_kernel(count, parts, *refs):
    pairs, outs = refs[: 2 * count], refs[-parts:]
    width = outs[0].shape[1]
    for index in range(count):

        @pl.when(pl.program_id(0) == index)
        def _():
            total = pairs[index][...].astype(jnp.float32) + pairs[count + index][...].astype(
                jnp.float32
            )
            for i, out in enumerate(outs):
                out[...] = total[:, i * width : (i + 1) * width]


def merge(own, far, parts, pieces=None, before=None):
    count = len(own)
    begin = pieces if before else 0
    before = before or []
    pieces = begin + count if before else pieces or count
    rows, width = own[0].shape
    return pl.pallas_call(
        functools.partial(merge_kernel, count, parts),
        grid=(count,),
        in_specs=[pl.BlockSpec((rows, width), lambda i: (0, 0))] * (2 * count)
        + [pl.BlockSpec(memory_space=pl.ANY)] * len(before),
        out_specs=[pl.BlockSpec((rows, width // parts), lambda i: (begin + i, 0))] * parts,
        out_shape=[jax.ShapeDtypeStruct((pieces * rows, width // parts), jnp.float32)] * parts,
        input_output_aliases={2 * count + i: i for i in range(len(before))},
        cost_estimate=pl.CostEstimate(
            flops=count * rows * width,
            bytes_accessed=8 * count * rows * width,
            transcendentals=0,
        ),
        compiler_params=pltpu.CompilerParams(vmem_limit_bytes=28 * 2**20),
        name="merge",
    )(*own, *far, *before)


def project_kernel(order, left_t, left_next_t, right, out):
    left = jnp.concatenate([left_t[...].T, left_next_t[...].T], axis=0)
    out[...] = mm(left, right[...]).astype(out.dtype)


def project(order, left_t, right, rows, first, count):
    depth, width = right.shape
    begin = first // rows
    return pl.pallas_call(
        project_kernel,
        grid_spec=pltpu.PrefetchScalarGridSpec(
            num_scalar_prefetch=1,
            grid=(count // (2 * rows),),
            in_specs=[
                pl.BlockSpec((depth, rows), lambda i, order: (0, order[begin + 2 * i])),
                pl.BlockSpec((depth, rows), lambda i, order: (0, order[begin + 2 * i + 1])),
                pl.BlockSpec((depth, width), lambda i, order: (0, 0)),
            ],
            out_specs=pl.BlockSpec((2 * rows, width), lambda i, order: (i, 0)),
        ),
        out_shape=jax.ShapeDtypeStruct((count, width), jnp.bfloat16),
        cost_estimate=pl.CostEstimate(
            flops=2 * count * depth * width,
            bytes_accessed=2 * (count * (depth + width) + depth * width),
            transcendentals=0,
        ),
        compiler_params=pltpu.CompilerParams(vmem_limit_bytes=28 * 2**20),
        name="project",
    )(order, left_t, left_t, right)


scalars = pl.BlockSpec(memory_space=pltpu.SMEM)
vectors = pl.BlockSpec(memory_space=pltpu.VMEM)


def lanes(order, index, rows):
    return pl.ds(pl.multiple_of(order[index] * rows, rows), rows)


def stack_kernel(rows, order, left_t, *refs):
    *blocks, out = refs
    for index in range(0, len(blocks), 4):
        four = range(index, index + 4)
        left = jnp.concatenate([left_t[:, lanes(order, i, rows)] for i in four], axis=1)
        right = jnp.concatenate([blocks[i][:rows] for i in four], axis=0)
        term = mm(left, right)
        if index == 0:
            out[...] = term
        else:
            out[...] += term


def stack_product(order, left_t, rows, blocks):
    width = blocks[0].shape[1]
    return pl.pallas_call(
        functools.partial(stack_kernel, rows),
        in_specs=[scalars, vectors] + [vectors] * len(blocks),
        out_specs=vectors,
        out_shape=jax.ShapeDtypeStruct((left_t.shape[0], width), jnp.float32),
        cost_estimate=pl.CostEstimate(
            flops=2 * left_t.size * width,
            bytes_accessed=2 * len(blocks) * rows * width,
            transcendentals=0,
        ),
        compiler_params=pltpu.CompilerParams(vmem_limit_bytes=28 * 2**20),
        name="stack_product",
    )(order, left_t, *blocks)


def heads_kernel(rows, order, weight, *refs):
    *blocks, query_t, key_t, value, value_t, squares = refs
    for index in range(0, len(blocks), 4):
        four = range(index, index + 4)
        raw = mm(jnp.concatenate([blocks[i][:rows] for i in four], axis=0), weight[...])
        for i in four:
            own = raw[(i - index) * rows : (i - index + 1) * rows]
            here = lanes(order, i, rows)
            query = own[:, :HEAD_DIM].T
            key = own[:, HEAD_DIM : 2 * HEAD_DIM].T
            query_t[:, here] = query
            key_t[:, here] = key
            value[here, :] = own[:, 2 * HEAD_DIM :].astype(value.dtype)
            value_t[:, here] = own[:, 2 * HEAD_DIM :].T.astype(value.dtype)
            squares[0:1, here] = jnp.sum(query * query, axis=0, keepdims=True)
            squares[1:2, here] = jnp.sum(key * key, axis=0, keepdims=True)


def heads_in(order, weight, rows, blocks):
    width = blocks[0].shape[1]
    count = len(blocks) * rows
    return pl.pallas_call(
        functools.partial(heads_kernel, rows),
        in_specs=[scalars, vectors] + [vectors] * len(blocks),
        out_specs=[vectors] * 5,
        out_shape=[
            jax.ShapeDtypeStruct((HEAD_DIM, count), jnp.float32),
            jax.ShapeDtypeStruct((HEAD_DIM, count), jnp.float32),
            jax.ShapeDtypeStruct((count, HEAD_DIM), jnp.bfloat16),
            jax.ShapeDtypeStruct((HEAD_DIM, count), jnp.bfloat16),
            jax.ShapeDtypeStruct((2, count), jnp.float32),
        ],
        cost_estimate=pl.CostEstimate(
            flops=2 * count * width * 3 * HEAD_DIM,
            bytes_accessed=2 * count * width,
            transcendentals=0,
        ),
        name="heads_in",
    )(order, weight, *blocks)


def tail_kernel(*refs):
    *blocks, out = refs
    rows = blocks[0].shape[0]
    for index, block in enumerate(blocks):
        out[index * rows : (index + 1) * rows, :] = block[...]


def tail_specs(blocks, rows, tail):
    width = blocks[0].shape[1]
    return [pl.BlockSpec((tail, width), lambda i: (rows // tail, 0))] * len(blocks)


def tails(blocks, rows, tail):
    width = blocks[0].shape[1]
    return pl.pallas_call(
        tail_kernel,
        grid=(1,),
        in_specs=tail_specs(blocks, rows, tail),
        out_specs=pl.BlockSpec((len(blocks) * tail, width), lambda i: (0, 0)),
        out_shape=jax.ShapeDtypeStruct((len(blocks) * tail, width), jnp.bfloat16),
        name="tails",
    )(*blocks)


def four(refs, index):
    return jnp.concatenate([ref[...] for ref in refs[index : index + 4]], axis=0)


def far_four(far, cross, index):
    rows = far.shape[0] // 2
    ref, at = (far, index // 4) if index < 8 else (cross, index // 4 - 2)
    return ref[at * rows : (at + 1) * rows, :]


def out_kernel(where, attended, resid, gain, *refs):
    *near, far, cross, middle, normed = refs
    count = len(near)
    half = HEAD_DIM // 2
    first_group = where[count] == 0
    total = resid[...].astype(jnp.float32)
    for index in range(0, count, 4):
        near_left, far_left = [], []
        for i in range(index, index + 4):
            columns = attended[where[i]].astype(jnp.float32)
            low, high = columns[:, :half], columns[:, half:]
            near_left.append(jnp.where(first_group, low, high))
            far_left.append(jnp.where(first_group, high, low))
        total += mm(jnp.concatenate(near_left, axis=1).astype(jnp.bfloat16), four(near, index))
        total += mm(
            jnp.concatenate(far_left, axis=1).astype(jnp.bfloat16), far_four(far, cross, index)
        )
    middle[...] = total
    inverse = lax.rsqrt(jnp.mean(total * total, axis=-1, keepdims=True) + eps)
    normed[...] = (total * inverse * gain[...]).astype(normed.dtype)


def whole_specs(*arrays):
    return [pl.BlockSpec(array.shape, lambda i, rank=array.ndim: (0,) * rank) for array in arrays]


def out_project(where, attended, resid, gain, blocks, far, cross):
    rows, width = resid.shape
    tail = blocks[0].shape[0] - rows
    return pl.pallas_call(
        out_kernel,
        grid=(1,),
        in_specs=[scalars]
        + whole_specs(attended, resid, gain)
        + tail_specs(blocks, rows, tail)
        + whole_specs(far, cross),
        out_specs=whole_specs(resid, resid),
        out_shape=[
            jax.ShapeDtypeStruct((rows, width), jnp.float32),
            jax.ShapeDtypeStruct((rows, width), jnp.bfloat16),
        ],
        cost_estimate=pl.CostEstimate(
            flops=2 * rows * width * width,
            bytes_accessed=2 * width * width,
            transcendentals=0,
        ),
        name="out_project",
    )(where, attended, resid, gain, *blocks, far, cross)


def out_back_kernel(where, branch, *refs):
    *near_refs, far_ref, cross, out = refs
    count = len(near_refs)
    half = HEAD_DIM // 2
    first_group = where[count] == 0
    for index in range(0, count, 4):
        near = contract_cols(branch[...], four(near_refs, index))
        far = contract_cols(branch[...], far_four(far_ref, cross, index))
        for i in range(index, index + 4):
            here = slice((i - index) * half, (i - index + 1) * half)
            low = jnp.where(first_group, near[:, here], far[:, here])
            high = jnp.where(first_group, far[:, here], near[:, here])
            out[where[i]] = jnp.concatenate([low, high], axis=1).astype(out.dtype)


def out_project_back(where, branch, blocks, far, cross):
    rows, width = branch.shape
    tail = blocks[0].shape[0] - rows
    shape = (len(blocks), rows, HEAD_DIM)
    return pl.pallas_call(
        out_back_kernel,
        grid=(1,),
        in_specs=[scalars]
        + whole_specs(branch)
        + tail_specs(blocks, rows, tail)
        + whole_specs(far, cross),
        out_specs=pl.BlockSpec(shape, lambda i: (0, 0, 0)),
        out_shape=jax.ShapeDtypeStruct(shape, jnp.bfloat16),
        cost_estimate=pl.CostEstimate(
            flops=2 * rows * width * width,
            bytes_accessed=2 * width * width,
            transcendentals=0,
        ),
        name="out_project_back",
    )(where, branch, *blocks, far, cross)


def turn(values, cosine, rope_sine):
    half = HEAD_DIM // 2
    first, second = values[:half], values[half:]
    return jnp.concatenate(
        [first * cosine - second * rope_sine, second * cosine + first * rope_sine], axis=0
    )


def attend_kernel(
    query_raw,
    key_raw,
    value_t,
    inverse,
    inverse_all,
    gains,
    cosine,
    rope_sine,
    cosine_all,
    rope_sine_all,
    key_seg,
    query_seg,
    query_t,
    query,
    key_t,
    key,
    out,
    out_t,
    log_total,
):
    @pl.when(pl.program_id(0) == 0)
    def _():
        turned = turn(
            key_raw[...] * inverse_all[1:2, :] * gains[:, 1:2], cosine_all[...], rope_sine_all[...]
        ).astype(jnp.bfloat16)
        key_t[...] = turned
        key[...] = turned.T

    turned = turn(
        query_raw[...] * inverse[0:1, :] * gains[:, 0:1], cosine[...], rope_sine[...]
    ).astype(jnp.bfloat16)
    query_t[...] = turned
    query[...] = turned.T
    scores = mm(key[...], turned) * score_scale
    scores = jnp.where(key_seg[:, :1] == query_seg[...], scores, negative)
    peak = jnp.max(scores, axis=0, keepdims=True)
    weights = jnp.exp(scores - peak)
    total = jnp.sum(weights, axis=0, keepdims=True)
    result = mm(value_t[...], weights.astype(jnp.bfloat16)) / total
    out_t[...] = result.astype(out_t.dtype)
    out[...] = result.T.astype(out.dtype)
    log_total[...] = peak + jnp.log(total)


def attend(query_raw, key_raw, value_t, inverse, gains, cosine, rope_sine, key_seg, query_seg):
    count = query_raw.shape[1]
    whole = lambda i: (0, 0)
    across = lambda rows: pl.BlockSpec((rows, query_block), lambda i: (0, i))
    down = pl.BlockSpec((query_block, HEAD_DIM), lambda i: (i, 0))
    all_of = lambda rows: pl.BlockSpec((rows, count), whole)
    low, half = jnp.bfloat16, HEAD_DIM // 2
    return pl.pallas_call(
        attend_kernel,
        grid=(count // query_block,),
        in_specs=[
            across(HEAD_DIM),
            all_of(HEAD_DIM),
            all_of(HEAD_DIM),
            across(2),
            all_of(2),
            pl.BlockSpec((HEAD_DIM, 2), whole),
            across(half),
            across(half),
            all_of(half),
            all_of(half),
            pl.BlockSpec((count, HEAD_DIM), whole),
            across(1),
        ],
        out_specs=[
            across(HEAD_DIM),
            down,
            all_of(HEAD_DIM),
            pl.BlockSpec((count, HEAD_DIM), whole),
            down,
            across(HEAD_DIM),
            across(1),
        ],
        out_shape=[
            jax.ShapeDtypeStruct((HEAD_DIM, count), low),
            jax.ShapeDtypeStruct((count, HEAD_DIM), low),
            jax.ShapeDtypeStruct((HEAD_DIM, count), low),
            jax.ShapeDtypeStruct((count, HEAD_DIM), low),
            jax.ShapeDtypeStruct((count, HEAD_DIM), low),
            jax.ShapeDtypeStruct((HEAD_DIM, count), low),
            jax.ShapeDtypeStruct((1, count), jnp.float32),
        ],
        cost_estimate=pl.CostEstimate(
            flops=4 * count * count * HEAD_DIM,
            bytes_accessed=count * HEAD_DIM * 24,
            transcendentals=count * count,
        ),
        name="attend",
    )(
        query_raw,
        key_raw,
        value_t,
        inverse,
        inverse,
        gains,
        cosine,
        rope_sine,
        cosine,
        rope_sine,
        key_seg,
        query_seg,
    )


def attend_back_kernel(
    key_seg,
    query_seg,
    log_total,
    query_t,
    query,
    upstream,
    key,
    key_t,
    value,
    query_raw,
    key_raw,
    inverse,
    inverse_all,
    gains,
    cosine,
    rope_sine,
    cosine_all,
    rope_sine_all,
    weighted_query,
    weighted_key,
    dvalue_t,
    inner_query,
    inner_key,
    gain_sums,
    dkey,
    dvalue,
):
    step = pl.program_id(0)

    @pl.when(step == 0)
    def _():
        dkey[...] = jnp.zeros_like(dkey)
        dvalue[...] = jnp.zeros_like(dvalue)
        gain_sums[...] = jnp.zeros_like(gain_sums)

    scores = mm(key[...], query_t[...]) * score_scale
    probs = jnp.where(key_seg[:, :1] == query_seg[...], jnp.exp(scores - log_total[...]), 0.0)
    dvalue[...] += mm(probs.astype(jnp.bfloat16), upstream[...])
    dprobs = contract_cols(value[...], upstream[...])
    delta = jnp.sum(probs * dprobs, axis=0, keepdims=True)
    dscores = (probs * (dprobs - delta)).astype(jnp.bfloat16)
    dkey[...] += mm(dscores, query[...])
    turned = turn(mm(key_t[...], dscores) * score_scale, cosine[...], -rope_sine[...])
    product = turned * (query_raw[...] * inverse[0:1, :])
    weighted_query[...] = turned * gains[:, 0:1]
    inner_query[...] = jnp.sum(product * gains[:, 0:1], axis=0, keepdims=True)
    gain_sums[:, 0:1] += jnp.sum(product, axis=1, keepdims=True)

    @pl.when(step == pl.num_programs(0) - 1)
    def _():
        turned = turn(dkey[...].T * score_scale, cosine_all[...], -rope_sine_all[...])
        product = turned * (key_raw[...] * inverse_all[1:2, :])
        weighted_key[...] = turned * gains[:, 1:2]
        inner_key[...] = jnp.sum(product * gains[:, 1:2], axis=0, keepdims=True)
        gain_sums[:, 1:2] = jnp.sum(product, axis=1, keepdims=True)
        dvalue_t[...] = dvalue[...].T.astype(dvalue_t.dtype)


def attend_back(
    key_seg,
    query_seg,
    log_total,
    query_t,
    query,
    upstream,
    key,
    key_t,
    value,
    query_raw,
    key_raw,
    inverse,
    gains,
    cosine,
    rope_sine,
):
    count = query.shape[0]
    whole = lambda i: (0, 0)
    across = lambda rows: pl.BlockSpec((rows, query_block), lambda i: (0, i))
    down = pl.BlockSpec((query_block, HEAD_DIM), lambda i: (i, 0))
    all_of = lambda rows: pl.BlockSpec((rows, count), whole)
    tall = pl.BlockSpec((count, HEAD_DIM), whole)
    half = HEAD_DIM // 2
    return pl.pallas_call(
        attend_back_kernel,
        grid=(count // query_block,),
        in_specs=[
            tall,
            across(1),
            across(1),
            across(HEAD_DIM),
            down,
            down,
            tall,
            all_of(HEAD_DIM),
            tall,
            across(HEAD_DIM),
            all_of(HEAD_DIM),
            across(2),
            all_of(2),
            pl.BlockSpec((HEAD_DIM, 2), whole),
            across(half),
            across(half),
            all_of(half),
            all_of(half),
        ],
        out_specs=[
            across(HEAD_DIM),
            all_of(HEAD_DIM),
            all_of(HEAD_DIM),
            across(1),
            all_of(1),
            pl.BlockSpec((HEAD_DIM, 2), whole),
        ],
        out_shape=[
            jax.ShapeDtypeStruct((HEAD_DIM, count), jnp.float32),
            jax.ShapeDtypeStruct((HEAD_DIM, count), jnp.float32),
            jax.ShapeDtypeStruct((HEAD_DIM, count), jnp.bfloat16),
            jax.ShapeDtypeStruct((1, count), jnp.float32),
            jax.ShapeDtypeStruct((1, count), jnp.float32),
            jax.ShapeDtypeStruct((HEAD_DIM, 2), jnp.float32),
        ],
        scratch_shapes=[
            pltpu.VMEM((count, HEAD_DIM), jnp.float32),
            pltpu.VMEM((count, HEAD_DIM), jnp.float32),
        ],
        cost_estimate=pl.CostEstimate(
            flops=10 * count * count * HEAD_DIM,
            bytes_accessed=count * HEAD_DIM * 40,
            transcendentals=count * count,
        ),
        name="attend_back",
    )(
        key_seg,
        query_seg,
        log_total,
        query_t,
        query,
        upstream,
        key,
        key_t,
        value,
        query_raw,
        key_raw,
        inverse,
        inverse,
        gains,
        cosine,
        rope_sine,
        cosine,
        rope_sine,
    )


def local(
    tokens,
    segments,
    routes,
    route_gates,
    attn_gain,
    query_gain,
    key_gain,
    ffn_gain,
    w_query,
    w_key,
    w_value,
    w_out,
    w_gate,
    w_up,
    w_down,
    cotangent,
):
    row_count, width = tokens.shape
    top_count = routes.shape[1]
    devices = lax.axis_size("expert")
    groups = lax.axis_size("dp")
    me = lax.axis_index("expert")
    my_group = lax.axis_index("dp")
    seq_length = row_count * devices
    part = width // devices
    sharing = HEAD_DIM // part
    head = me // sharing
    sub = me % sharing
    w_rows = w_query.shape[0]
    w_half = w_rows // 2

    grouped = devices == 16 and groups == 2
    order = arrival_order(me) if grouped else jnp.arange(devices, dtype=jnp.int32)
    where = jnp.concatenate([order, my_group[None].astype(jnp.int32)])

    def gather(block):
        return Rounds(gather_rounds(block) if grouped else gather_whole(block))

    def scatter(make, tie=lambda addends: addends, both_first=False):
        kind = scatter_rounds if grouped else scatter_whole
        return Rounds(kind(make, seq_length, tie, both_first))

    def exchange(values):
        return lax.all_to_all(values, "expert", split_axis=0, concat_axis=0, tiled=True)

    def to_heads(rows):
        blocks = rows.reshape(rows.shape[0], HEADS, HEAD_DIM).transpose(1, 0, 2)
        return jnp.repeat(blocks, sharing, axis=0)

    def my_part(columns, axis):
        if sharing == 1:
            return columns
        return lax.dynamic_slice_in_dim(columns, sub * part, part, axis=axis)

    def by_half(values, axis):
        return jnp.where(my_group == 0, values, jnp.flip(values, axis))

    def dp_start(values):
        return swap(values, "dp", 1) if groups == 2 else lax.psum(values, "dp")

    def dp_end(values, arrived):
        total = arrived.astype(jnp.float32)
        return total + values.astype(jnp.float32) if groups == 2 else total

    waiting = []

    def weight_grad(left, right):
        pieces = left.shape[1] // 256 if grouped else 1
        step = left.shape[1] // pieces
        own = [
            contract_rows(left[:, i * step : (i + 1) * step], right).astype(jnp.bfloat16)
            for i in range(pieces)
        ]
        far = [dp_start(values) for values in own]
        waiting.extend((far, i) for i in range(pieces))
        return own, far

    def cross(*others):
        if not (waiting and grouped):
            return others
        far, i = waiting.pop(0)
        *others, far[i] = together(*others, far[i])
        return others

    def ride(rounds, *others):
        if not (waiting and grouped):
            return rounds.step(*others)
        far, i = waiting.pop(0)
        *others, far[i] = rounds.step(*others, far[i])
        return others

    resid_in = tokens.astype(jnp.float32)
    pre_in, normal_in, inverse_in = norm_rows(resid_in, attn_gain)
    normed_in = pre_in.astype(jnp.bfloat16)

    experts_all = devices * w_gate.shape[0]
    slots = min(row_count, row_count * top_count * 3 // (2 * experts_all))
    hits = routes[:, :, None] == jnp.arange(experts_all, dtype=jnp.int32)[None, None, :]
    gate_table = jnp.sum(jnp.where(hits, route_gates[:, :, None], 0.0), axis=1).T
    gate_high = lax.reduce_precision(gate_table, exponent_bits=8, mantissa_bits=7)
    gate_rows = jnp.pad(
        jnp.stack([gate_high, gate_table - gate_high], axis=1).astype(jnp.bfloat16),
        ((0, 0), (0, 14), (0, 3 * HEAD_DIM - row_count)),
    )
    if grouped:
        take = lambda w: lax.dynamic_slice_in_dim(w, my_group * w_half, w_half)
    else:
        take = lambda w: w
    sent_w = jnp.concatenate([to_heads(take(w)) for w in (w_query, w_key, w_value)], axis=2)
    taken = sent_w.shape[1]
    arrived = exchange(jnp.concatenate([sent_w, gate_rows], axis=1))

    key_seg = jnp.broadcast_to(segments[:, None], (seq_length, HEAD_DIM))
    query_seg = segments[None, :]
    cosine, rope_sine = rope_tables(jnp.arange(seq_length, dtype=jnp.int32))
    gains = jnp.stack(
        [
            lax.dynamic_slice_in_dim(query_gain, head * HEAD_DIM, HEAD_DIM),
            lax.dynamic_slice_in_dim(key_gain, head * HEAD_DIM, HEAD_DIM),
        ],
        axis=1,
    )
    if grouped:
        rounds = gather(jnp.concatenate([normed_in, take(w_out)], axis=0))
        rounds.step()
        rounds.step(key_seg, cosine, rope_sine, gains)
        (arrived,) = rounds.step(arrived)
        head_w = arrived[:, :taken]
        head_w_far = swap(head_w, "dp", 1)
        rounds.step()
        blocks = rounds.finish()
        head_w = by_half(jnp.stack([head_w, head_w_far], axis=1), 1).reshape(width, 3 * HEAD_DIM)
        out_far = swap(tails(blocks[: devices // 2], row_count, w_half), "dp", 1)
    else:
        blocks = gather(normed_in).finish()
        head_w = arrived[:, :taken].reshape(width, 3 * HEAD_DIM)
        out_full = lax.all_gather(w_out, "expert", axis=0, tiled=True)

    gate_pair = arrived[:, taken : taken + 2, :row_count].astype(jnp.float32)
    gate_mine = (gate_pair[:, 0] + gate_pair[:, 1])[order]
    chosen = gate_mine > 0.0
    before = jnp.arange(row_count)[:, None] < jnp.arange(row_count)[None, :]
    rank = mm(chosen.astype(jnp.bfloat16), before.astype(jnp.bfloat16)).astype(jnp.int32)
    rank = jnp.where(chosen, rank, -1)
    slot = jnp.arange(slots, dtype=jnp.int32)
    picks = rank[:, None, :] == slot[None, :, None]
    slot_gate = jnp.sum(jnp.where(picks, gate_mine[:, None, :], 0.0), axis=2).reshape(-1, 1)
    picks = picks.astype(jnp.bfloat16)
    unpicks = (rank[:, :, None] == slot[None, None, :]).astype(jnp.bfloat16)
    ones = jnp.ones_like(slot_gate)
    ff = w_gate.shape[2]
    w_both = jnp.concatenate([w_gate[0], w_up[0]], axis=1)

    cot_rounds = gather(cotangent)
    query_raw, key_raw, value, value_t, squares = heads_in(order, head_w, row_count, blocks)
    if sharing > 1:
        squares = jnp.stack(
            [jnp.sum(jnp.square(my_part(raw, 0)), axis=0) for raw in (query_raw, key_raw)]
        )
    (squares,) = cot_rounds.step(squares)
    squares = butterfly(squares, "expert")
    inverse = lax.rsqrt(squares / width + eps)
    query_t, query, key_t, key, attended, attended_t, log_total = attend(
        query_raw, key_raw, value_t, inverse, gains, cosine, rope_sine, key_seg, query_seg
    )
    if grouped:
        attended, out_far = cot_rounds.step(attended, out_far)
        out_cross = send(out_far, swap_core)

    attended_low = exchange(my_part(attended, 1).reshape(devices, row_count, part))
    if grouped:
        middle, normed_mid = out_project(
            where, attended_low, tokens, ffn_gain[None, :], blocks, out_far, out_cross
        )
    else:
        attended_low = attended_low.transpose(1, 0, 2).reshape(row_count, width)
        middle = resid_in + mm(attended_low, out_full)
        normed_mid = norm_rows(middle, ffn_gain)[0].astype(jnp.bfloat16)
    (normed_mid,) = cot_rounds.step(normed_mid)

    mid_rounds = gather(normed_mid)
    head_w_t = jnp.concatenate(
        [my_part(head_w[:, i * HEAD_DIM : (i + 1) * HEAD_DIM], 1).T for i in range(3)], axis=0
    )
    (head_w_t,) = mid_rounds.step(head_w_t)
    rows_in = pick(picks, ones, mid_rounds.finish())
    (rows_in,) = cot_rounds.step(rows_in)
    grad_eo = pick(picks, slot_gate, cot_rounds.finish())
    gate_up = mm(rows_in, w_both)
    gate_in, up_in = gate_up[:, :ff], gate_up[:, ff:]
    sigmoid_in = jax.nn.sigmoid(gate_in)
    silu_in = gate_in * sigmoid_in
    hidden = (silu_in * up_in).astype(jnp.bfloat16)
    grad_down, down_far = weight_grad(hidden, grad_eo)

    def give_back(produce):
        def some(first, count):
            here = slice(first // row_count, (first + count) // row_count)
            rows = produce(slice(here.start * slots, here.stop * slots))
            return jnp.einsum(
                "bts,bsd->btd",
                unpicks[here],
                rows.astype(jnp.bfloat16).reshape(-1, slots, width),
                preferred_element_type=jnp.bfloat16,
            ).reshape(count, width)

        return some

    hidden_next, grad_eo_next = together(hidden, grad_eo, *grad_down)[:2]
    mix_rounds = scatter(
        give_back(lambda some: mm(hidden_next[some], w_down[0]) * slot_gate[some])
    )
    grad_hidden = contract_cols(grad_eo_next, w_down[0])
    grad_pre = jnp.concatenate(
        [
            (
                grad_hidden * up_in * sigmoid_in * (1.0 + gate_in * (1.0 - sigmoid_in))
            ).astype(jnp.bfloat16),
            (grad_hidden * silu_in).astype(jnp.bfloat16),
        ],
        axis=1,
    )
    (grad_pre,) = ride(mix_rounds, grad_pre)
    row_rounds = scatter(
        give_back(lambda some: contract_cols(grad_pre[some], w_both)),
        lambda addends: ride(mix_rounds, addends)[0],
    )
    grad_both, both_far = weight_grad(rows_in, grad_pre)
    far, i = waiting.pop(0) if grouped else (None, 0)
    if grouped:
        (far[i], *_) = step_all([row_rounds, mix_rounds], far[i], *grad_both[:1])
    else:
        row_rounds.step()
    ride(row_rounds, *mix_rounds.sent, *grad_both[1:2])
    row_rounds.step(*grad_both[2:4])
    ride(row_rounds, *grad_both[4:5])
    ride(row_rounds, *grad_both[5:6])
    grad_normed_mid = row_rounds.finish()

    grad_out = cotangent.astype(jnp.float32)
    _, normal_mid, inverse_mid = norm_rows(middle, ffn_gain)
    mid_back, grad_ffn_gain = norm_back(grad_normed_mid, normal_mid, inverse_mid, ffn_gain)
    grad_middle = grad_out + mid_back
    grad_branch = grad_middle.astype(jnp.bfloat16)
    if grouped:
        grad_columns = out_project_back(where, grad_branch, blocks, out_far, out_cross)
        (grad_columns,) = ride(mix_rounds, grad_columns)
    else:
        grad_columns = to_heads(contract_cols(grad_branch, out_full).astype(jnp.bfloat16))
    grad_attended = exchange(grad_columns).reshape(seq_length, HEAD_DIM)
    if groups == 2:
        (down_total,) = merge(grad_down, down_far, 1)
        grad_attended, down_total, *_ = cross(grad_attended, down_total, *grad_both[6:])
    else:
        down_total = down_far[0].astype(jnp.float32)
    mixed = mix_rounds.finish()
    activations = (middle + mixed).astype(jnp.bfloat16)
    branch_all = lax.all_gather(
        after(grad_branch, grad_attended), "expert", axis=0, tiled=True
    )

    weighted_query, weighted_key, grad_value_t, inner_query, inner_key, gain_sums = attend_back(
        key_seg,
        query_seg,
        log_total,
        query_t,
        query,
        grad_attended,
        key,
        key_t,
        value,
        query_raw,
        key_raw,
        inverse,
        gains,
        cosine,
        rope_sine,
    )
    inner = jnp.concatenate([inner_query, inner_key], axis=0)
    if sharing > 1:
        inner = jnp.stack(
            [
                jnp.sum(my_part(weighted * raw * at, 0), axis=0)
                for weighted, raw, at in (
                    (weighted_query, query_raw, inverse[0:1]),
                    (weighted_key, key_raw, inverse[1:2]),
                )
            ]
        )
    (inner,) = cross(inner)
    inner = butterfly(inner, "expert") / width
    grad_raw_t = jnp.concatenate(
        [
            my_part(
                (at * (weighted - raw * at * mean)).astype(jnp.bfloat16),
                0,
            )
            for weighted, raw, at, mean in (
                (weighted_query, query_raw, inverse[0:1], inner[0:1]),
                (weighted_key, key_raw, inverse[1:2], inner[1:2]),
            )
        ]
        + [my_part(grad_value_t, 0)],
        axis=0,
    )
    in_rounds = scatter(
        lambda first, count: project(order, grad_raw_t, head_w_t, row_count, first, count),
        both_first=True,
    )
    (grad_raw_t,) = in_rounds.step(grad_raw_t)
    grad_w_t = stack_product(order, grad_raw_t, row_count, blocks)
    grad_attn_gain = jnp.sum(grad_w_t * head_w_t.astype(jnp.float32), axis=0) / attn_gain
    (grad_w_t,) = ride(in_rounds, grad_w_t)
    w_columns = exchange(
        grad_w_t.astype(jnp.bfloat16).reshape(3 * part, devices, w_rows).transpose(1, 0, 2)
    )

    def placed(values):
        return lax.dynamic_update_slice_in_dim(
            jnp.zeros((width,), jnp.float32), values, me * part, 0
        )

    gain_parts = jnp.stack(
        [
            grad_attn_gain,
            placed(my_part(gain_sums[:, 0], 0)),
            placed(my_part(gain_sums[:, 1], 0)),
            grad_ffn_gain,
        ]
    )
    out_part = mm(my_part(attended_t, 0), branch_all).astype(jnp.bfloat16)
    dense = [
        w_columns[:, i * part : (i + 1) * part].reshape(width, w_rows).T for i in range(3)
    ]
    out_part, *dense = ride(in_rounds, out_part, *dense)
    out_part_far = dp_start(out_part)
    dense_far = [dp_start(values) for values in dense]
    if groups == 2:
        both_total = list(merge(grad_both[:4], both_far[:4], 2, len(grad_both)))
        gain_parts, both_total[0], both_total[1] = ride(in_rounds, gain_parts, *both_total)
        both_total = merge(grad_both[4:], both_far[4:], 2, 4, both_total)
    else:
        in_rounds.step()
        both_total = both_far[0].astype(jnp.float32)
        both_total = (both_total[:, :ff], both_total[:, ff:])
    out_part_far, dense_far[0], *both_total = in_rounds.step(
        out_part_far, dense_far[0], *both_total
    )
    gate_total, up_total = both_total
    grad_normed_in = in_rounds.finish()
    grad_normed_in, gain_parts = together(grad_normed_in, gain_parts)
    gain_parts = butterfly(gain_parts, "expert")
    gain_parts, dense_far[2], gate_total = together(gain_parts, dense_far[2], gate_total)
    gain_total = butterfly(gain_parts, "dp")
    in_back, _ = norm_back(grad_normed_in, normal_in, inverse_in, attn_gain)
    input_grad = (grad_middle + in_back).astype(jnp.bfloat16)

    return (
        activations,
        input_grad,
        gain_total[0],
        gain_total[1],
        gain_total[2],
        gain_total[3],
        dp_end(dense[0], dense_far[0]),
        dp_end(dense[1], dense_far[1]),
        dp_end(dense[2], dense_far[2]),
        dp_end(out_part, out_part_far),
        gate_total[None],
        up_total[None],
        down_total[None],
    )


def solution(mesh):
    in_specs = (
        P(("dp", "expert"), None),
        P("dp"),
        P(("dp", "expert"), None),
        P(("dp", "expert"), None),
        P(),
        P(),
        P(),
        P(),
        P("expert", None),
        P("expert", None),
        P("expert", None),
        P("expert", None),
        P("expert", None, None),
        P("expert", None, None),
        P("expert", None, None),
        P(("dp", "expert"), None),
    )
    out_specs = (
        P(("dp", "expert"), None),
        P(("dp", "expert"), None),
        P(),
        P(),
        P(),
        P(),
        P("expert", None),
        P("expert", None),
        P("expert", None),
        P("expert", None),
        P("expert", None, None),
        P("expert", None, None),
        P("expert", None, None),
    )
    return jax.shard_map(local, mesh=mesh, in_specs=in_specs, out_specs=out_specs, check_vma=False)
```

```python
import functools

import jax
import jax.numpy as jnp
from jax import lax
from jax.experimental import pallas as pl
from jax.experimental.pallas import tpu as pltpu
from jax.sharding import PartitionSpec as P

HEADS = 16
HEAD_DIM = 128


eps = 1e-05
rope_base = 50000.0
negative = -1e30
score_scale = HEAD_DIM ** (-0.5)
def query_block_of(count):
    return 512 if count <= 2048 else 256


def norm_rows(values, norm_gain):
    inverse = lax.rsqrt(jnp.mean(values * values, axis=-1, keepdims=True) + eps)
    normal = values * inverse
    return (normal * norm_gain, normal, inverse)


def norm_back(upstream, normal, inverse, norm_gain):
    weighted = upstream * norm_gain
    inner_mean = jnp.mean(weighted * normal, axis=-1, keepdims=True)
    return (inverse * (weighted - normal * inner_mean), jnp.sum(upstream * normal, axis=0))


def rope_tables(positions):
    half_dim = HEAD_DIM // 2
    frequency = rope_base ** (-(jnp.arange(half_dim, dtype=jnp.float32) * 2.0 / HEAD_DIM))
    theta = frequency[:, None] * positions.astype(jnp.float32)[None, :]
    return (jnp.cos(theta), jnp.sin(theta))


def mm(left, right):
    return jnp.dot(left, right, preferred_element_type=jnp.float32)


def contract_rows(left, right):
    return lax.dot_general(
        left, right, (((0,), (0,)), ((), ())), preferred_element_type=jnp.float32
    )


def contract_cols(left, right):
    return lax.dot_general(
        left, right, (((1,), (1,)), ((), ())), preferred_element_type=jnp.float32
    )


def swap(values, axis, step):
    count = lax.axis_size(axis)
    return lax.ppermute(values, axis, [(i, i ^ step) for i in range(count)])


def together(*values):
    return lax.optimization_barrier(values)


def after(values, *others):
    return lax.optimization_barrier((values,) + others)[0]


def butterfly(values, axis):
    step = 1
    while step < lax.axis_size(axis):
        if 2 * step < lax.axis_size(axis):
            one, two, three = [swap(values, axis, times * step) for times in (1, 2, 3)]
            values = (values + one) + (two + three)
            step *= 4
        else:
            values = values + swap(values, axis, step)
            step *= 2
    return values


near_order = ((0, 1, 2, 3), (1, 0, 2, 3), (2, 3, 1, 0), (3, 2, 1, 0))


def moves(target):
    pairs = []
    for index in range(16):
        far = target(index // 4)
        if far is not None:
            pairs.append((index, far * 4 + index % 4))
    return pairs


swap_near = moves(lambda z: z ^ 1)
swap_middle = moves(lambda z: {1: 2, 2: 1}.get(z))
move_out = moves(lambda z: {1: 0, 2: 3}.get(z))
move_in = moves(lambda z: {0: 1, 3: 2}.get(z))
swap_row = [(i, i ^ 2) for i in range(16)]
swap_core = [(i, i ^ 1) for i in range(16)]


def send(values, pairs):
    return lax.ppermute(values, "expert", pairs)


def arrival_order(me):
    near = jnp.asarray(near_order, jnp.int32)[me // 4] * 4
    row, core = (me // 2) % 2, me % 2
    return jnp.concatenate(
        [near + (row ^ j) * 2 + (core ^ i) for i in (0, 1) for j in (0, 1)]
    ).astype(jnp.int32)


class Rounds:
    def __init__(self, steps):
        self.steps = steps
        self.result = None
        self.over = False
        self.sent = ()
        self._go(None)

    def _go(self, arrived):
        try:
            self.sent = self.steps.send(arrived)
        except StopIteration as stop:
            self.result, self.sent, self.over = stop.value, (), True

    def step(self, *others):
        return step_all([self], *others)

    def finish(self):
        while not self.over:
            self.step()
        return self.result


def step_all(rounds, *others):
    sent = [values for one in rounds for values in one.sent]
    values = together(*sent, *others) if sent or others else ()
    at = 0
    for one in rounds:
        count = len(one.sent)
        if not one.over:
            one._go(values[at : at + count])
        at += count
    return values[at:]


def gather_rounds(block):
    at = lax.axis_index("expert") // 4
    outer = (at == 0) | (at == 3)
    first, second, row = yield (
        send(block, swap_near),
        send(block, swap_middle),
        send(block, swap_row),
    )
    third, second_out, row_first, core = yield (
        send(first, swap_middle),
        send(second, move_out),
        send(first, swap_row),
        send(block, swap_core),
    )
    second = jnp.where(outer, second_out, second)
    third_out, row_second, core_first, core_row = yield (
        send(third, move_out),
        send(second, swap_row),
        send(first, swap_core),
        send(row, swap_core),
    )
    third = jnp.where(outer, third_out, third)
    row_third, core_second, core_third, core_row_first, core_row_second = yield (
        send(third, swap_row),
        send(second, swap_core),
        send(third, swap_core),
        send(row_first, swap_core),
        send(row_second, swap_core),
    )
    (core_row_third,) = yield (send(row_third, swap_core),)
    return [
        block,
        first,
        second,
        third,
        row,
        row_first,
        row_second,
        row_third,
        core,
        core_first,
        core_second,
        core_third,
        core_row,
        core_row_first,
        core_row_second,
        core_row_third,
    ]


def gather_whole(block):
    yield ()
    return list(lax.all_gather(block, "expert", axis=0))


def add_low(left, right):
    return (left.astype(jnp.float32) + right.astype(jnp.float32)).astype(jnp.bfloat16)


def scatter_rounds(make, count, tie, both_first):
    far = send(tie(make(count // 2, count // 2)), swap_core)
    if both_first:
        far, close = yield (far, make(0, count // 2))
    else:
        (far,) = yield (far,)
        close = make(0, count // 2)
    rows = count // 16

    def both(j, k):
        here = slice((j * 4 + k) * rows, (j * 4 + k + 1) * rows)
        return add_low(close[here], far[here])

    (row,) = yield (send(both(1, 3), swap_row),)
    third = add_low(both(0, 3), row)
    row, third_in = yield (send(both(1, 2), swap_row), send(third, move_in))
    second = add_low(both(0, 2), row)
    third = add_low(third, third_in)
    row, second_in, third_in = yield (
        send(both(1, 1), swap_row),
        send(second, move_in),
        send(third, swap_middle),
    )
    first = add_low(add_low(both(0, 1), row), third_in)
    second = add_low(second, second_in)
    row, second_in, first_in = yield (
        send(both(1, 0), swap_row),
        send(second, swap_middle),
        send(first, swap_near),
    )
    return (
        both(0, 0).astype(jnp.float32)
        + row.astype(jnp.float32)
        + second_in.astype(jnp.float32)
        + first_in.astype(jnp.float32)
    )


def scatter_whole(make, count, tie, both_first):
    yield ()
    return lax.psum_scatter(
        tie(make(0, count)), "expert", scatter_dimension=0, tiled=True
    ).astype(jnp.float32)


def pick_kernel(picks, scale, *refs):
    *blocks, out = refs
    slots = picks.shape[1]
    for index, block in enumerate(blocks):
        here = slice(index * slots, (index + 1) * slots)
        out[here, :] = (mm(picks[index], block[...]) * scale[here, :]).astype(out.dtype)


def pick(picks, scale, blocks):
    count, slots, tokens = picks.shape
    width = blocks[0].shape[1]
    return pl.pallas_call(
        pick_kernel,
        out_shape=jax.ShapeDtypeStruct((count * slots, width), jnp.bfloat16),
        cost_estimate=pl.CostEstimate(
            flops=2 * count * tokens * slots * width,
            bytes_accessed=2 * count * (tokens + slots) * width,
            transcendentals=0,
        ),
        name="pick",
    )(picks, scale, *blocks)


def merge_kernel(count, parts, *refs):
    pairs, outs = refs[: 2 * count], refs[-parts:]
    width = outs[0].shape[1]
    for index in range(count):

        @pl.when(pl.program_id(0) == index)
        def _():
            total = pairs[index][...].astype(jnp.float32) + pairs[count + index][...].astype(
                jnp.float32
            )
            for i, out in enumerate(outs):
                out[...] = total[:, i * width : (i + 1) * width]


def merge(own, far, parts, pieces=None, before=None):
    count = len(own)
    begin = pieces if before else 0
    before = before or []
    pieces = begin + count if before else pieces or count
    rows, width = own[0].shape
    return pl.pallas_call(
        functools.partial(merge_kernel, count, parts),
        grid=(count,),
        in_specs=[pl.BlockSpec((rows, width), lambda i: (0, 0))] * (2 * count)
        + [pl.BlockSpec(memory_space=pl.ANY)] * len(before),
        out_specs=[pl.BlockSpec((rows, width // parts), lambda i: (begin + i, 0))] * parts,
        out_shape=[jax.ShapeDtypeStruct((pieces * rows, width // parts), jnp.float32)] * parts,
        input_output_aliases={2 * count + i: i for i in range(len(before))},
        cost_estimate=pl.CostEstimate(
            flops=count * rows * width,
            bytes_accessed=8 * count * rows * width,
            transcendentals=0,
        ),
        compiler_params=pltpu.CompilerParams(vmem_limit_bytes=28 * 2**20),
        name="merge",
    )(*own, *far, *before)


def project_kernel(order, left_t, left_next_t, right, out):
    left = jnp.concatenate([left_t[...].T, left_next_t[...].T], axis=0)
    out[...] = mm(left, right[...]).astype(out.dtype)


def project(order, left_t, right, rows, first, count):
    depth, width = right.shape
    begin = first // rows
    return pl.pallas_call(
        project_kernel,
        grid_spec=pltpu.PrefetchScalarGridSpec(
            num_scalar_prefetch=1,
            grid=(count // (2 * rows),),
            in_specs=[
                pl.BlockSpec((depth, rows), lambda i, order: (0, order[begin + 2 * i])),
                pl.BlockSpec((depth, rows), lambda i, order: (0, order[begin + 2 * i + 1])),
                pl.BlockSpec((depth, width), lambda i, order: (0, 0)),
            ],
            out_specs=pl.BlockSpec((2 * rows, width), lambda i, order: (i, 0)),
        ),
        out_shape=jax.ShapeDtypeStruct((count, width), jnp.bfloat16),
        cost_estimate=pl.CostEstimate(
            flops=2 * count * depth * width,
            bytes_accessed=2 * (count * (depth + width) + depth * width),
            transcendentals=0,
        ),
        compiler_params=pltpu.CompilerParams(vmem_limit_bytes=28 * 2**20),
        name="project",
    )(order, left_t, left_t, right)


scalars = pl.BlockSpec(memory_space=pltpu.SMEM)
vectors = pl.BlockSpec(memory_space=pltpu.VMEM)


def lanes(order, index, rows):
    return pl.ds(pl.multiple_of(order[index] * rows, rows), rows)


def stack_kernel(rows, order, left_t, *refs):
    *blocks, out = refs
    for index in range(0, len(blocks), 4):
        four = range(index, index + 4)
        left = jnp.concatenate([left_t[:, lanes(order, i, rows)] for i in four], axis=1)
        right = jnp.concatenate([blocks[i][:rows] for i in four], axis=0)
        term = mm(left, right)
        if index == 0:
            out[...] = term
        else:
            out[...] += term


def stack_product(order, left_t, rows, blocks):
    width = blocks[0].shape[1]
    return pl.pallas_call(
        functools.partial(stack_kernel, rows),
        in_specs=[scalars, vectors] + [vectors] * len(blocks),
        out_specs=vectors,
        out_shape=jax.ShapeDtypeStruct((left_t.shape[0], width), jnp.float32),
        cost_estimate=pl.CostEstimate(
            flops=2 * left_t.size * width,
            bytes_accessed=2 * len(blocks) * rows * width,
            transcendentals=0,
        ),
        compiler_params=pltpu.CompilerParams(vmem_limit_bytes=28 * 2**20),
        name="stack_product",
    )(order, left_t, *blocks)


def heads_kernel(rows, order, weight, *refs):
    *blocks, query_t, key_t, value, value_t, squares = refs
    for index in range(0, len(blocks), 4):
        four = range(index, index + 4)
        raw = mm(jnp.concatenate([blocks[i][:rows] for i in four], axis=0), weight[...])
        for i in four:
            own = raw[(i - index) * rows : (i - index + 1) * rows]
            here = lanes(order, i, rows)
            query = own[:, :HEAD_DIM].T
            key = own[:, HEAD_DIM : 2 * HEAD_DIM].T
            query_t[:, here] = query
            key_t[:, here] = key
            value[here, :] = own[:, 2 * HEAD_DIM :].astype(value.dtype)
            value_t[:, here] = own[:, 2 * HEAD_DIM :].T.astype(value.dtype)
            squares[0:1, here] = jnp.sum(query * query, axis=0, keepdims=True)
            squares[1:2, here] = jnp.sum(key * key, axis=0, keepdims=True)


def heads_in(order, weight, rows, blocks):
    width = blocks[0].shape[1]
    count = len(blocks) * rows
    return pl.pallas_call(
        functools.partial(heads_kernel, rows),
        in_specs=[scalars, vectors] + [vectors] * len(blocks),
        out_specs=[vectors] * 5,
        out_shape=[
            jax.ShapeDtypeStruct((HEAD_DIM, count), jnp.float32),
            jax.ShapeDtypeStruct((HEAD_DIM, count), jnp.float32),
            jax.ShapeDtypeStruct((count, HEAD_DIM), jnp.bfloat16),
            jax.ShapeDtypeStruct((HEAD_DIM, count), jnp.bfloat16),
            jax.ShapeDtypeStruct((2, count), jnp.float32),
        ],
        cost_estimate=pl.CostEstimate(
            flops=2 * count * width * 3 * HEAD_DIM,
            bytes_accessed=2 * count * width,
            transcendentals=0,
        ),
        name="heads_in",
    )(order, weight, *blocks)


def tail_kernel(*refs):
    *blocks, out = refs
    rows = blocks[0].shape[0]
    for index, block in enumerate(blocks):
        out[index * rows : (index + 1) * rows, :] = block[...]


def tail_specs(blocks, rows, tail):
    width = blocks[0].shape[1]
    return [pl.BlockSpec((tail, width), lambda i: (rows // tail, 0))] * len(blocks)


def tails(blocks, rows, tail):
    width = blocks[0].shape[1]
    return pl.pallas_call(
        tail_kernel,
        grid=(1,),
        in_specs=tail_specs(blocks, rows, tail),
        out_specs=pl.BlockSpec((len(blocks) * tail, width), lambda i: (0, 0)),
        out_shape=jax.ShapeDtypeStruct((len(blocks) * tail, width), jnp.bfloat16),
        name="tails",
    )(*blocks)


def four(refs, index):
    return jnp.concatenate([ref[...] for ref in refs[index : index + 4]], axis=0)


def far_four(far, cross, index):
    rows = far.shape[0] // 2
    ref, at = (far, index // 4) if index < 8 else (cross, index // 4 - 2)
    return ref[at * rows : (at + 1) * rows, :]


def out_kernel(where, attended, resid, gain, *refs):
    *near, far, cross, middle, normed = refs
    count = len(near)
    half = HEAD_DIM // 2
    first_group = where[count] == 0
    total = resid[...].astype(jnp.float32)
    for index in range(0, count, 4):
        near_left, far_left = [], []
        for i in range(index, index + 4):
            columns = attended[where[i]].astype(jnp.float32)
            low, high = columns[:, :half], columns[:, half:]
            near_left.append(jnp.where(first_group, low, high))
            far_left.append(jnp.where(first_group, high, low))
        total += mm(jnp.concatenate(near_left, axis=1).astype(jnp.bfloat16), four(near, index))
        total += mm(
            jnp.concatenate(far_left, axis=1).astype(jnp.bfloat16), far_four(far, cross, index)
        )
    middle[...] = total
    inverse = lax.rsqrt(jnp.mean(total * total, axis=-1, keepdims=True) + eps)
    normed[...] = (total * inverse * gain[...]).astype(normed.dtype)


def whole_specs(*arrays):
    return [pl.BlockSpec(array.shape, lambda i, rank=array.ndim: (0,) * rank) for array in arrays]


def out_project(where, attended, resid, gain, blocks, far, cross):
    rows, width = resid.shape
    tail = blocks[0].shape[0] - rows
    return pl.pallas_call(
        out_kernel,
        grid=(1,),
        in_specs=[scalars]
        + whole_specs(attended, resid, gain)
        + tail_specs(blocks, rows, tail)
        + whole_specs(far, cross),
        out_specs=whole_specs(resid, resid),
        out_shape=[
            jax.ShapeDtypeStruct((rows, width), jnp.float32),
            jax.ShapeDtypeStruct((rows, width), jnp.bfloat16),
        ],
        cost_estimate=pl.CostEstimate(
            flops=2 * rows * width * width,
            bytes_accessed=2 * width * width,
            transcendentals=0,
        ),
        name="out_project",
    )(where, attended, resid, gain, *blocks, far, cross)


def out_back_kernel(where, branch, *refs):
    *near_refs, far_ref, cross, out = refs
    count = len(near_refs)
    half = HEAD_DIM // 2
    first_group = where[count] == 0
    for index in range(0, count, 4):
        near = contract_cols(branch[...], four(near_refs, index))
        far = contract_cols(branch[...], far_four(far_ref, cross, index))
        for i in range(index, index + 4):
            here = slice((i - index) * half, (i - index + 1) * half)
            low = jnp.where(first_group, near[:, here], far[:, here])
            high = jnp.where(first_group, far[:, here], near[:, here])
            out[where[i]] = jnp.concatenate([low, high], axis=1).astype(out.dtype)


def out_project_back(where, branch, blocks, far, cross):
    rows, width = branch.shape
    tail = blocks[0].shape[0] - rows
    shape = (len(blocks), rows, HEAD_DIM)
    return pl.pallas_call(
        out_back_kernel,
        grid=(1,),
        in_specs=[scalars]
        + whole_specs(branch)
        + tail_specs(blocks, rows, tail)
        + whole_specs(far, cross),
        out_specs=pl.BlockSpec(shape, lambda i: (0, 0, 0)),
        out_shape=jax.ShapeDtypeStruct(shape, jnp.bfloat16),
        cost_estimate=pl.CostEstimate(
            flops=2 * rows * width * width,
            bytes_accessed=2 * width * width,
            transcendentals=0,
        ),
        name="out_project_back",
    )(where, branch, *blocks, far, cross)


def turn(values, cosine, rope_sine):
    half = HEAD_DIM // 2
    first, second = values[:half], values[half:]
    return jnp.concatenate(
        [first * cosine - second * rope_sine, second * cosine + first * rope_sine], axis=0
    )


def attend_kernel(
    query_raw,
    key_raw,
    value_t,
    inverse,
    inverse_all,
    gains,
    cosine,
    rope_sine,
    cosine_all,
    rope_sine_all,
    key_seg,
    query_seg,
    query_t,
    query,
    key_t,
    key,
    out,
    out_t,
    log_total,
):
    @pl.when(pl.program_id(0) == 0)
    def _():
        turned = turn(
            key_raw[...] * inverse_all[1:2, :] * gains[:, 1:2], cosine_all[...], rope_sine_all[...]
        ).astype(jnp.bfloat16)
        key_t[...] = turned
        key[...] = turned.T

    turned = turn(
        query_raw[...] * inverse[0:1, :] * gains[:, 0:1], cosine[...], rope_sine[...]
    ).astype(jnp.bfloat16)
    query_t[...] = turned
    query[...] = turned.T
    scores = mm(key[...], turned) * score_scale
    scores = jnp.where(key_seg[:, :1] == query_seg[...], scores, negative)
    peak = jnp.max(scores, axis=0, keepdims=True)
    weights = jnp.exp(scores - peak)
    total = jnp.sum(weights, axis=0, keepdims=True)
    result = mm(value_t[...], weights.astype(jnp.bfloat16)) / total
    out_t[...] = result.astype(out_t.dtype)
    out[...] = result.T.astype(out.dtype)
    log_total[...] = peak + jnp.log(total)


def attend(query_raw, key_raw, value_t, inverse, gains, cosine, rope_sine, key_seg, query_seg):
    count = query_raw.shape[1]
    query_block = query_block_of(count)
    whole = lambda i: (0, 0)
    across = lambda rows: pl.BlockSpec((rows, query_block), lambda i: (0, i))
    down = pl.BlockSpec((query_block, HEAD_DIM), lambda i: (i, 0))
    all_of = lambda rows: pl.BlockSpec((rows, count), whole)
    low, half = jnp.bfloat16, HEAD_DIM // 2
    return pl.pallas_call(
        attend_kernel,
        grid=(count // query_block,),
        in_specs=[
            across(HEAD_DIM),
            all_of(HEAD_DIM),
            all_of(HEAD_DIM),
            across(2),
            all_of(2),
            pl.BlockSpec((HEAD_DIM, 2), whole),
            across(half),
            across(half),
            all_of(half),
            all_of(half),
            pl.BlockSpec((count, HEAD_DIM), whole),
            across(1),
        ],
        out_specs=[
            across(HEAD_DIM),
            down,
            all_of(HEAD_DIM),
            pl.BlockSpec((count, HEAD_DIM), whole),
            down,
            across(HEAD_DIM),
            across(1),
        ],
        out_shape=[
            jax.ShapeDtypeStruct((HEAD_DIM, count), low),
            jax.ShapeDtypeStruct((count, HEAD_DIM), low),
            jax.ShapeDtypeStruct((HEAD_DIM, count), low),
            jax.ShapeDtypeStruct((count, HEAD_DIM), low),
            jax.ShapeDtypeStruct((count, HEAD_DIM), low),
            jax.ShapeDtypeStruct((HEAD_DIM, count), low),
            jax.ShapeDtypeStruct((1, count), jnp.float32),
        ],
        cost_estimate=pl.CostEstimate(
            flops=4 * count * count * HEAD_DIM,
            bytes_accessed=count * HEAD_DIM * 24,
            transcendentals=count * count,
        ),
        name="attend",
    )(
        query_raw,
        key_raw,
        value_t,
        inverse,
        inverse,
        gains,
        cosine,
        rope_sine,
        cosine,
        rope_sine,
        key_seg,
        query_seg,
    )


def attend_back_kernel(
    key_seg,
    query_seg,
    log_total,
    query_t,
    query,
    upstream,
    key,
    key_t,
    value,
    query_raw,
    key_raw,
    inverse,
    inverse_all,
    gains,
    cosine,
    rope_sine,
    cosine_all,
    rope_sine_all,
    weighted_query,
    weighted_key,
    dvalue_t,
    inner_query,
    inner_key,
    gain_sums,
    dkey,
    dvalue,
):
    step = pl.program_id(0)

    @pl.when(step == 0)
    def _():
        dkey[...] = jnp.zeros_like(dkey)
        dvalue[...] = jnp.zeros_like(dvalue)
        gain_sums[...] = jnp.zeros_like(gain_sums)

    scores = mm(key[...], query_t[...]) * score_scale
    probs = jnp.where(key_seg[:, :1] == query_seg[...], jnp.exp(scores - log_total[...]), 0.0)
    dvalue[...] += mm(probs.astype(jnp.bfloat16), upstream[...])
    dprobs = contract_cols(value[...], upstream[...])
    delta = jnp.sum(probs * dprobs, axis=0, keepdims=True)
    dscores = (probs * (dprobs - delta)).astype(jnp.bfloat16)
    dkey[...] += mm(dscores, query[...])
    turned = turn(mm(key_t[...], dscores) * score_scale, cosine[...], -rope_sine[...])
    product = turned * (query_raw[...] * inverse[0:1, :])
    weighted_query[...] = turned * gains[:, 0:1]
    inner_query[...] = jnp.sum(product * gains[:, 0:1], axis=0, keepdims=True)
    gain_sums[:, 0:1] += jnp.sum(product, axis=1, keepdims=True)

    @pl.when(step == pl.num_programs(0) - 1)
    def _():
        turned = turn(dkey[...].T * score_scale, cosine_all[...], -rope_sine_all[...])
        product = turned * (key_raw[...] * inverse_all[1:2, :])
        weighted_key[...] = turned * gains[:, 1:2]
        inner_key[...] = jnp.sum(product * gains[:, 1:2], axis=0, keepdims=True)
        gain_sums[:, 1:2] = jnp.sum(product, axis=1, keepdims=True)
        dvalue_t[...] = dvalue[...].T.astype(dvalue_t.dtype)


def attend_back(
    key_seg,
    query_seg,
    log_total,
    query_t,
    query,
    upstream,
    key,
    key_t,
    value,
    query_raw,
    key_raw,
    inverse,
    gains,
    cosine,
    rope_sine,
):
    count = query.shape[0]
    query_block = query_block_of(count)
    whole = lambda i: (0, 0)
    across = lambda rows: pl.BlockSpec((rows, query_block), lambda i: (0, i))
    down = pl.BlockSpec((query_block, HEAD_DIM), lambda i: (i, 0))
    all_of = lambda rows: pl.BlockSpec((rows, count), whole)
    tall = pl.BlockSpec((count, HEAD_DIM), whole)
    half = HEAD_DIM // 2
    return pl.pallas_call(
        attend_back_kernel,
        grid=(count // query_block,),
        in_specs=[
            tall,
            across(1),
            across(1),
            across(HEAD_DIM),
            down,
            down,
            tall,
            all_of(HEAD_DIM),
            tall,
            across(HEAD_DIM),
            all_of(HEAD_DIM),
            across(2),
            all_of(2),
            pl.BlockSpec((HEAD_DIM, 2), whole),
            across(half),
            across(half),
            all_of(half),
            all_of(half),
        ],
        out_specs=[
            across(HEAD_DIM),
            all_of(HEAD_DIM),
            all_of(HEAD_DIM),
            across(1),
            all_of(1),
            pl.BlockSpec((HEAD_DIM, 2), whole),
        ],
        out_shape=[
            jax.ShapeDtypeStruct((HEAD_DIM, count), jnp.float32),
            jax.ShapeDtypeStruct((HEAD_DIM, count), jnp.float32),
            jax.ShapeDtypeStruct((HEAD_DIM, count), jnp.bfloat16),
            jax.ShapeDtypeStruct((1, count), jnp.float32),
            jax.ShapeDtypeStruct((1, count), jnp.float32),
            jax.ShapeDtypeStruct((HEAD_DIM, 2), jnp.float32),
        ],
        scratch_shapes=[
            pltpu.VMEM((count, HEAD_DIM), jnp.float32),
            pltpu.VMEM((count, HEAD_DIM), jnp.float32),
        ],
        cost_estimate=pl.CostEstimate(
            flops=10 * count * count * HEAD_DIM,
            bytes_accessed=count * HEAD_DIM * 40,
            transcendentals=count * count,
        ),
        name="attend_back",
    )(
        key_seg,
        query_seg,
        log_total,
        query_t,
        query,
        upstream,
        key,
        key_t,
        value,
        query_raw,
        key_raw,
        inverse,
        inverse,
        gains,
        cosine,
        rope_sine,
        cosine,
        rope_sine,
    )


def local(
    tokens,
    segments,
    routes,
    route_gates,
    attn_gain,
    query_gain,
    key_gain,
    ffn_gain,
    w_query,
    w_key,
    w_value,
    w_out,
    w_gate,
    w_up,
    w_down,
    cotangent,
):
    row_count, width = tokens.shape
    top_count = routes.shape[1]
    devices = lax.axis_size("expert")
    groups = lax.axis_size("dp")
    me = lax.axis_index("expert")
    my_group = lax.axis_index("dp")
    seq_length = row_count * devices
    part = width // devices
    sharing = HEAD_DIM // part
    head = me // sharing
    sub = me % sharing
    w_rows = w_query.shape[0]
    w_half = w_rows // 2

    grouped = devices == 16 and groups == 2
    order = arrival_order(me) if grouped else jnp.arange(devices, dtype=jnp.int32)
    where = jnp.concatenate([order, my_group[None].astype(jnp.int32)])

    def gather(block):
        return Rounds(gather_rounds(block) if grouped else gather_whole(block))

    def scatter(make, tie=lambda addends: addends, both_first=False):
        kind = scatter_rounds if grouped else scatter_whole
        return Rounds(kind(make, seq_length, tie, both_first))

    def exchange(values):
        return lax.all_to_all(values, "expert", split_axis=0, concat_axis=0, tiled=True)

    def to_heads(rows):
        blocks = rows.reshape(rows.shape[0], HEADS, HEAD_DIM).transpose(1, 0, 2)
        return jnp.repeat(blocks, sharing, axis=0)

    def my_part(columns, axis):
        if sharing == 1:
            return columns
        return lax.dynamic_slice_in_dim(columns, sub * part, part, axis=axis)

    def by_half(values, axis):
        return jnp.where(my_group == 0, values, jnp.flip(values, axis))

    def dp_start(values):
        return swap(values, "dp", 1) if groups == 2 else lax.psum(values, "dp")

    def dp_end(values, arrived):
        total = arrived.astype(jnp.float32)
        return total + values.astype(jnp.float32) if groups == 2 else total

    waiting = []

    def weight_grad(left, right):
        pieces = left.shape[1] // 256 if grouped else 1
        step = left.shape[1] // pieces
        own = [
            contract_rows(left[:, i * step : (i + 1) * step], right).astype(jnp.bfloat16)
            for i in range(pieces)
        ]
        far = [dp_start(values) for values in own]
        waiting.extend((far, i) for i in range(pieces))
        return own, far

    def cross(*others):
        if not (waiting and grouped):
            return others
        far, i = waiting.pop(0)
        *others, far[i] = together(*others, far[i])
        return others

    def ride(rounds, *others):
        if not (waiting and grouped):
            return rounds.step(*others)
        far, i = waiting.pop(0)
        *others, far[i] = rounds.step(*others, far[i])
        return others

    resid_in = tokens.astype(jnp.float32)
    pre_in, normal_in, inverse_in = norm_rows(resid_in, attn_gain)
    normed_in = pre_in.astype(jnp.bfloat16)

    experts_all = devices * w_gate.shape[0]
    slots = min(row_count, row_count * top_count * 3 // (2 * experts_all))
    hits = routes[:, :, None] == jnp.arange(experts_all, dtype=jnp.int32)[None, None, :]
    gate_table = jnp.sum(jnp.where(hits, route_gates[:, :, None], 0.0), axis=1).T
    gate_high = lax.reduce_precision(gate_table, exponent_bits=8, mantissa_bits=7)
    gate_rows = jnp.pad(
        jnp.stack([gate_high, gate_table - gate_high], axis=1).astype(jnp.bfloat16),
        ((0, 0), (0, 14), (0, 3 * HEAD_DIM - row_count)),
    )
    if grouped:
        take = lambda w: lax.dynamic_slice_in_dim(w, my_group * w_half, w_half)
    else:
        take = lambda w: w
    sent_w = jnp.concatenate([to_heads(take(w)) for w in (w_query, w_key, w_value)], axis=2)
    taken = sent_w.shape[1]
    arrived = exchange(jnp.concatenate([sent_w, gate_rows], axis=1))

    key_seg = jnp.broadcast_to(segments[:, None], (seq_length, HEAD_DIM))
    query_seg = segments[None, :]
    cosine, rope_sine = rope_tables(jnp.arange(seq_length, dtype=jnp.int32))
    gains = jnp.stack(
        [
            lax.dynamic_slice_in_dim(query_gain, head * HEAD_DIM, HEAD_DIM),
            lax.dynamic_slice_in_dim(key_gain, head * HEAD_DIM, HEAD_DIM),
        ],
        axis=1,
    )
    if grouped:
        rounds = gather(jnp.concatenate([normed_in, take(w_out)], axis=0))
        rounds.step()
        rounds.step(key_seg, cosine, rope_sine, gains)
        (arrived,) = rounds.step(arrived)
        head_w = arrived[:, :taken]
        head_w_far = swap(head_w, "dp", 1)
        rounds.step()
        blocks = rounds.finish()
        head_w = by_half(jnp.stack([head_w, head_w_far], axis=1), 1).reshape(width, 3 * HEAD_DIM)
        out_far = swap(tails(blocks[: devices // 2], row_count, w_half), "dp", 1)
    else:
        blocks = gather(normed_in).finish()
        head_w = arrived[:, :taken].reshape(width, 3 * HEAD_DIM)
        out_full = lax.all_gather(w_out, "expert", axis=0, tiled=True)

    gate_pair = arrived[:, taken : taken + 2, :row_count].astype(jnp.float32)
    gate_mine = (gate_pair[:, 0] + gate_pair[:, 1])[order]
    chosen = gate_mine > 0.0
    before = jnp.arange(row_count)[:, None] < jnp.arange(row_count)[None, :]
    rank = mm(chosen.astype(jnp.bfloat16), before.astype(jnp.bfloat16)).astype(jnp.int32)
    rank = jnp.where(chosen, rank, -1)
    slot = jnp.arange(slots, dtype=jnp.int32)
    picks = rank[:, None, :] == slot[None, :, None]
    slot_gate = jnp.sum(jnp.where(picks, gate_mine[:, None, :], 0.0), axis=2).reshape(-1, 1)
    picks = picks.astype(jnp.bfloat16)
    unpicks = (rank[:, :, None] == slot[None, None, :]).astype(jnp.bfloat16)
    ones = jnp.ones_like(slot_gate)
    ff = w_gate.shape[2]
    w_both = jnp.concatenate([w_gate[0], w_up[0]], axis=1)

    cot_rounds = gather(cotangent)
    query_raw, key_raw, value, value_t, squares = heads_in(order, head_w, row_count, blocks)
    if sharing > 1:
        squares = jnp.stack(
            [jnp.sum(jnp.square(my_part(raw, 0)), axis=0) for raw in (query_raw, key_raw)]
        )
    (squares,) = cot_rounds.step(squares)
    squares = butterfly(squares, "expert")
    inverse = lax.rsqrt(squares / width + eps)
    query_t, query, key_t, key, attended, attended_t, log_total = attend(
        query_raw, key_raw, value_t, inverse, gains, cosine, rope_sine, key_seg, query_seg
    )
    if grouped:
        attended, out_far = cot_rounds.step(attended, out_far)
        out_cross = send(out_far, swap_core)

    attended_low = exchange(my_part(attended, 1).reshape(devices, row_count, part))
    if grouped:
        middle, normed_mid = out_project(
            where, attended_low, tokens, ffn_gain[None, :], blocks, out_far, out_cross
        )
    else:
        attended_low = attended_low.transpose(1, 0, 2).reshape(row_count, width)
        middle = resid_in + mm(attended_low, out_full)
        normed_mid = norm_rows(middle, ffn_gain)[0].astype(jnp.bfloat16)
    (normed_mid,) = cot_rounds.step(normed_mid)

    mid_rounds = gather(normed_mid)
    head_w_t = jnp.concatenate(
        [my_part(head_w[:, i * HEAD_DIM : (i + 1) * HEAD_DIM], 1).T for i in range(3)], axis=0
    )
    (head_w_t,) = mid_rounds.step(head_w_t)
    rows_in = pick(picks, ones, mid_rounds.finish())
    (rows_in,) = cot_rounds.step(rows_in)
    grad_eo = pick(picks, slot_gate, cot_rounds.finish())
    gate_up = mm(rows_in, w_both)
    gate_in, up_in = gate_up[:, :ff], gate_up[:, ff:]
    sigmoid_in = jax.nn.sigmoid(gate_in)
    silu_in = gate_in * sigmoid_in
    hidden = (silu_in * up_in).astype(jnp.bfloat16)
    grad_down, down_far = weight_grad(hidden, grad_eo)

    def give_back(produce):
        def some(first, count):
            here = slice(first // row_count, (first + count) // row_count)
            rows = produce(slice(here.start * slots, here.stop * slots))
            return jnp.einsum(
                "bts,bsd->btd",
                unpicks[here],
                rows.astype(jnp.bfloat16).reshape(-1, slots, width),
                preferred_element_type=jnp.bfloat16,
            ).reshape(count, width)

        return some

    hidden_next, grad_eo_next = together(hidden, grad_eo, *grad_down)[:2]
    mix_rounds = scatter(
        give_back(lambda some: mm(hidden_next[some], w_down[0]) * slot_gate[some])
    )
    grad_hidden = contract_cols(grad_eo_next, w_down[0])
    grad_pre = jnp.concatenate(
        [
            (
                grad_hidden * up_in * sigmoid_in * (1.0 + gate_in * (1.0 - sigmoid_in))
            ).astype(jnp.bfloat16),
            (grad_hidden * silu_in).astype(jnp.bfloat16),
        ],
        axis=1,
    )
    (grad_pre,) = ride(mix_rounds, grad_pre)
    row_rounds = scatter(
        give_back(lambda some: contract_cols(grad_pre[some], w_both)),
        lambda addends: ride(mix_rounds, addends)[0],
    )
    grad_both, both_far = weight_grad(rows_in, grad_pre)
    far, i = waiting.pop(0) if grouped else (None, 0)
    if grouped:
        (far[i], *_) = step_all([row_rounds, mix_rounds], far[i], *grad_both[:1])
    else:
        row_rounds.step()
    ride(row_rounds, *mix_rounds.sent, *grad_both[1:2])
    row_rounds.step(*grad_both[2:4])
    ride(row_rounds, *grad_both[4:5])
    ride(row_rounds, *grad_both[5:6])
    grad_normed_mid = row_rounds.finish()

    grad_out = cotangent.astype(jnp.float32)
    _, normal_mid, inverse_mid = norm_rows(middle, ffn_gain)
    mid_back, grad_ffn_gain = norm_back(grad_normed_mid, normal_mid, inverse_mid, ffn_gain)
    grad_middle = grad_out + mid_back
    grad_branch = grad_middle.astype(jnp.bfloat16)
    if grouped:
        grad_columns = out_project_back(where, grad_branch, blocks, out_far, out_cross)
        (grad_columns,) = ride(mix_rounds, grad_columns)
    else:
        grad_columns = to_heads(contract_cols(grad_branch, out_full).astype(jnp.bfloat16))
    grad_attended = exchange(grad_columns).reshape(seq_length, HEAD_DIM)
    if groups == 2:
        (down_total,) = merge(grad_down, down_far, 1)
        grad_attended, down_total, *_ = cross(grad_attended, down_total, *grad_both[6:])
    else:
        down_total = down_far[0].astype(jnp.float32)
    mixed = mix_rounds.finish()
    activations = (middle + mixed).astype(jnp.bfloat16)
    branch_all = lax.all_gather(
        after(grad_branch, grad_attended), "expert", axis=0, tiled=True
    )

    weighted_query, weighted_key, grad_value_t, inner_query, inner_key, gain_sums = attend_back(
        key_seg,
        query_seg,
        log_total,
        query_t,
        query,
        grad_attended,
        key,
        key_t,
        value,
        query_raw,
        key_raw,
        inverse,
        gains,
        cosine,
        rope_sine,
    )
    inner = jnp.concatenate([inner_query, inner_key], axis=0)
    if sharing > 1:
        inner = jnp.stack(
            [
                jnp.sum(my_part(weighted * raw * at, 0), axis=0)
                for weighted, raw, at in (
                    (weighted_query, query_raw, inverse[0:1]),
                    (weighted_key, key_raw, inverse[1:2]),
                )
            ]
        )
    (inner,) = cross(inner)
    inner = butterfly(inner, "expert") / width
    grad_raw_t = jnp.concatenate(
        [
            my_part(
                (at * (weighted - raw * at * mean)).astype(jnp.bfloat16),
                0,
            )
            for weighted, raw, at, mean in (
                (weighted_query, query_raw, inverse[0:1], inner[0:1]),
                (weighted_key, key_raw, inverse[1:2], inner[1:2]),
            )
        ]
        + [my_part(grad_value_t, 0)],
        axis=0,
    )
    in_rounds = scatter(
        lambda first, count: project(order, grad_raw_t, head_w_t, row_count, first, count),
        both_first=True,
    )
    (grad_raw_t,) = in_rounds.step(grad_raw_t)
    grad_w_t = stack_product(order, grad_raw_t, row_count, blocks)
    grad_attn_gain = jnp.sum(grad_w_t * head_w_t.astype(jnp.float32), axis=0) / attn_gain
    (grad_w_t,) = ride(in_rounds, grad_w_t)
    w_columns = exchange(
        grad_w_t.astype(jnp.bfloat16).reshape(3 * part, devices, w_rows).transpose(1, 0, 2)
    )

    def placed(values):
        return lax.dynamic_update_slice_in_dim(
            jnp.zeros((width,), jnp.float32), values, me * part, 0
        )

    gain_parts = jnp.stack(
        [
            grad_attn_gain,
            placed(my_part(gain_sums[:, 0], 0)),
            placed(my_part(gain_sums[:, 1], 0)),
            grad_ffn_gain,
        ]
    )
    out_part = mm(my_part(attended_t, 0), branch_all).astype(jnp.bfloat16)
    out_part, w_columns = ride(in_rounds, out_part, w_columns)
    out_part_far = dp_start(out_part)
    dense = [
        w_columns[:, i * part : (i + 1) * part].reshape(width, w_rows).T for i in range(3)
    ]
    if groups == 2:
        both_total = list(merge(grad_both[:4], both_far[:4], 2, len(grad_both)))
        gain_parts, both_total[0], both_total[1], *dense = ride(
            in_rounds, gain_parts, *both_total, *dense
        )
        both_total = merge(grad_both[4:], both_far[4:], 2, 4, both_total)
    else:
        in_rounds.step()
        both_total = both_far[0].astype(jnp.float32)
        both_total = (both_total[:, :ff], both_total[:, ff:])
    dense_far = [dp_start(values) for values in dense]
    out_part_far, dense_far[0], *both_total = in_rounds.step(
        out_part_far, dense_far[0], *both_total
    )
    gate_total, up_total = both_total
    grad_normed_in = in_rounds.finish()
    grad_normed_in, gain_parts = together(grad_normed_in, gain_parts)
    gain_parts = butterfly(gain_parts, "expert")
    gain_parts, dense_far[2], gate_total = together(gain_parts, dense_far[2], gate_total)
    gain_total = butterfly(gain_parts, "dp")
    in_back, _ = norm_back(grad_normed_in, normal_in, inverse_in, attn_gain)
    input_grad = (grad_middle + in_back).astype(jnp.bfloat16)

    return (
        activations,
        input_grad,
        gain_total[0],
        gain_total[1],
        gain_total[2],
        gain_total[3],
        dp_end(dense[0], dense_far[0]),
        dp_end(dense[1], dense_far[1]),
        dp_end(dense[2], dense_far[2]),
        dp_end(out_part, out_part_far),
        gate_total[None],
        up_total[None],
        down_total[None],
    )


def solution(mesh):
    in_specs = (
        P(("dp", "expert"), None),
        P("dp"),
        P(("dp", "expert"), None),
        P(("dp", "expert"), None),
        P(),
        P(),
        P(),
        P(),
        P("expert", None),
        P("expert", None),
        P("expert", None),
        P("expert", None),
        P("expert", None, None),
        P("expert", None, None),
        P("expert", None, None),
        P(("dp", "expert"), None),
    )
    out_specs = (
        P(("dp", "expert"), None),
        P(("dp", "expert"), None),
        P(),
        P(),
        P(),
        P(),
        P("expert", None),
        P("expert", None),
        P("expert", None),
        P("expert", None),
        P("expert", None, None),
        P("expert", None, None),
        P("expert", None, None),
    )
    return jax.shard_map(local, mesh=mesh, in_specs=in_specs, out_specs=out_specs, check_vma=False)
```
